32 devices in a mesh: dom: 8 (over z, y), box: 4 (over x, core).
Axes of the slice: x: 2, y: 2, z: 4, core: 2. Of those that a mesh axis runs over, the one named last changes fastest.
Arguments:
- old_history: bfloat16 [256, 128, 128], P(('dom', 'box')), may hold values from -24 to 24
- box_route: int32 [256], P(('dom', 'box')), may hold values from 0 to 3, as said below
- entry_slot: int32 [256, 4], P(('dom', 'box')), may hold values from 0 to 15, as said below
- entry_count: int32 [256], P(('dom', 'box')), may hold values from 1 to 4, as said below
- weights: bfloat16 [256, 4, 128, 128], P(('dom', 'box')), may hold values from 0.049804688 to 1
- owner_route: int32 [32768], P(('dom', 'box')), may hold values from 0 to 7, as said below
- owner_slot: int32 [32768], P(('dom', 'box')), may hold values from 0 to 1023, as said below
- connectivity: int32 [8, 32768], P(None, ('dom', 'box')), may hold values from 0 to 1023
- shared_nodes: int32 [4, 4096], P(None, ('dom', 'box')), may hold values from 0 to 1023, as said below
- node_motion: float32 [3, 32768], P(None, ('dom', 'box')), may hold values from -6 to 6
- elem_size: float32 [32768], P(('dom', 'box')), may hold values from 0.7 to 1.4
- decay: float32 [128], replicated, may hold values from 0.2 to 0.95
- couple: float32 [128, 6], replicated, may hold values from -2.5 to 2.5
- readout: float32 [128, 6], replicated, may hold values from -0.5 to 0.5
Outputs:
- new_history: bfloat16 [32768, 128], P(('dom', 'box'))
- node_force: float32 [3, 32768], P(None, ('dom', 'box'))
The draws below stay inside these ranges and needn't reach their ends.
Inputs may be any that keep to these rules, and one draw needn't show every extreme that they name: `box_route`: among the 8 blocks of one device at most 4 name the same box. For every dom index one box receives exactly 4 blocks from each of the 4 devices of that dom index; every box receives at least one block. `entry_slot`: each entry names a filled received slot of its own device, as in the reference program. `entry_count`: entries at or beyond a target's count are padding. Every device has a target with 4 entries. Within one box index, the pairs (owner_route, owner_slot) of all rows are distinct, so each new owner receives exactly 1024 rows. A device sends 128 rows to every new owner of its box index except 256 to one and none to another. `owner_slot`: see owner_route. `shared_nodes`: the 512 entries of one device are distinct local nodes. Entry m of row 0 on a device is the same node as entry m of row 1 on the device one lower along dom; rows 2 and 3 likewise along box.
All inputs are finite; a program needn't handle non-finite values.
Results may differ from the reference program's by a relative error of at most 0.0029.
Values may be sent and summed in bfloat16 or wider, within the bound.
No kernel may reach another device: no remote copies, remote signals or barrier semaphores. Data moves between devices by JAX's collectives and lax.ppermute only.
A program may use at most 64 MiB of HBM per device.

```python
import math
import jax
import jax.numpy as jnp
from jax import lax

H = 128
E = 128
NL = 4
UNIT_PRIOR_CELLS = 8
NT = 8
BIN_GROUP_CEILING = 4
NE = 1024
B0 = 128
NN = 1024
NS = 128
OLD_BLOCKS = 256
TARGETS = 256
ROWS = 32768
NODES = 32768
N_DOM = 8
N_BOX = 4


def route_table(key):
    device_total = N_DOM * N_BOX
    hot_key, device_key = jax.random.split(key)
    hot = jax.random.randint(hot_key, (N_DOM,), 0, N_BOX).astype(jnp.int32)
    hot_device = jnp.repeat(hot, N_BOX)
    own_box = jnp.arange(device_total, dtype=jnp.int32) % N_BOX

    def one_device(subkey, hot_box, local_unit):
        first_key, second_key = jax.random.split(subkey)
        seat_ordinals = jnp.arange((N_BOX - 1) * BIN_GROUP_CEILING, dtype=jnp.int32)
        remote_units = (hot_box + 1 + seat_ordinals // BIN_GROUP_CEILING) % N_BOX
        bin_ratings = jax.random.randint(first_key, seat_ordinals.shape, 0, 1 << 20)
        rating_reward = jnp.where((remote_units == local_unit) & (seat_ordinals % BIN_GROUP_CEILING == 0), 1 << 21, 0)
        selected_bins = jnp.argsort(-(bin_ratings + rating_reward), stable=True)[:UNIT_PRIOR_CELLS - BIN_GROUP_CEILING]
        dests = jnp.concatenate([jnp.full((BIN_GROUP_CEILING,), hot_box, jnp.int32), remote_units[selected_bins].astype(jnp.int32)])
        return jax.random.permutation(second_key, dests)
    keys = jax.random.split(device_key, device_total)
    return jax.vmap(one_device)(keys, hot_device, own_box).reshape(-1).astype(jnp.int32)


def draw_box_route(key, part):
    return route_table(jax.random.fold_in(key, 7))


def draw_entry_slot(key, part):
    routes = route_table(jax.random.fold_in(key, 7)).reshape(N_DOM, N_BOX, UNIT_PRIOR_CELLS)
    boxes = jnp.arange(N_BOX, dtype=jnp.int32)
    counts = jnp.sum((routes[:, :, :, None] == boxes[None, None, None, :]).astype(jnp.int32), axis=2)
    counts = jnp.transpose(counts, (0, 2, 1))
    seat_ordinals = jnp.arange(N_BOX * BIN_GROUP_CEILING, dtype=jnp.int32)
    filled = (seat_ordinals % BIN_GROUP_CEILING)[None, None, :] < jnp.repeat(counts, BIN_GROUP_CEILING, axis=2)
    ordering = jnp.argsort(1 - filled.astype(jnp.int32), axis=-1, stable=True).astype(jnp.int32)
    total = jnp.sum(filled.astype(jnp.int32), axis=-1)
    picks = jax.random.randint(jax.random.fold_in(key, 9), (N_DOM, N_BOX, NT * NL), 0, total[:, :, None])
    slots = jnp.take_along_axis(ordering, picks, axis=-1)
    return slots.reshape(N_DOM * N_BOX * NT, NL).astype(jnp.int32)


def draw_entry_count(key, part):
    device_total = N_DOM * N_BOX
    first_key, second_key = jax.random.split(jax.random.fold_in(key, 5))
    counts = jax.random.randint(first_key, (device_total, NT), 1, NL + 1)
    full_target = jax.random.randint(second_key, (device_total,), 0, NT)
    counts = jnp.where(jnp.arange(NT)[None, :] == full_target[:, None], NL, counts)
    return counts.reshape(-1).astype(jnp.int32)


def owner_table(key):

    def one_group(subkey):
        first_key, second_key, third_key = jax.random.split(subkey, 3)
        order = jax.random.permutation(first_key, N_DOM).astype(jnp.int32)
        shifted = jnp.roll(order, -1)
        columns = jnp.arange(N_DOM, dtype=jnp.int32)
        loads = B0 + B0 * ((columns[None, :] == order[:, None]).astype(jnp.int32) - (columns[None, :] == shifted[:, None]).astype(jnp.int32))
        cumulative = jnp.cumsum(loads, axis=1)
        row_ids = jnp.arange(NE, dtype=jnp.int32)

        def sorted_dest(row):
            return jnp.searchsorted(row, row_ids, side='right').astype(jnp.int32)
        dest_sorted = jax.vmap(sorted_dest)(cumulative)
        row_start = jnp.take_along_axis(cumulative - loads, dest_sorted, axis=1)
        within = row_ids[None, :] - row_start
        offset = jnp.cumsum(loads, axis=0) - loads
        base = jnp.take_along_axis(offset, dest_sorted, axis=1) + within

        def permute(inner):
            return jax.random.permutation(inner, NE).astype(jnp.int32)
        placement = jax.vmap(permute)(jax.random.split(second_key, N_DOM))
        positions = placement[dest_sorted, base]
        shuffle = jax.vmap(permute)(jax.random.split(third_key, N_DOM))
        source_ids = jnp.broadcast_to(jnp.arange(N_DOM, dtype=jnp.int32)[:, None], (N_DOM, NE))
        out_dest = jnp.zeros((N_DOM, NE), jnp.int32).at[source_ids, shuffle].set(dest_sorted)
        out_position = jnp.zeros((N_DOM, NE), jnp.int32).at[source_ids, shuffle].set(positions)
        return (out_dest, out_position)
    dests, positions = jax.vmap(one_group)(jax.random.split(key, N_BOX))
    dests = jnp.transpose(dests, (1, 0, 2)).reshape(-1).astype(jnp.int32)
    positions = jnp.transpose(positions, (1, 0, 2)).reshape(-1).astype(jnp.int32)
    return (dests, positions)


def draw_owner_route(key, part):
    return owner_table(jax.random.fold_in(key, 11))[0]


def draw_owner_slot(key, part):
    return owner_table(jax.random.fold_in(key, 11))[1]


def draw_shared_nodes(key, part):
    device_total = N_DOM * N_BOX

    def one_device(subkey):
        return jax.random.permutation(subkey, NN)[:4 * NS].astype(jnp.int32)
    lists = jax.vmap(one_device)(jax.random.split(jax.random.fold_in(key, 13), device_total))
    lists = jnp.transpose(lists.reshape(device_total, 4, NS), (1, 0, 2))
    return lists.reshape(4, device_total * NS).astype(jnp.int32)


def with_ends(result, rng, least, largest):
    dims = result.shape
    index_at = [jax.random.randint(jax.random.fold_in(rng, axis), (), 0, dims[axis]) for axis in range(len(dims))]
    result = result.at[tuple(index_at)].set(least)
    longest = dims.index(max(dims))
    index_at[longest] = (index_at[longest] + 1) % dims[longest]
    return result.at[tuple(index_at)].set(largest)


def level_of(key, shape, cuts, least, top_value):
    loudness, own = 1.0, jax.random.fold_in(key, 6)
    for position, shards_of in cuts:
        draws = jnp.exp(jax.random.uniform(jax.random.fold_in(own, position), (shards_of,), jnp.float32, least / len(cuts), top_value / len(cuts)))
        loudness = loudness * jnp.repeat(draws, shape[position] // shards_of).reshape([-1 if axis == position else 1 for axis in range(len(shape))])
    return loudness


def centred(rng, shape, spread, reach, pieces=(), held_as=jnp.bfloat16):
    drawn = jax.random.normal(rng, shape, jnp.float32) * spread
    if len(pieces) > 0:
        drawn = level_of(rng, shape, pieces, -0.22, 0.18) * drawn
    return jnp.clip(drawn, min=-reach, max=reach).astype(held_as)


def setup_inputs(seed: int = 0) -> dict:
    seeds = jax.random.split(jax.random.key(seed), 15)
    old_history = centred(seeds[0], (OLD_BLOCKS, H, E), 4.0, 24.0, ((0, 32),))
    box_route = draw_box_route(jax.random.fold_in(seeds[14], 71), 0)
    entry_slot = draw_entry_slot(jax.random.fold_in(seeds[14], 71), 0)
    entry_count = draw_entry_count(jax.random.fold_in(seeds[14], 71), 0)
    weights = jnp.clip(0.049804688 + 0.9501953 * jax.random.uniform(seeds[4], (TARGETS, NL, E, E), jnp.float32) ** level_of(seeds[4], (TARGETS, NL, E, E), ((0, 32),), -0.2, 0.2), 0.049804688, 1.0).astype(jnp.bfloat16)
    owner_route = draw_owner_route(jax.random.fold_in(seeds[14], 71), 0)
    owner_slot = draw_owner_slot(jax.random.fold_in(seeds[14], 71), 0)
    connectivity = with_ends(jax.random.randint(seeds[7], (8, ROWS), 0, NN), jax.random.fold_in(seeds[7], 1), 0, NN - 1).astype(jnp.int32)
    shared_nodes = draw_shared_nodes(jax.random.fold_in(seeds[14], 71), 0)
    node_motion = centred(seeds[9], (3, NODES), 1.0, 6.0, ((1, 32),), jnp.float32)
    elem_size = jnp.clip(jnp.exp(math.log(1.4) - 0.6931472 * jax.random.uniform(seeds[10], (ROWS,), jnp.float32) ** level_of(seeds[10], (ROWS,), ((0, 32),), -0.2, 0.2)), 0.7, 1.4)
    decay = jnp.clip(jax.random.uniform(seeds[11], (H,), jnp.float32, 0.2, 0.95), 0.2, 0.95)
    couple = centred(seeds[12], (H, 6), 6 ** -0.5, 2.5, (), jnp.float32)
    readout = centred(seeds[13], (H, 6), H ** -0.5, 0.5, (), jnp.float32)
    return {"old_history": old_history, "box_route": box_route, "entry_slot": entry_slot, "entry_count": entry_count, "weights": weights, "owner_route": owner_route, "owner_slot": owner_slot, "connectivity": connectivity, "shared_nodes": shared_nodes, "node_motion": node_motion, "elem_size": elem_size, "decay": decay, "couple": couple, "readout": readout}


def corner_signs():
    corners = jnp.arange(8, dtype=jnp.int32)
    directions = jnp.arange(3, dtype=jnp.int32)
    return (2 * ((corners[None, :] >> directions[:, None]) & 1) - 1).astype(jnp.float32)


def element_forces(arrived, connectivity, node_motion, elem_size, decay, couple, readout):
    highest = lax.Precision.HIGHEST
    signs = corner_signs()
    corner_motion = node_motion[:, connectivity]
    gradient = jnp.einsum("ca,iae->ice", signs, corner_motion, precision=highest) / (4.0 * elem_size)[None, None, :]
    strain = jnp.stack([gradient[0, 0], gradient[1, 1], gradient[2, 2],
                        gradient[0, 1] + gradient[1, 0], gradient[1, 2] + gradient[2, 1],
                        gradient[2, 0] + gradient[0, 2]])
    history = arrived.astype(jnp.float32) * decay[None, :] + jnp.einsum("ce,hc->eh", strain, couple, precision=highest)
    volume_part = 1.2 * (strain[0] + strain[1] + strain[2])
    elastic = jnp.stack([volume_part + 1.6 * strain[0], volume_part + 1.6 * strain[1], volume_part + 1.6 * strain[2],
                         0.8 * strain[3], 0.8 * strain[4], 0.8 * strain[5]])
    stress = elastic + jnp.einsum("eh,hc->ce", history, readout, precision=highest)
    tensor = jnp.stack([jnp.stack([stress[0], stress[3], stress[5]]),
                        jnp.stack([stress[3], stress[1], stress[4]]),
                        jnp.stack([stress[5], stress[4], stress[2]])])
    corner_force = (elem_size * elem_size / 4.0)[None, None, :] * jnp.einsum("ca,ice->iae", signs, tensor, precision=highest)
    local = jax.ops.segment_sum(corner_force.reshape(3, -1).T, connectivity.reshape(-1),
                                num_segments=node_motion.shape[1]).T
    return history.astype(jnp.bfloat16), local


def project(inputs):
    held, slots, alive, crossing = inputs
    picked = held[slots] * alive.astype(jnp.bfloat16)[:, :, None, None]
    numerator = jnp.einsum("tlhi,tlij->tjh", picked.astype(jnp.float32), crossing.astype(jnp.float32))
    mass = jnp.einsum("tl,tlij->tj", alive.astype(jnp.float32), crossing.astype(jnp.float32))
    return (numerator / mass[:, :, None]).astype(jnp.bfloat16).reshape(NE, H)


def reference(old_history, box_route, entry_slot, entry_count, weights, owner_route, owner_slot,
              connectivity, shared_nodes, node_motion, elem_size, decay, couple, readout):
    device_total = N_DOM * N_BOX
    blocks = old_history.reshape(N_DOM, N_BOX, UNIT_PRIOR_CELLS, H, E)
    routes = box_route.reshape(N_DOM, N_BOX, UNIT_PRIOR_CELLS)
    one_hot = (routes[..., None] == jnp.arange(N_BOX, dtype=jnp.int32)).astype(jnp.int32)
    order_in = jnp.sum((jnp.cumsum(one_hot, axis=2) - one_hot) * one_hot, axis=3).astype(jnp.int32)
    dom_ids = jnp.broadcast_to(jnp.arange(N_DOM, dtype=jnp.int32)[:, None, None], routes.shape)
    source_box = jnp.broadcast_to(jnp.arange(N_BOX, dtype=jnp.int32)[None, :, None], routes.shape)
    received = jnp.zeros((N_DOM, N_BOX, N_BOX * BIN_GROUP_CEILING, H, E), jnp.bfloat16)
    received = received.at[dom_ids, routes, source_box * BIN_GROUP_CEILING + order_in].set(blocks)
    received = received.reshape(device_total, N_BOX * BIN_GROUP_CEILING, H, E)
    live = jnp.arange(NL, dtype=jnp.int32)[None, :] < entry_count[:, None]
    projected = lax.map(project, (received, entry_slot.reshape(device_total, NT, NL),
                                  live.reshape(device_total, NT, NL),
                                  weights.reshape(device_total, NT, NL, E, E)))
    projected = projected.reshape(N_DOM, N_BOX, NE, H)
    owner_dom = owner_route.reshape(N_DOM, N_BOX, NE)
    positions = owner_slot.reshape(N_DOM, N_BOX, NE)
    box_ids = jnp.broadcast_to(jnp.arange(N_BOX, dtype=jnp.int32)[None, :, None], owner_dom.shape)
    arrived = jnp.zeros((N_DOM, N_BOX, NE, H), jnp.bfloat16).at[owner_dom, box_ids, positions].set(projected)
    arrived = arrived.reshape(ROWS, H)
    offsets = (NN * jnp.arange(device_total, dtype=jnp.int32))[None, :, None]
    global_nodes = (connectivity.reshape(8, device_total, NE) + offsets).reshape(8, ROWS)
    new_history, local = element_forces(arrived, global_nodes, node_motion, elem_size, decay, couple, readout)
    local_four = local.reshape(3, N_DOM, N_BOX, NN)
    shared_four = shared_nodes.reshape(4, N_DOM, N_BOX, NS)
    exports = [jnp.take_along_axis(local_four, shared_four[which][None], axis=3) for which in range(4)]
    zero_dom = jnp.zeros((3, 1, N_BOX, NS), jnp.float32)
    zero_box = jnp.zeros((3, N_DOM, 1, NS), jnp.float32)
    below_dom = jnp.concatenate([zero_dom, exports[1][:, :-1]], axis=1)
    above_dom = jnp.concatenate([exports[0][:, 1:], zero_dom], axis=1)
    below_box = jnp.concatenate([zero_box, exports[3][:, :, :-1]], axis=2)
    above_box = jnp.concatenate([exports[2][:, :, 1:], zero_box], axis=2)
    comp_index = jnp.arange(3, dtype=jnp.int32)[:, None, None, None]
    dom_index = jnp.arange(N_DOM, dtype=jnp.int32)[None, :, None, None]
    box_index = jnp.arange(N_BOX, dtype=jnp.int32)[None, None, :, None]
    force = local_four.at[comp_index, dom_index, box_index, shared_four[0][None]].add(below_dom)
    force = force.at[comp_index, dom_index, box_index, shared_four[1][None]].add(above_dom)
    force = force.at[comp_index, dom_index, box_index, shared_four[2][None]].add(below_box)
    force = force.at[comp_index, dom_index, box_index, shared_four[3][None]].add(above_box)
    return new_history, force.reshape(3, NODES)
```

```python
import functools

import jax
import jax.numpy as jnp
from jax import lax
from jax.experimental import pallas as pl
from jax.experimental.pallas import tpu as pltpu
from jax.sharding import PartitionSpec as P

BF = jnp.bfloat16
F32 = jnp.float32
I32 = jnp.int32
LANES = 128
SUBS = 8
POS_ROWS = 16
NOWHERE = 16.0
TENSOR = ((0, 3, 5), (3, 1, 4), (5, 4, 2))
NT_DIMS = (((1,), (1,)), ((), ()))
TN_DIMS = (((0,), (0,)), ((), ()))
HIGHEST = lax.Precision.HIGHEST


def iota(shape, dim):
    return lax.broadcasted_iota(I32, shape, dim)


def pieces(x, count):
    out = []
    for _ in range(count - 1):
        high = x.astype(BF)
        out.append(high)
        x = x - high.astype(F32)
    out.append(x.astype(BF))
    return out


def as_onehot(mask):
    return jnp.where(mask, 1.0, 0.0).astype(BF)


def lookup(rows, index):
    low = index & (LANES - 1)
    high = index >> 7
    out = jnp.zeros(index.shape, F32)
    for r, row in enumerate(rows):
        got = jnp.take_along_axis(
            jnp.broadcast_to(row, index.shape), low, axis=1, mode="promise_in_bounds"
        )
        out = jnp.where(high == r, got, out)
    return out


def pack_blocks(route, old, *rest):
    outs, table = rest[:-1], rest[-1]
    me = lax.axis_index("box")
    capacity = outs[0].shape[0]
    for m in range(len(outs) * capacity):
        table[m] = 0
    routes = [route[i] for i in range(old.shape[0])]
    for i, target in enumerate(routes):
        order = jnp.int32(0)
        for earlier in routes[:i]:
            order = order + (earlier == target).astype(I32)
        table[(target ^ me) * capacity + order] = i
    for k, out in enumerate(outs):
        for s in range(capacity):
            out[s] = old[table[k * capacity + s]]


def sort_rows(count, owner_route, owner_slot, weights, sorter, positions, chunks, mass_inv,
              high_rows, low_rows, starts):
    dom_total = positions.shape[0]
    row_groups = owner_route.shape[0]
    rows = row_groups * LANES
    me = lax.axis_index("dom")
    route = owner_route[...]
    picks = jnp.concatenate([as_onehot(route == d) for d in range(dom_total)], axis=0)
    span = dom_total * row_groups
    ahead = as_onehot(iota((LANES, LANES), 0) < iota((LANES, LANES), 1))
    within = jnp.dot(picks, ahead, preferred_element_type=F32)
    totals = jnp.dot(picks, jnp.ones((LANES, LANES), BF), preferred_element_type=F32).astype(BF)
    before = as_onehot(iota((span, span), 1) < iota((span, span), 0))
    base = jnp.dot(before, totals, preferred_element_type=F32)
    ranked = within + base
    place = jnp.zeros((row_groups, LANES), F32)
    for d in range(dom_total):
        place = jnp.where(route == d, ranked[d * row_groups : (d + 1) * row_groups], place)
        starts[d] = jnp.max(base[d * row_groups : d * row_groups + 1]).astype(I32)
    starts[dom_total] = rows
    place = place.astype(I32)
    slots = iota((rows, LANES), 0)
    for g in range(row_groups):
        sorter[:, g * LANES : (g + 1) * LANES] = as_onehot(slots == place[g : g + 1])
    slot = owner_slot[...]
    which = iota((POS_ROWS, rows), 0)
    parts = jnp.where(which == 0, slot >> 7, jnp.where(which == 1, slot & (LANES - 1), 0))
    ordered = lax.dot_general(
        parts.astype(F32).astype(BF), sorter[...], NT_DIMS, preferred_element_type=F32
    )
    for g in range(row_groups):
        high_rows[g : g + 1] = ordered[0:1, g * LANES : (g + 1) * LANES]
        low_rows[g : g + 1] = ordered[1:2, g * LANES : (g + 1) * LANES]
    which = iota((POS_ROWS, LANES), 0)
    for k in range(dom_total):
        owner = lax.rem(me + k, dom_total)
        start = starts[owner]
        held = starts[owner + 1] - start
        block = jnp.zeros((POS_ROWS, LANES), F32)
        for j in range(2):
            chunk = jnp.minimum(start // LANES + j, row_groups - 1)
            chunks[2 * k + j] = chunk
            high = jnp.where(held > j * LANES, high_rows[pl.ds(chunk, 1)], NOWHERE)
            block = jnp.where(which == j, high, block)
            block = jnp.where(which == 2 + j, low_rows[pl.ds(chunk, 1)], block)
        positions[k] = block.astype(BF)
    entries = weights.shape[1] // LANES
    for t in range(weights.shape[0]):
        total = jnp.zeros((1, LANES), F32)
        for l in range(entries):
            part = jnp.sum(
                weights[t, l * LANES : (l + 1) * LANES, :].astype(F32), axis=0, keepdims=True
            )
            total = total + jnp.where(l < count[t], part, 0.0)
        mass_inv[t : t + 1] = 1.0 / total


def element_parts(connectivity, motion, size, couple, readout, shared, drive, base, onehot,
                  chosen, inverse, strain, elastic, wide):
    elements = connectivity.shape[1]
    corners = connectivity.shape[0]
    groups = motion.shape[1] // LANES
    corner = iota((corners, LANES), 0)
    signs = [(2 * ((corner >> c) & 1) - 1).astype(F32) for c in range(3)]
    low_iota = iota((LANES, LANES), 0)
    strain[...] = jnp.zeros_like(strain)
    elastic[...] = jnp.zeros_like(elastic)
    for j in range(elements // LANES):
        lanes = slice(j * LANES, (j + 1) * LANES)
        nodes = connectivity[:, lanes]
        scale = 1.0 / (4.0 * size[:, lanes])
        grad = []
        for i in range(3):
            moved = lookup(
                [motion[i : i + 1, r * LANES : (r + 1) * LANES] for r in range(groups)], nodes
            )
            grad.append(
                [jnp.sum(moved * signs[c], axis=0, keepdims=True) * scale for c in range(3)]
            )
        rows = [
            grad[0][0],
            grad[1][1],
            grad[2][2],
            grad[0][1] + grad[1][0],
            grad[1][2] + grad[2][1],
            grad[2][0] + grad[0][2],
        ]
        volume = 1.2 * (rows[0] + rows[1] + rows[2])
        for c in range(6):
            strain[c : c + 1, lanes] = rows[c]
            elastic[c : c + 1, lanes] = volume + 1.6 * rows[c] if c < 3 else 0.8 * rows[c]
        for a in range(corners):
            onehot[a, :, lanes] = as_onehot(low_iota == (nodes[a : a + 1] & (LANES - 1)))
    wide[...] = jnp.zeros_like(wide)
    wide[0, 0:6] = couple[...]
    wide[1, 0:6] = readout[...]
    drive[...] = lax.dot_general(
        strain[...], wide[0], TN_DIMS, preferred_element_type=F32, precision=HIGHEST
    )
    base[...] = elastic[...] + lax.dot_general(
        wide[1], drive[...], NT_DIMS, preferred_element_type=F32, precision=HIGHEST
    )
    odd_dom = lax.axis_index("dom") & 1
    odd_box = lax.axis_index("box") & 1
    chosen[...] = jnp.zeros_like(chosen)
    chosen[0:1] = shared[pl.ds(1 - odd_dom, 1)]
    chosen[1:2] = shared[pl.ds(odd_dom, 1)]
    chosen[2:3] = shared[pl.ds(3 - odd_box, 1)]
    chosen[3:4] = shared[pl.ds(2 + odd_box, 1)]
    group = iota((groups, LANES), 0)
    lane = iota((groups, LANES), 1)
    total = jnp.zeros((2 * groups, LANES), F32)
    for m in range(4):
        nodes = chosen[m : m + 1]
        here = group == (nodes >> 7)
        marks = jnp.concatenate(
            [jnp.where(here, m + 1, 0), jnp.where(here, lane, 0)], axis=0
        ).astype(F32)
        total = total + lax.dot_general(
            marks.astype(BF),
            as_onehot(low_iota == (nodes & (LANES - 1))),
            NT_DIMS,
            preferred_element_type=F32,
        )
    total = total.astype(I32)
    inverse[0] = total[:groups] - 1
    inverse[1] = total[groups:]


def project_rows(slot, count, chunks, weights, mass_inv, sorter, positions, *rest):
    dom_total = positions.shape[0]
    box_total = lax.axis_size("box")
    received = rest[:box_total]
    outs = rest[box_total : box_total + dom_total]
    held, turned, ordered = rest[box_total + dom_total :]
    me = lax.axis_index("box")
    capacity = received[0].shape[0]
    for k, block in enumerate(received):
        for s in range(capacity):
            held[k * capacity + s] = block[s]
    targets = weights.shape[0]
    entries = slot.shape[0]
    for t in range(targets):
        picked = []
        for l in range(entries):
            entry = slot[l, t]
            source = lax.div(entry, capacity) ^ me
            block = held[source * capacity + lax.rem(entry, capacity)]
            picked.append(jnp.where(l < count[t], block, jnp.zeros_like(block)))
        numerator = jnp.dot(
            jnp.concatenate(picked, axis=1), weights[t], preferred_element_type=F32
        )
        turned[:, t * LANES : (t + 1) * LANES] = (numerator * mass_inv[t : t + 1]).astype(BF)
    sort = lax.dot_general(sorter[...], turned[...], NT_DIMS, preferred_element_type=F32)
    for g in range(ordered.shape[0]):
        ordered[g] = sort[g * LANES : (g + 1) * LANES].astype(BF)
    for k, out in enumerate(outs):
        for j in range(2):
            out[j * LANES : (j + 1) * LANES] = ordered[chunks[2 * k + j]]
        out[2 * LANES :] = positions[k]


def finish(placed, sources, *refs):
    payloads = refs[:sources]
    drive, base, size, connectivity, onehot, decay, readout, chosen = refs[sources : sources + 8]
    history, local = refs[sources + 8 : sources + 10]
    exports = refs[sources + 10 : sources + 14]
    scratch = refs[sources + 14 :]
    elements = base.shape[1]
    groups = elements // LANES
    if placed:
        arrived = payloads[0][...]
        wide = arrived.astype(F32)
    else:
        placing, rows = scratch
        low_iota = iota((LANES, LANES), 0)
        for k, payload in enumerate(payloads):
            rows[k * 2 * LANES : (k + 1) * 2 * LANES] = payload[: 2 * LANES]
            where = payload[2 * LANES :].astype(F32).astype(I32)
            for j in range(2):
                match = low_iota == where[2 + j : 3 + j]
                lanes = slice((2 * k + j) * LANES, (2 * k + j + 1) * LANES)
                for g in range(groups):
                    placing[g * LANES : (g + 1) * LANES, lanes] = as_onehot(
                        match & (where[j : j + 1] == g)
                    )
        wide = jnp.dot(placing[...], rows[...], preferred_element_type=F32)
        arrived = wide.astype(BF)
    history[...] = (wide * decay[...] + drive[...]).astype(BF)
    taken = readout[...] * decay[...]
    taken = jnp.concatenate([taken, jnp.zeros((SUBS - 6, LANES), F32)], axis=0)
    share = lax.dot_general(
        jnp.concatenate(pieces(taken, 3), axis=0), arrived, NT_DIMS, preferred_element_type=F32
    )
    stress = base[...] + (share[0:SUBS] + share[SUBS : 2 * SUBS] + share[2 * SUBS : 3 * SUBS])
    row = iota((3 * SUBS, 2 * SUBS), 0)
    column = iota((3 * SUBS, 2 * SUBS), 1) & (SUBS - 1)
    spread = jnp.zeros(row.shape, I32)
    for i in range(3):
        for c in range(3):
            spread = jnp.where(
                ((row >> 3) == i) & (column == TENSOR[i][c]),
                2 * ((row >> c) & 1) - 1,
                spread,
            )
    forces = jnp.dot(
        spread.astype(F32).astype(BF),
        jnp.concatenate(pieces(stress, 2), axis=0),
        preferred_element_type=F32,
    )
    edge = size[...]
    forces = forces * (edge * edge * 0.25)
    group = iota((SUBS, elements), 0)
    total = jnp.zeros((6 * SUBS, LANES), F32)
    for a in range(SUBS):
        here = group == (connectivity[a : a + 1] >> 7)
        highs, lows = [], []
        for i in range(3):
            value = jnp.where(here, forces[i * SUBS + a : i * SUBS + a + 1], 0.0)
            high, low = pieces(value, 2)
            highs.append(high)
            lows.append(low)
        total = total + lax.dot_general(
            jnp.concatenate(highs + lows, axis=0), onehot[a], NT_DIMS, preferred_element_type=F32
        )
    nodes = chosen[...]
    for i in range(3):
        summed = (
            total[i * SUBS : (i + 1) * SUBS] + total[(3 + i) * SUBS : (4 + i) * SUBS]
        )
        local[i] = summed
        got = lookup([summed[r : r + 1] for r in range(SUBS)], nodes)
        for m, out in enumerate(exports):
            out[i : i + 1] = got[m : m + 1]


def add_shared(local, inverse, *rest):
    received, force = rest[:-1], rest[-1]
    row, column = inverse[0], inverse[1]
    for i in range(local.shape[0]):
        total = local[i]
        for m, got in enumerate(received):
            share = jnp.take_along_axis(
                jnp.broadcast_to(got[i : i + 1], column.shape),
                column,
                axis=1,
                mode="promise_in_bounds",
            )
            total = total + jnp.where(row == m, share, 0.0)
        for r in range(local.shape[1]):
            force[i : i + 1, r * LANES : (r + 1) * LANES] = total[r : r + 1]


VMEM = pl.BlockSpec(memory_space=pltpu.VMEM)
SMEM = pl.BlockSpec(memory_space=pltpu.SMEM)


def call(kernel, name, ins, outs, scratch, args, cost=100_000, out_specs=None):
    single = not isinstance(outs, (list, tuple))
    return pl.pallas_call(
        kernel,
        name=name,
        out_shape=outs,
        in_specs=ins,
        out_specs=out_specs or (VMEM if single else [VMEM] * len(outs)),
        scratch_shapes=scratch,
        cost_estimate=pl.CostEstimate(flops=1000, bytes_accessed=cost, transcendentals=0),
        compiler_params=pltpu.CompilerParams(vmem_limit_bytes=24 * 1024 * 1024),
    )(*args)


def swaps(axis, first):
    total = lax.axis_size(axis)
    pairs = []
    for i in range(first, total - 1, 2):
        pairs += [(i, i + 1), (i + 1, i)]
    return pairs


def arrays(shape, dtype):
    return jax.ShapeDtypeStruct(shape, dtype)


def exclusive_order(targets, choice_total):
    one_hot = (targets[:, None] == jnp.arange(choice_total, dtype=I32)[None, :]).astype(I32)
    return jnp.sum((jnp.cumsum(one_hot, axis=0) - one_hot) * one_hot, axis=1)


def spread_rows(received, entry_slot, entry_count, weights, owner_route, owner_slot):
    targets, entries = entry_slot.shape
    block_size = weights.shape[-1]
    capacity, width, _ = received[0].shape
    me = lax.axis_index("box")
    stacked = jnp.concatenate(received, axis=0)
    held = ((entry_slot // capacity) ^ me) * capacity + entry_slot % capacity
    live = (jnp.arange(entries, dtype=I32)[None, :] < entry_count[:, None]).astype(BF)
    mass = jnp.einsum("tl,tlij->tj", live, weights, preferred_element_type=F32)
    picked = stacked[held] * live[:, :, None, None]
    numerator = jnp.einsum("tlhi,tlij->tjh", picked, weights, preferred_element_type=F32)
    projected = (numerator / mass[:, :, None]).astype(BF).reshape(targets * block_size, width)
    total = projected.shape[0]
    dom_total = lax.axis_size("dom")
    owner_capacity = 2 * (total // dom_total)
    place = owner_route * owner_capacity + exclusive_order(owner_route, dom_total)
    rows = jnp.zeros((dom_total * owner_capacity, width), BF).at[place].set(projected)
    spots = jnp.full((dom_total * owner_capacity,), total, I32).at[place].set(owner_slot)
    rows = lax.all_to_all(
        rows.reshape(dom_total, owner_capacity, width), "dom", 0, 0, tiled=True
    )
    spots = lax.all_to_all(spots.reshape(dom_total, owner_capacity), "dom", 0, 0, tiled=True)
    return (
        jnp.zeros((total, width), BF)
        .at[spots.reshape(-1)]
        .set(rows.reshape(-1, width), mode="drop")
    )


def body(old_history, box_route, entry_slot, entry_count, weights, owner_route, owner_slot,
         connectivity, shared_nodes, node_motion, elem_size, decay, couple, readout):
    blocks, width, block_size = old_history.shape
    targets, entries = entry_slot.shape
    box_total = lax.axis_size("box")
    dom_total = lax.axis_size("dom")
    capacity = blocks // 2
    rows = targets * block_size
    row_groups = rows // LANES
    elements = connectivity.shape[1]
    nodes = node_motion.shape[1]

    packed = call(
        pack_blocks, "pack_blocks", [SMEM, VMEM],
        [arrays((capacity, width, block_size), BF)] * box_total,
        [pltpu.SMEM((box_total * capacity,), I32)],
        (box_route, old_history),
    )
    received = [packed[0]] + [
        lax.ppermute(packed[k], "box", [(i, i ^ k) for i in range(box_total)])
        for k in range(1, box_total)
    ]
    flat_weights = weights.reshape(targets, entries * block_size, block_size)
    edge = elem_size.reshape(1, elements)
    drive, base, onehot, chosen, inverse = call(
        element_parts, "element_parts", [VMEM] * 6,
        [
            arrays((elements, width), F32),
            arrays((SUBS, elements), F32),
            arrays((connectivity.shape[0], LANES, elements), BF),
            arrays((SUBS, shared_nodes.shape[1]), I32),
            arrays((2, nodes // LANES, LANES), I32),
        ],
        [
            pltpu.VMEM((SUBS, elements), F32),
            pltpu.VMEM((SUBS, elements), F32),
            pltpu.VMEM((2, SUBS, width), F32),
        ],
        (connectivity, node_motion, edge, couple.T, readout.T, shared_nodes),
    )
    usual = rows // dom_total
    if usual == LANES:
        sorter, positions, chunks, mass_inv = call(
            sort_rows, "sort_rows", [SMEM, VMEM, VMEM, VMEM],
            [
                arrays((rows, rows), BF),
                arrays((dom_total, POS_ROWS, LANES), BF),
                arrays((2 * dom_total,), I32),
                arrays((targets, block_size), F32),
            ],
            [
                pltpu.VMEM((row_groups, LANES), F32),
                pltpu.VMEM((row_groups, LANES), F32),
                pltpu.SMEM((dom_total + 1,), I32),
            ],
            (
                entry_count,
                owner_route.reshape(row_groups, LANES),
                owner_slot.reshape(1, rows),
                flat_weights,
            ),
            out_specs=[VMEM, VMEM, SMEM, VMEM],
        )
        payload = arrays((2 * usual + POS_ROWS, width), BF)
        outgoing = call(
            project_rows, "project_rows", [SMEM, SMEM, SMEM] + [VMEM] * (4 + box_total),
            [payload] * dom_total,
            [
                pltpu.VMEM((box_total * capacity, width, block_size), BF),
                pltpu.VMEM((width, rows), BF),
                pltpu.VMEM((row_groups, LANES, width), BF),
            ],
            (entry_slot.T, entry_count, chunks, flat_weights, mass_inv, sorter, positions, *received),
        )
        payloads = [outgoing[0]] + [
            lax.ppermute(outgoing[k], "dom", [(i, (i + k) % dom_total) for i in range(dom_total)])
            for k in range(1, dom_total)
        ]
        placed = False
        scratch = [
            pltpu.VMEM((elements, dom_total * 2 * usual), BF),
            pltpu.VMEM((dom_total * 2 * usual, width), BF),
        ]
    else:
        payloads = [
            spread_rows(received, entry_slot, entry_count, weights, owner_route, owner_slot)
        ]
        placed, scratch = True, []
    export = arrays((3, shared_nodes.shape[1]), F32)
    history, local, *exports = call(
        functools.partial(finish, placed, len(payloads)), "finish",
        [VMEM] * (len(payloads) + 8),
        [arrays((elements, width), BF), arrays((3, nodes // LANES, LANES), F32)] + [export] * 4,
        scratch,
        (
            *payloads, drive, base, edge, connectivity, onehot,
            decay.reshape(1, width), readout.T, chosen,
        ),
    )
    halo = [
        lax.ppermute(exports[0], "dom", swaps("dom", 0)),
        lax.ppermute(exports[1], "dom", swaps("dom", 1)),
        lax.ppermute(exports[2], "box", swaps("box", 0)),
        lax.ppermute(exports[3], "box", swaps("box", 1)),
    ]
    force = call(
        add_shared, "add_shared", [VMEM] * (2 + len(halo)), arrays((3, nodes), F32), [],
        (local, inverse, *halo),
    )
    return history, force


def solution(mesh):
    return jax.shard_map(
        body,
        mesh=mesh,
        in_specs=(
            P(("dom", "box"), None, None),
            P(("dom", "box")),
            P(("dom", "box"), None),
            P(("dom", "box")),
            P(("dom", "box"), None, None, None),
            P(("dom", "box")),
            P(("dom", "box")),
            P(None, ("dom", "box")),
            P(None, ("dom", "box")),
            P(None, ("dom", "box")),
            P(("dom", "box")),
            P(),
            P(),
            P(),
        ),
        out_specs=(P(("dom", "box"), None), P(None, ("dom", "box"))),
        check_vma=False,
    )
```

```python
import functools

import jax
import jax.numpy as jnp
from jax import lax
from jax.experimental import pallas as pl
from jax.experimental.pallas import tpu as pltpu
from jax.sharding import PartitionSpec as P

BF = jnp.bfloat16
F32 = jnp.float32
I32 = jnp.int32
LANES = 128
SUBS = 8
POS_ROWS = 16
NOWHERE = 16.0
TENSOR = ((0, 3, 5), (3, 1, 4), (5, 4, 2))
NT_DIMS = (((1,), (1,)), ((), ()))
TN_DIMS = (((0,), (0,)), ((), ()))
HIGHEST = lax.Precision.HIGHEST


def iota(shape, dim):
    return lax.broadcasted_iota(I32, shape, dim)


def pieces(x, count):
    out = []
    for _ in range(count - 1):
        high = x.astype(BF)
        out.append(high)
        x = x - high.astype(F32)
    out.append(x.astype(BF))
    return out


def as_onehot(mask):
    return jnp.where(mask, 1.0, 0.0).astype(BF)


def lookup(rows, index):
    low = index & (LANES - 1)
    high = index >> 7
    out = jnp.zeros(index.shape, F32)
    for r, row in enumerate(rows):
        got = jnp.take_along_axis(
            jnp.broadcast_to(row, index.shape), low, axis=1, mode="promise_in_bounds"
        )
        out = jnp.where(high == r, got, out)
    return out


def fetch(pairs, sems):
    copies = [
        pltpu.make_async_copy(source, target, sems.at[i])
        for i, (source, target) in enumerate(pairs)
    ]
    for copy in copies:
        copy.start()
    for copy in copies:
        copy.wait()


def pack_blocks(route_hbm, old_hbm, *rest):
    outs = rest[:-4]
    table, route, old, sems = rest[-4:]
    fetch([(route_hbm, route), (old_hbm, old)], sems)
    me = lax.axis_index("box")
    capacity = outs[0].shape[0]
    for m in range(len(outs) * capacity):
        table[m] = 0
    routes = [route[i] for i in range(old.shape[0])]
    for i, target in enumerate(routes):
        order = jnp.int32(0)
        for earlier in routes[:i]:
            order = order + (earlier == target).astype(I32)
        table[(target ^ me) * capacity + order] = i
    for k, out in enumerate(outs):
        for s in range(capacity):
            out[s] = old[table[k * capacity + s]]


def sort_rows(capacity, slot_hbm, count_hbm, route_hbm, place_hbm, weights_hbm, sorter, positions, table,
              mass_inv, masked, high_rows, low_rows, starts, slot, count, owner_route, owner_slot,
              sems):
    fetch(
        [
            (slot_hbm, slot),
            (count_hbm, count),
            (route_hbm, owner_route),
            (place_hbm, owner_slot),
            (weights_hbm, masked),
        ],
        sems,
    )
    dom_total = positions.shape[0]
    row_groups = owner_route.shape[0]
    rows = row_groups * LANES
    me = lax.axis_index("dom")
    route = owner_route[...]
    picks = jnp.concatenate([as_onehot(route == d) for d in range(dom_total)], axis=0)
    span = dom_total * row_groups
    ahead = as_onehot(iota((LANES, LANES), 0) < iota((LANES, LANES), 1))
    within = jnp.dot(picks, ahead, preferred_element_type=F32)
    totals = jnp.dot(picks, jnp.ones((LANES, LANES), BF), preferred_element_type=F32).astype(BF)
    before = as_onehot(iota((span, span), 1) < iota((span, span), 0))
    base = jnp.dot(before, totals, preferred_element_type=F32)
    ranked = within + base
    place = jnp.zeros((row_groups, LANES), F32)
    for d in range(dom_total):
        place = jnp.where(route == d, ranked[d * row_groups : (d + 1) * row_groups], place)
        starts[d] = jnp.max(base[d * row_groups : d * row_groups + 1]).astype(I32)
    starts[dom_total] = rows
    place = place.astype(I32)
    slots = iota((rows, LANES), 0)
    for g in range(row_groups):
        sorter[:, g * LANES : (g + 1) * LANES] = as_onehot(slots == place[g : g + 1])
    spot = owner_slot[...]
    which = iota((POS_ROWS, rows), 0)
    parts = jnp.where(which == 0, spot >> 7, jnp.where(which == 1, spot & (LANES - 1), 0))
    ordered = lax.dot_general(
        parts.astype(F32).astype(BF), sorter[...], NT_DIMS, preferred_element_type=F32
    )
    for g in range(row_groups):
        high_rows[g : g + 1] = ordered[0:1, g * LANES : (g + 1) * LANES]
        low_rows[g : g + 1] = ordered[1:2, g * LANES : (g + 1) * LANES]
    which = iota((POS_ROWS, LANES), 0)
    for k in range(dom_total):
        owner = me ^ k
        start = starts[owner]
        held = starts[owner + 1] - start
        block = jnp.zeros((POS_ROWS, LANES), F32)
        for j in range(2):
            chunk = jnp.minimum(start // LANES + j, row_groups - 1)
            table[2 * k + j] = chunk
            high = jnp.where(held > j * LANES, high_rows[pl.ds(chunk, 1)], NOWHERE)
            block = jnp.where(which == j, high, block)
            block = jnp.where(which == 2 + j, low_rows[pl.ds(chunk, 1)], block)
        positions[k] = block.astype(BF)
    targets = masked.shape[0]
    entries = masked.shape[1] // LANES
    box = lax.axis_index("box")
    for t in range(targets):
        total = jnp.zeros((1, LANES), F32)
        for l in range(entries):
            live = l < count[t]
            span = slice(l * LANES, (l + 1) * LANES)
            part = masked[t, span, :]
            part = jnp.where(live, part, jnp.zeros_like(part))
            masked[t, span, :] = part
            total = total + jnp.sum(part.astype(F32), axis=0, keepdims=True)
            entry = jnp.where(live, slot[l, t], slot[0, t])
            source = lax.div(entry, capacity)
            table[2 * dom_total + t * entries + l] = (source ^ box) * capacity + lax.rem(entry, capacity)
        mass_inv[t : t + 1] = 1.0 / total


def element_parts(connectivity, motion, size, couple, readout, shared, drive, base, onehot,
                  chosen, inverse, strain, elastic, wide):
    elements = connectivity.shape[1]
    corners = connectivity.shape[0]
    groups = motion.shape[1] // LANES
    corner = iota((corners, LANES), 0)
    signs = [(2 * ((corner >> c) & 1) - 1).astype(F32) for c in range(3)]
    low_iota = iota((LANES, LANES), 0)
    lane_iota = iota((LANES, LANES), 1).astype(F32)
    strain[...] = jnp.zeros_like(strain)
    elastic[...] = jnp.zeros_like(elastic)
    for j in range(elements // LANES):
        lanes = slice(j * LANES, (j + 1) * LANES)
        nodes = connectivity[:, lanes]
        scale = 1.0 / (4.0 * size[:, lanes])
        grad = []
        for i in range(3):
            moved = lookup(
                [motion[i : i + 1, r * LANES : (r + 1) * LANES] for r in range(groups)], nodes
            )
            grad.append(
                [jnp.sum(moved * signs[c], axis=0, keepdims=True) * scale for c in range(3)]
            )
        rows = [
            grad[0][0],
            grad[1][1],
            grad[2][2],
            grad[0][1] + grad[1][0],
            grad[1][2] + grad[2][1],
            grad[2][0] + grad[0][2],
        ]
        volume = 1.2 * (rows[0] + rows[1] + rows[2])
        for c in range(6):
            strain[c : c + 1, lanes] = rows[c]
            elastic[c : c + 1, lanes] = volume + 1.6 * rows[c] if c < 3 else 0.8 * rows[c]
        turned = (nodes & (LANES - 1)).astype(F32).T
        for a in range(corners):
            onehot[a, lanes, :] = as_onehot(lane_iota == turned[:, a : a + 1])
    wide[...] = jnp.zeros_like(wide)
    wide[0, 0:6] = couple[...]
    wide[1, 0:6] = readout[...]
    drive[...] = lax.dot_general(
        strain[...], wide[0], TN_DIMS, preferred_element_type=F32, precision=HIGHEST
    )
    base[...] = elastic[...] + lax.dot_general(
        wide[1], drive[...], NT_DIMS, preferred_element_type=F32, precision=HIGHEST
    )
    odd_dom = lax.axis_index("dom") & 1
    odd_box = lax.axis_index("box") & 1
    chosen[...] = jnp.zeros_like(chosen)
    chosen[0:1] = shared[pl.ds(1 - odd_dom, 1)]
    chosen[1:2] = shared[pl.ds(odd_dom, 1)]
    chosen[2:3] = shared[pl.ds(3 - odd_box, 1)]
    chosen[3:4] = shared[pl.ds(2 + odd_box, 1)]
    group = iota((groups, LANES), 0)
    lane = iota((groups, LANES), 1)
    total = jnp.zeros((2 * groups, LANES), F32)
    for m in range(4):
        nodes = chosen[m : m + 1]
        here = group == (nodes >> 7)
        marks = jnp.concatenate(
            [jnp.where(here, m + 1, 0), jnp.where(here, lane, 0)], axis=0
        ).astype(F32)
        total = total + lax.dot_general(
            marks.astype(BF),
            as_onehot(low_iota == (nodes & (LANES - 1))),
            NT_DIMS,
            preferred_element_type=F32,
        )
    total = total.astype(I32)
    inverse[0] = total[:groups] - 1
    inverse[1] = total[groups:]


def project_rows(table, masked, mass_inv, sorter, positions, *rest):
    dom_total = positions.shape[0]
    box_total = lax.axis_size("box")
    received = rest[:box_total]
    outs = rest[box_total : box_total + dom_total]
    held, turned, ordered = rest[box_total + dom_total :]
    capacity = received[0].shape[0]
    for k, block in enumerate(received):
        for s in range(capacity):
            held[k * capacity + s] = block[s]
    targets = masked.shape[0]
    entries = masked.shape[1] // LANES
    for t in range(targets):
        picked = [held[table[2 * dom_total + t * entries + l]] for l in range(entries)]
        numerator = jnp.dot(
            jnp.concatenate(picked, axis=1), masked[t], preferred_element_type=F32
        )
        turned[:, t * LANES : (t + 1) * LANES] = (numerator * mass_inv[t : t + 1]).astype(BF)
    sort = lax.dot_general(sorter[...], turned[...], NT_DIMS, preferred_element_type=F32)
    for g in range(ordered.shape[0]):
        ordered[g] = sort[g * LANES : (g + 1) * LANES].astype(BF)
    for k, out in enumerate(outs):
        for j in range(2):
            out[j * LANES : (j + 1) * LANES] = ordered[table[2 * k + j]]
        out[2 * LANES :] = positions[k]


def place(payloads, placing, rows):
    groups = placing.shape[0] // LANES
    low_iota = iota((LANES, LANES), 0).astype(F32).astype(BF)
    for k, payload in enumerate(payloads):
        rows[k * 2 * LANES : (k + 1) * 2 * LANES] = payload[: 2 * LANES]
        where = payload[2 * LANES :].astype(F32)
        for j in range(2):
            low = jnp.broadcast_to(where[2 + j : 3 + j], (LANES, LANES)).astype(BF)
            match = jnp.where(low_iota == low, jnp.ones_like(low), jnp.zeros_like(low))
            lanes = slice((2 * k + j) * LANES, (2 * k + j + 1) * LANES)
            for g in range(groups):
                here = jnp.where(where[j : j + 1] == g, 1.0, 0.0)
                placing[g * LANES : (g + 1) * LANES, lanes] = match * jnp.broadcast_to(
                    here, (LANES, LANES)
                ).astype(BF)
    return jnp.dot(placing[...], rows[...], preferred_element_type=F32)


def place_early(count, *refs):
    out, placing, rows = refs[count:]
    out[...] = place(refs[:count], placing, rows)


def finish(placed, count, *refs):
    payloads = refs[:count]
    early, base, size, connectivity, onehot, decay, readout, chosen = refs[count : count + 8]
    settled, local = refs[count + 8 : count + 10]
    exports = refs[count + 10 : count + 14]
    scratch = refs[count + 14 :]
    elements = base.shape[1]
    if placed:
        arrived = early[...]
    else:
        arrived = (early[...] + place(payloads, *scratch)).astype(BF)
    settled[...] = arrived
    taken = readout[...] * decay[...]
    taken = jnp.concatenate([taken, jnp.zeros((SUBS - 6, LANES), F32)], axis=0)
    share = lax.dot_general(
        jnp.concatenate(pieces(taken, 3), axis=0), arrived, NT_DIMS, preferred_element_type=F32
    )
    stress = base[...] + (share[0:SUBS] + share[SUBS : 2 * SUBS] + share[2 * SUBS : 3 * SUBS])
    row = iota((3 * SUBS, 2 * SUBS), 0)
    column = iota((3 * SUBS, 2 * SUBS), 1) & (SUBS - 1)
    spread = jnp.zeros(row.shape, I32)
    for i in range(3):
        for c in range(3):
            spread = jnp.where(
                ((row >> 3) == i) & (column == TENSOR[i][c]),
                2 * ((row >> c) & 1) - 1,
                spread,
            )
    forces = jnp.dot(
        spread.astype(F32).astype(BF),
        jnp.concatenate(pieces(stress, 2), axis=0),
        preferred_element_type=F32,
    )
    edge = size[...]
    forces = forces * (edge * edge * 0.25)
    group = iota((SUBS, elements), 0)
    halves = [jnp.zeros((6 * SUBS, LANES), F32) for _ in range(2)]
    for a in range(SUBS):
        here = group == (connectivity[a : a + 1] >> 7)
        highs, lows = [], []
        for i in range(3):
            value = jnp.where(here, forces[i * SUBS + a : i * SUBS + a + 1], 0.0)
            high, low = pieces(value, 2)
            highs.append(high)
            lows.append(low)
        halves[a % 2] = halves[a % 2] + jnp.dot(
            jnp.concatenate(highs + lows, axis=0), onehot[a], preferred_element_type=F32
        )
    total = halves[0] + halves[1]
    nodes = chosen[...]
    for i in range(3):
        summed = (
            total[i * SUBS : (i + 1) * SUBS] + total[(3 + i) * SUBS : (4 + i) * SUBS]
        )
        local[i] = summed
        got = lookup([summed[r : r + 1] for r in range(SUBS)], nodes)
        for m, out in enumerate(exports):
            out[i : i + 1] = got[m : m + 1]


def relax(arrived, drive, decay, history):
    history[...] = (arrived[...].astype(F32) * decay[...] + drive[...]).astype(BF)


def add_shared(local, inverse, *rest):
    received, force = rest[:-1], rest[-1]
    row, column = inverse[0], inverse[1]
    for i in range(local.shape[0]):
        total = local[i]
        for m, got in enumerate(received):
            share = jnp.take_along_axis(
                jnp.broadcast_to(got[i : i + 1], column.shape),
                column,
                axis=1,
                mode="promise_in_bounds",
            )
            total = total + jnp.where(row == m, share, 0.0)
        for r in range(local.shape[1]):
            force[i : i + 1, r * LANES : (r + 1) * LANES] = total[r : r + 1]


VMEM = pl.BlockSpec(memory_space=pltpu.VMEM)
SMEM = pl.BlockSpec(memory_space=pltpu.SMEM)
HBM = pl.BlockSpec(memory_space=pltpu.HBM)


def call(kernel, name, ins, outs, scratch, args, cost=100_000, out_specs=None):
    single = not isinstance(outs, (list, tuple))
    return pl.pallas_call(
        kernel,
        name=name,
        out_shape=outs,
        in_specs=ins,
        out_specs=out_specs or (VMEM if single else [VMEM] * len(outs)),
        scratch_shapes=scratch,
        cost_estimate=pl.CostEstimate(flops=1000, bytes_accessed=cost, transcendentals=0),
        compiler_params=pltpu.CompilerParams(vmem_limit_bytes=24 * 1024 * 1024),
    )(*args)


def swaps(axis, first):
    total = lax.axis_size(axis)
    pairs = []
    for i in range(first, total - 1, 2):
        pairs += [(i, i + 1), (i + 1, i)]
    return pairs


def arrays(shape, dtype):
    return jax.ShapeDtypeStruct(shape, dtype)


def exclusive_order(targets, choice_total):
    one_hot = (targets[:, None] == jnp.arange(choice_total, dtype=I32)[None, :]).astype(I32)
    return jnp.sum((jnp.cumsum(one_hot, axis=0) - one_hot) * one_hot, axis=1)


def spread_rows(received, entry_slot, entry_count, weights, owner_route, owner_slot):
    targets, entries = entry_slot.shape
    block_size = weights.shape[-1]
    capacity, width, _ = received[0].shape
    me = lax.axis_index("box")
    stacked = jnp.concatenate(received, axis=0)
    held = ((entry_slot // capacity) ^ me) * capacity + entry_slot % capacity
    live = (jnp.arange(entries, dtype=I32)[None, :] < entry_count[:, None]).astype(BF)
    mass = jnp.einsum("tl,tlij->tj", live, weights, preferred_element_type=F32)
    picked = stacked[held] * live[:, :, None, None]
    numerator = jnp.einsum("tlhi,tlij->tjh", picked, weights, preferred_element_type=F32)
    projected = (numerator / mass[:, :, None]).astype(BF).reshape(targets * block_size, width)
    total = projected.shape[0]
    dom_total = lax.axis_size("dom")
    owner_capacity = 2 * (total // dom_total)
    place = owner_route * owner_capacity + exclusive_order(owner_route, dom_total)
    rows = jnp.zeros((dom_total * owner_capacity, width), BF).at[place].set(projected)
    spots = jnp.full((dom_total * owner_capacity,), total, I32).at[place].set(owner_slot)
    rows = lax.all_to_all(
        rows.reshape(dom_total, owner_capacity, width), "dom", 0, 0, tiled=True
    )
    spots = lax.all_to_all(spots.reshape(dom_total, owner_capacity), "dom", 0, 0, tiled=True)
    return (
        jnp.zeros((total, width), BF)
        .at[spots.reshape(-1)]
        .set(rows.reshape(-1, width), mode="drop")
    )


def body(old_history, box_route, entry_slot, entry_count, weights, owner_route, owner_slot,
         connectivity, shared_nodes, node_motion, elem_size, decay, couple, readout):
    blocks, width, block_size = old_history.shape
    targets, entries = entry_slot.shape
    box_total = lax.axis_size("box")
    dom_total = lax.axis_size("dom")
    capacity = blocks // 2
    rows = targets * block_size
    row_groups = rows // LANES
    elements = connectivity.shape[1]
    nodes = node_motion.shape[1]

    packed = call(
        pack_blocks, "pack_blocks", [HBM, HBM],
        [arrays((capacity, width, block_size), BF)] * box_total,
        [
            pltpu.SMEM((box_total * capacity,), I32),
            pltpu.SMEM((blocks,), I32),
            pltpu.VMEM(old_history.shape, BF),
            pltpu.SemaphoreType.DMA((2,)),
        ],
        (box_route, old_history),
    )
    received = {0: packed[0]}
    for k in [k for k in range(2, box_total)] + [1]:
        received[k] = lax.ppermute(packed[k], "box", [(i, i ^ k) for i in range(box_total)])
    received = [received[k] for k in range(box_total)]
    flat_weights = weights.reshape(targets, entries * block_size, block_size)
    edge = elem_size.reshape(1, elements)
    drive, base, onehot, chosen, inverse = call(
        element_parts, "element_parts", [VMEM] * 6,
        [
            arrays((elements, width), F32),
            arrays((SUBS, elements), F32),
            arrays((connectivity.shape[0], elements, LANES), BF),
            arrays((SUBS, shared_nodes.shape[1]), I32),
            arrays((2, nodes // LANES, LANES), I32),
        ],
        [
            pltpu.VMEM((SUBS, elements), F32),
            pltpu.VMEM((SUBS, elements), F32),
            pltpu.VMEM((2, SUBS, width), F32),
        ],
        (connectivity, node_motion, edge, couple.T, readout.T, shared_nodes),
    )
    usual = rows // dom_total
    relaxing = decay.reshape(1, width)
    if usual == LANES:
        sorter, positions, table, mass_inv, masked = call(
            functools.partial(sort_rows, capacity), "sort_rows", [HBM] * 5,
            [
                arrays((rows, rows), BF),
                arrays((dom_total, POS_ROWS, LANES), BF),
                arrays((2 * dom_total + targets * entries,), I32),
                arrays((targets, block_size), F32),
                arrays(flat_weights.shape, BF),
            ],
            [
                pltpu.VMEM((row_groups, LANES), F32),
                pltpu.VMEM((row_groups, LANES), F32),
                pltpu.SMEM((dom_total + 1,), I32),
                pltpu.SMEM((entries, targets), I32),
                pltpu.SMEM((targets,), I32),
                pltpu.VMEM((row_groups, LANES), I32),
                pltpu.VMEM((1, rows), I32),
                pltpu.SemaphoreType.DMA((5,)),
            ],
            (
                entry_slot.T,
                entry_count,
                owner_route.reshape(row_groups, LANES),
                owner_slot.reshape(1, rows),
                flat_weights,
            ),
            out_specs=[VMEM, VMEM, SMEM, VMEM, VMEM],
        )
        payload = arrays((2 * usual + POS_ROWS, width), BF)
        outgoing = call(
            project_rows, "project_rows", [SMEM] + [VMEM] * (4 + box_total),
            [payload] * dom_total,
            [
                pltpu.VMEM((box_total * capacity, width, block_size), BF),
                pltpu.VMEM((width, rows), BF),
                pltpu.VMEM((row_groups, LANES, width), BF),
            ],
            (table, masked, mass_inv, sorter, positions, *received),
        )
        far = dom_total // 2
        order = [*range(far, dom_total), *range(2, far), 1]
        payloads = {0: outgoing[0]}
        for k in order:
            payloads[k] = lax.ppermute(
                outgoing[k], "dom", [(i, i ^ k) for i in range(dom_total)]
            )
        soon = [0, *range(1, far + 1)]
        late = [payloads[k] for k in range(far + 1, dom_total)]

        def placing(count):
            return [
                pltpu.VMEM((elements, count * 2 * usual), BF),
                pltpu.VMEM((count * 2 * usual, width), BF),
            ]

        early = call(
            functools.partial(place_early, len(soon)), "place_early", [VMEM] * len(soon),
            arrays((elements, width), F32), placing(len(soon)), [payloads[k] for k in soon],
        )
        placed, scratch = False, placing(len(late))
    else:
        early = spread_rows(received, entry_slot, entry_count, weights, owner_route, owner_slot)
        late = []
        placed, scratch = True, []
    export = arrays((3, shared_nodes.shape[1]), F32)
    arrived, local, *exports = call(
        functools.partial(finish, placed, len(late)), "finish",
        [VMEM] * (len(late) + 8),
        [arrays((elements, width), BF), arrays((3, nodes // LANES, LANES), F32)] + [export] * 4,
        scratch,
        (*late, early, base, edge, connectivity, onehot, relaxing, readout.T, chosen),
    )
    history = call(
        relax, "relax", [VMEM] * 3, arrays((elements, width), BF), [], (arrived, drive, relaxing)
    )
    halo = [None] * 4
    for m, axis, first in ((3, "box", 1), (1, "dom", 1), (0, "dom", 0), (2, "box", 0)):
        halo[m] = lax.ppermute(exports[m], axis, swaps(axis, first))
    force = call(
        add_shared, "add_shared", [VMEM] * (2 + len(halo)), arrays((3, nodes), F32), [],
        (local, inverse, *halo),
    )
    return history, force


def solution(mesh):
    return jax.shard_map(
        body,
        mesh=mesh,
        in_specs=(
            P(("dom", "box"), None, None),
            P(("dom", "box")),
            P(("dom", "box"), None),
            P(("dom", "box")),
            P(("dom", "box"), None, None, None),
            P(("dom", "box")),
            P(("dom", "box")),
            P(None, ("dom", "box")),
            P(None, ("dom", "box")),
            P(None, ("dom", "box")),
            P(("dom", "box")),
            P(),
            P(),
            P(),
        ),
        out_specs=(P(("dom", "box"), None), P(None, ("dom", "box"))),
        check_vma=False,
    )
```

```python
import functools

import jax
import jax.numpy as jnp
from jax import lax
from jax.experimental import pallas as pl
from jax.experimental.pallas import tpu as pltpu
from jax.sharding import PartitionSpec as P


BF = jnp.bfloat16
F32 = jnp.float32
I32 = jnp.int32
LANES = 128
SUBS = 8
POS_ROWS = 16
NOWHERE = 16.0
TENSOR = ((0, 3, 5), (3, 1, 4), (5, 4, 2))
NT_DIMS = (((1,), (1,)), ((), ()))
TN_DIMS = (((0,), (0,)), ((), ()))
HIGHEST = lax.Precision.HIGHEST


def iota(shape, dim):
    return lax.broadcasted_iota(I32, shape, dim)


def pieces(x, count):
    out = []
    for _ in range(count - 1):
        high = x.astype(BF)
        out.append(high)
        x = x - high.astype(F32)
    out.append(x.astype(BF))
    return out


def as_onehot(mask):
    return jnp.where(mask, 1.0, 0.0).astype(BF)


def lookup(rows, index):
    low = index & (LANES - 1)
    high = index >> 7
    out = jnp.zeros(index.shape, F32)
    for r, row in enumerate(rows):
        got = jnp.take_along_axis(
            jnp.broadcast_to(row, index.shape), low, axis=1, mode="promise_in_bounds"
        )
        out = jnp.where(high == r, got, out)
    return out


def pack_blocks(route, old, *rest):
    outs, table = rest[:-1], rest[-1]
    me = lax.axis_index("box")
    capacity = outs[0].shape[0]
    for m in range(len(outs) * capacity):
        table[m] = 0
    routes = [route[i] for i in range(old.shape[0])]
    for i, target in enumerate(routes):
        order = jnp.int32(0)
        for earlier in routes[:i]:
            order = order + (earlier == target).astype(I32)
        table[(target ^ me) * capacity + order] = i
    for k, out in enumerate(outs):
        for s in range(capacity):
            out[s] = old[table[k * capacity + s]]


def mark_places(target, column, high, low):
    low_iota = iota((LANES, LANES), 0).astype(F32).astype(BF)
    low = jnp.broadcast_to(low, (LANES, LANES)).astype(BF)
    match = jnp.where(low_iota == low, jnp.ones_like(low), jnp.zeros_like(low))
    lanes = slice(column * LANES, (column + 1) * LANES)
    for g in range(target.shape[0] // LANES):
        here = jnp.broadcast_to(jnp.where(high == g, 1.0, 0.0), (LANES, LANES)).astype(BF)
        target[g * LANES : (g + 1) * LANES, lanes] = match * here


def sort_rows(owner_route, owner_slot, sorter, positions, table, high_rows, low_rows, starts):
    dom_total = positions.shape[0]
    row_groups = owner_route.shape[0]
    rows = row_groups * LANES
    me = lax.axis_index("dom")
    route = owner_route[...]
    picks = jnp.concatenate([as_onehot(route == d) for d in range(dom_total)], axis=0)
    span = dom_total * row_groups
    ahead = as_onehot(iota((LANES, LANES), 0) < iota((LANES, LANES), 1))
    within = jnp.dot(picks, ahead, preferred_element_type=F32)
    totals = jnp.dot(picks, jnp.ones((LANES, LANES), BF), preferred_element_type=F32).astype(BF)
    before = as_onehot(iota((span, span), 1) < iota((span, span), 0))
    base = jnp.dot(before, totals, preferred_element_type=F32)
    ranked = within + base
    place = jnp.zeros((row_groups, LANES), F32)
    for d in range(dom_total):
        place = jnp.where(route == d, ranked[d * row_groups : (d + 1) * row_groups], place)
        starts[d] = jnp.max(base[d * row_groups : d * row_groups + 1]).astype(I32)
    starts[dom_total] = rows
    place = place.astype(I32)
    high = (place >> 7).astype(F32)
    low = (place & (LANES - 1)).astype(F32)
    for g in range(row_groups):
        mark_places(sorter, g, high[g : g + 1], low[g : g + 1])
    spot = owner_slot[...]
    which = iota((POS_ROWS, rows), 0)
    parts = jnp.where(which == 0, spot >> 7, jnp.where(which == 1, spot & (LANES - 1), 0))
    ordered = lax.dot_general(
        parts.astype(F32).astype(BF), sorter[...], NT_DIMS, preferred_element_type=F32
    )
    for g in range(row_groups):
        high_rows[g : g + 1] = ordered[0:1, g * LANES : (g + 1) * LANES]
        low_rows[g : g + 1] = ordered[1:2, g * LANES : (g + 1) * LANES]
    which = iota((POS_ROWS, LANES), 0)
    for k in range(dom_total):
        owner = me ^ k
        start = starts[owner]
        held = starts[owner + 1] - start
        block = jnp.zeros((POS_ROWS, LANES), F32)
        for j in range(2):
            chunk = jnp.minimum(start // LANES + j, row_groups - 1)
            table[2 * k + j] = chunk
            high = jnp.where(held > j * LANES, high_rows[pl.ds(chunk, 1)], NOWHERE)
            block = jnp.where(which == j, high, block)
            block = jnp.where(which == 2 + j, low_rows[pl.ds(chunk, 1)], block)
        positions[k] = block.astype(BF)


def mask_weights(capacity, slot, count, weights, masked, mass_inv, blocks):
    targets = weights.shape[0]
    entries = weights.shape[1] // LANES
    box = lax.axis_index("box")
    for t in range(targets):
        total = jnp.zeros((1, LANES), F32)
        for l in range(entries):
            live = l < count[t]
            span = slice(l * LANES, (l + 1) * LANES)
            part = weights[t, span, :]
            part = jnp.where(live, part, jnp.zeros_like(part))
            masked[t, span, :] = part
            total = total + jnp.sum(part.astype(F32), axis=0, keepdims=True)
            entry = jnp.where(live, slot[l, t], slot[0, t])
            source = lax.div(entry, capacity) ^ box
            blocks[t * entries + l] = source * capacity + lax.rem(entry, capacity)
        mass_inv[t : t + 1] = 1.0 / total


def element_parts(connectivity, motion, size, couple, readout, shared, drive, base, onehot,
                  chosen, inverse, strain, elastic, wide):
    elements = connectivity.shape[1]
    corners = connectivity.shape[0]
    groups = motion.shape[1] // LANES
    corner = iota((corners, LANES), 0)
    signs = [(2 * ((corner >> c) & 1) - 1).astype(F32) for c in range(3)]
    low_iota = iota((LANES, LANES), 0)
    lane_iota = iota((LANES, LANES), 1).astype(F32)
    strain[...] = jnp.zeros_like(strain)
    elastic[...] = jnp.zeros_like(elastic)
    for j in range(elements // LANES):
        lanes = slice(j * LANES, (j + 1) * LANES)
        nodes = connectivity[:, lanes]
        scale = 1.0 / (4.0 * size[:, lanes])
        grad = []
        for i in range(3):
            moved = lookup(
                [motion[i : i + 1, r * LANES : (r + 1) * LANES] for r in range(groups)], nodes
            )
            grad.append(
                [jnp.sum(moved * signs[c], axis=0, keepdims=True) * scale for c in range(3)]
            )
        rows = [
            grad[0][0],
            grad[1][1],
            grad[2][2],
            grad[0][1] + grad[1][0],
            grad[1][2] + grad[2][1],
            grad[2][0] + grad[0][2],
        ]
        volume = 1.2 * (rows[0] + rows[1] + rows[2])
        for c in range(6):
            strain[c : c + 1, lanes] = rows[c]
            elastic[c : c + 1, lanes] = volume + 1.6 * rows[c] if c < 3 else 0.8 * rows[c]
        turned = (nodes & (LANES - 1)).astype(F32).T
        for a in range(corners):
            onehot[a, lanes, :] = as_onehot(lane_iota == turned[:, a : a + 1])
    wide[...] = jnp.zeros_like(wide)
    wide[0, 0:6] = couple[...]
    wide[1, 0:6] = readout[...]
    drive[...] = lax.dot_general(
        strain[...], wide[0], TN_DIMS, preferred_element_type=F32, precision=HIGHEST
    )
    base[...] = elastic[...] + lax.dot_general(
        wide[1], drive[...], NT_DIMS, preferred_element_type=F32, precision=HIGHEST
    )
    odd_dom = lax.axis_index("dom") & 1
    odd_box = lax.axis_index("box") & 1
    chosen[...] = jnp.zeros_like(chosen)
    chosen[0:1] = shared[pl.ds(1 - odd_dom, 1)]
    chosen[1:2] = shared[pl.ds(odd_dom, 1)]
    chosen[2:3] = shared[pl.ds(3 - odd_box, 1)]
    chosen[3:4] = shared[pl.ds(2 + odd_box, 1)]
    group = iota((groups, LANES), 0)
    lane = iota((groups, LANES), 1)
    total = jnp.zeros((2 * groups, LANES), F32)
    for m in range(4):
        nodes = chosen[m : m + 1]
        here = group == (nodes >> 7)
        marks = jnp.concatenate(
            [jnp.where(here, m + 1, 0), jnp.where(here, lane, 0)], axis=0
        ).astype(F32)
        total = total + lax.dot_general(
            marks.astype(BF),
            as_onehot(low_iota == (nodes & (LANES - 1))),
            NT_DIMS,
            preferred_element_type=F32,
        )
    total = total.astype(I32)
    inverse[0] = total[:groups] - 1
    inverse[1] = total[groups:]


def project_rows(table, blocks, masked, mass_inv, sorter, positions, *rest):
    dom_total = positions.shape[0]
    box_total = lax.axis_size("box")
    received = rest[:box_total]
    outs = rest[box_total : box_total + dom_total]
    held, turned, ordered = rest[box_total + dom_total :]
    capacity = received[0].shape[0]
    for k, block in enumerate(received):
        for s in range(capacity):
            held[k * capacity + s] = block[s]
    targets = masked.shape[0]
    entries = masked.shape[1] // LANES
    for t in range(targets):
        picked = [held[blocks[t * entries + l]] for l in range(entries)]
        numerator = jnp.dot(
            jnp.concatenate(picked, axis=1), masked[t], preferred_element_type=F32
        )
        turned[:, t * LANES : (t + 1) * LANES] = (numerator * mass_inv[t : t + 1]).astype(BF)
    sort = lax.dot_general(sorter[...], turned[...], NT_DIMS, preferred_element_type=F32)
    for g in range(ordered.shape[0]):
        ordered[g] = sort[g * LANES : (g + 1) * LANES].astype(BF)
    for k, out in enumerate(outs):
        for j in range(2):
            out[j * LANES : (j + 1) * LANES] = ordered[table[2 * k + j]]
        out[2 * LANES :] = positions[k]


def place(payloads, placing, rows):
    for k, payload in enumerate(payloads):
        rows[k * 2 * LANES : (k + 1) * 2 * LANES] = payload[: 2 * LANES]
        where = payload[2 * LANES :].astype(F32)
        for j in range(2):
            mark_places(placing, 2 * k + j, where[j : j + 1], where[2 + j : 3 + j])
    return jnp.dot(placing[...], rows[...], preferred_element_type=F32)


def place_early(count, *refs):
    out, placing, rows = refs[count:]
    out[...] = place(refs[:count], placing, rows)


def finish(placed, count, *refs):
    payloads = refs[:count]
    early, base, size, connectivity, onehot, decay, readout, chosen = refs[count : count + 8]
    settled, local = refs[count + 8 : count + 10]
    exports = refs[count + 10 : count + 14]
    scratch = refs[count + 14 :]
    elements = base.shape[1]
    if placed:
        arrived = early[...]
    else:
        arrived = (early[...] + place(payloads, *scratch)).astype(BF)
    settled[...] = arrived
    taken = readout[...] * decay[...]
    taken = jnp.concatenate([taken, jnp.zeros((SUBS - 6, LANES), F32)], axis=0)
    share = lax.dot_general(
        jnp.concatenate(pieces(taken, 3), axis=0), arrived, NT_DIMS, preferred_element_type=F32
    )
    stress = base[...] + (share[0:SUBS] + share[SUBS : 2 * SUBS] + share[2 * SUBS : 3 * SUBS])
    row = iota((3 * SUBS, 2 * SUBS), 0)
    column = iota((3 * SUBS, 2 * SUBS), 1) & (SUBS - 1)
    spread = jnp.zeros(row.shape, I32)
    for i in range(3):
        for c in range(3):
            spread = jnp.where(
                ((row >> 3) == i) & (column == TENSOR[i][c]),
                2 * ((row >> c) & 1) - 1,
                spread,
            )
    forces = jnp.dot(
        spread.astype(F32).astype(BF),
        jnp.concatenate(pieces(stress, 2), axis=0),
        preferred_element_type=F32,
    )
    edge = size[...]
    forces = forces * (edge * edge * 0.25)
    group = iota((SUBS, elements), 0)
    halves = [jnp.zeros((6 * SUBS, LANES), F32) for _ in range(2)]
    for a in range(SUBS):
        here = group == (connectivity[a : a + 1] >> 7)
        highs, lows = [], []
        for i in range(3):
            value = jnp.where(here, forces[i * SUBS + a : i * SUBS + a + 1], 0.0)
            high, low = pieces(value, 2)
            highs.append(high)
            lows.append(low)
        halves[a % 2] = halves[a % 2] + jnp.dot(
            jnp.concatenate(highs + lows, axis=0), onehot[a], preferred_element_type=F32
        )
    total = halves[0] + halves[1]
    nodes = chosen[...]
    for i in range(3):
        summed = (
            total[i * SUBS : (i + 1) * SUBS] + total[(3 + i) * SUBS : (4 + i) * SUBS]
        )
        local[i] = summed
        got = lookup([summed[r : r + 1] for r in range(SUBS)], nodes)
        for m, out in enumerate(exports):
            out[i : i + 1] = got[m : m + 1]


def relax(arrived, drive, decay, history):
    history[...] = (arrived[...].astype(F32) * decay[...] + drive[...]).astype(BF)


def add_shared(local, inverse, *rest):
    received, force = rest[:-1], rest[-1]
    row, column = inverse[0], inverse[1]
    for i in range(local.shape[0]):
        total = local[i]
        for m, got in enumerate(received):
            share = jnp.take_along_axis(
                jnp.broadcast_to(got[i : i + 1], column.shape),
                column,
                axis=1,
                mode="promise_in_bounds",
            )
            total = total + jnp.where(row == m, share, 0.0)
        for r in range(local.shape[1]):
            force[i : i + 1, r * LANES : (r + 1) * LANES] = total[r : r + 1]


VMEM = pl.BlockSpec(memory_space=pltpu.VMEM)
SMEM = pl.BlockSpec(memory_space=pltpu.SMEM)


def call(kernel, ins, outs, scratch, args, cost=100_000, out_specs=None):
    single = not isinstance(outs, (list, tuple))
    return pl.pallas_call(
        kernel,
        out_shape=outs,
        in_specs=ins,
        out_specs=out_specs or (VMEM if single else [VMEM] * len(outs)),
        scratch_shapes=scratch,
        cost_estimate=pl.CostEstimate(flops=1000, bytes_accessed=cost, transcendentals=0),
        compiler_params=pltpu.CompilerParams(vmem_limit_bytes=24 * 1024 * 1024),
    )(*args)


def swaps(axis, first):
    total = lax.axis_size(axis)
    pairs = []
    for i in range(first, total - 1, 2):
        pairs += [(i, i + 1), (i + 1, i)]
    return pairs


def arrays(shape, dtype):
    return jax.ShapeDtypeStruct(shape, dtype)


def exclusive_order(targets, choice_total):
    one_hot = (targets[:, None] == jnp.arange(choice_total, dtype=I32)[None, :]).astype(I32)
    return jnp.sum((jnp.cumsum(one_hot, axis=0) - one_hot) * one_hot, axis=1)


def spread_rows(received, entry_slot, entry_count, weights, owner_route, owner_slot):
    targets, entries = entry_slot.shape
    block_size = weights.shape[-1]
    capacity, width, _ = received[0].shape
    me = lax.axis_index("box")
    stacked = jnp.concatenate(received, axis=0)
    held = ((entry_slot // capacity) ^ me) * capacity + entry_slot % capacity
    live = (jnp.arange(entries, dtype=I32)[None, :] < entry_count[:, None]).astype(BF)
    mass = jnp.einsum("tl,tlij->tj", live, weights, preferred_element_type=F32)
    picked = stacked[held] * live[:, :, None, None]
    numerator = jnp.einsum("tlhi,tlij->tjh", picked, weights, preferred_element_type=F32)
    projected = (numerator / mass[:, :, None]).astype(BF).reshape(targets * block_size, width)
    total = projected.shape[0]
    dom_total = lax.axis_size("dom")
    owner_capacity = 2 * (total // dom_total)
    place = owner_route * owner_capacity + exclusive_order(owner_route, dom_total)
    rows = jnp.zeros((dom_total * owner_capacity, width), BF).at[place].set(projected)
    spots = jnp.full((dom_total * owner_capacity,), total, I32).at[place].set(owner_slot)
    rows = lax.all_to_all(
        rows.reshape(dom_total, owner_capacity, width), "dom", 0, 0, tiled=True
    )
    spots = lax.all_to_all(spots.reshape(dom_total, owner_capacity), "dom", 0, 0, tiled=True)
    return (
        jnp.zeros((total, width), BF)
        .at[spots.reshape(-1)]
        .set(rows.reshape(-1, width), mode="drop")
    )


def body(old_history, box_route, entry_slot, entry_count, weights, owner_route, owner_slot,
         connectivity, shared_nodes, node_motion, elem_size, decay, couple, readout):
    blocks, width, block_size = old_history.shape
    targets, entries = entry_slot.shape
    box_total = lax.axis_size("box")
    dom_total = lax.axis_size("dom")
    capacity = blocks // 2
    rows = targets * block_size
    row_groups = rows // LANES
    elements = connectivity.shape[1]
    nodes = node_motion.shape[1]

    packed = call(
        pack_blocks, [SMEM, VMEM],
        [arrays((capacity, width, block_size), BF)] * box_total,
        [pltpu.SMEM((box_total * capacity,), I32)],
        (box_route, old_history),
    )
    received = {0: packed[0]}
    for k in [k for k in range(2, box_total)] + [1]:
        received[k] = lax.ppermute(packed[k], "box", [(i, i ^ k) for i in range(box_total)])
    received = [received[k] for k in range(box_total)]
    flat_weights = weights.reshape(targets, entries * block_size, block_size)
    edge = elem_size.reshape(1, elements)
    drive, base, onehot, chosen, inverse = call(
        element_parts, [VMEM] * 6,
        [
            arrays((elements, width), F32),
            arrays((SUBS, elements), F32),
            arrays((connectivity.shape[0], elements, LANES), BF),
            arrays((SUBS, shared_nodes.shape[1]), I32),
            arrays((2, nodes // LANES, LANES), I32),
        ],
        [
            pltpu.VMEM((SUBS, elements), F32),
            pltpu.VMEM((SUBS, elements), F32),
            pltpu.VMEM((2, SUBS, width), F32),
        ],
        (connectivity, node_motion, edge, couple.T, readout.T, shared_nodes),
    )
    usual = rows // dom_total
    relaxing = decay.reshape(1, width)
    if usual == LANES:
        sorter, positions, table = call(
            sort_rows, [VMEM, VMEM],
            [
                arrays((rows, rows), BF),
                arrays((dom_total, POS_ROWS, LANES), BF),
                arrays((2 * dom_total,), I32),
            ],
            [
                pltpu.VMEM((row_groups, LANES), F32),
                pltpu.VMEM((row_groups, LANES), F32),
                pltpu.SMEM((dom_total + 1,), I32),
            ],
            (owner_route.reshape(row_groups, LANES), owner_slot.reshape(1, rows)),
            out_specs=[VMEM, VMEM, SMEM],
        )
        masked, mass_inv, block_of = call(
            functools.partial(mask_weights, capacity), [SMEM, SMEM, VMEM],
            [
                arrays(flat_weights.shape, BF),
                arrays((targets, block_size), F32),
                arrays((targets * entries,), I32),
            ],
            [],
            (entry_slot.T, entry_count, flat_weights),
            out_specs=[VMEM, VMEM, SMEM],
        )
        payload = arrays((2 * usual + POS_ROWS, width), BF)
        outgoing = call(
            project_rows, [SMEM, SMEM] + [VMEM] * (4 + box_total),
            [payload] * dom_total,
            [
                pltpu.VMEM((box_total * capacity, width, block_size), BF),
                pltpu.VMEM((width, rows), BF),
                pltpu.VMEM((row_groups, LANES, width), BF),
            ],
            (table, block_of, masked, mass_inv, sorter, positions, *received),
        )
        far = dom_total // 2
        payloads = {0: outgoing[0]}
        for k in range(1, dom_total):
            payloads[k] = lax.ppermute(outgoing[k], "dom", [(i, i ^ k) for i in range(dom_total)])
        soon = [0, *range(1, far + 1)]
        late = [payloads[k] for k in range(far + 1, dom_total)]

        def placing(count):
            return [
                pltpu.VMEM((elements, count * 2 * usual), BF),
                pltpu.VMEM((count * 2 * usual, width), BF),
            ]

        early = call(
            functools.partial(place_early, len(soon)), [VMEM] * len(soon),
            arrays((elements, width), F32), placing(len(soon)), [payloads[k] for k in soon],
        )
        placed, scratch = False, placing(len(late))
    else:
        early = spread_rows(received, entry_slot, entry_count, weights, owner_route, owner_slot)
        late = []
        placed, scratch = True, []
    export = arrays((3, shared_nodes.shape[1]), F32)
    arrived, local, *exports = call(
        functools.partial(finish, placed, len(late)),
        [VMEM] * (len(late) + 8),
        [arrays((elements, width), BF), arrays((3, nodes // LANES, LANES), F32)] + [export] * 4,
        scratch,
        (*late, early, base, edge, connectivity, onehot, relaxing, readout.T, chosen),
    )
    history = call(relax, [VMEM] * 3, arrays((elements, width), BF), [], (arrived, drive, relaxing))
    halo = [None] * 4
    for m, axis, first in ((3, "box", 1), (1, "dom", 1), (0, "dom", 0), (2, "box", 0)):
        halo[m] = lax.ppermute(exports[m], axis, swaps(axis, first))
    force = call(
        add_shared, [VMEM] * (2 + len(halo)), arrays((3, nodes), F32), [],
        (local, inverse, *halo),
    )
    return history, force


def solution(mesh):
    return jax.shard_map(
        body,
        mesh=mesh,
        in_specs=(
            P(("dom", "box"), None, None),
            P(("dom", "box")),
            P(("dom", "box"), None),
            P(("dom", "box")),
            P(("dom", "box"), None, None, None),
            P(("dom", "box")),
            P(("dom", "box")),
            P(None, ("dom", "box")),
            P(None, ("dom", "box")),
            P(None, ("dom", "box")),
            P(("dom", "box")),
            P(),
            P(),
            P(),
        ),
        out_specs=(P(("dom", "box"), None), P(None, ("dom", "box"))),
        check_vma=False,
    )
```

```python
import functools

import jax
import jax.numpy as jnp
from jax import lax
from jax.experimental import pallas as pl
from jax.experimental.pallas import tpu as pltpu
from jax.sharding import PartitionSpec as P


BF = jnp.bfloat16
F32 = jnp.float32
I32 = jnp.int32
LANES = 128
SUBS = 8
POS_ROWS = 16
NOWHERE = 16.0
TENSOR = ((0, 3, 5), (3, 1, 4), (5, 4, 2))
NT_DIMS = (((1,), (1,)), ((), ()))
TN_DIMS = (((0,), (0,)), ((), ()))
HIGHEST = lax.Precision.HIGHEST


def iota(shape, dim):
    return lax.broadcasted_iota(I32, shape, dim)


def pieces(x, count):
    out = []
    for _ in range(count - 1):
        high = x.astype(BF)
        out.append(high)
        x = x - high.astype(F32)
    out.append(x.astype(BF))
    return out


def as_onehot(mask):
    return jnp.where(mask, 1.0, 0.0).astype(BF)


def lookup(rows, index):
    low = index & (LANES - 1)
    high = index >> 7
    out = jnp.zeros(index.shape, F32)
    for r, row in enumerate(rows):
        got = jnp.take_along_axis(
            jnp.broadcast_to(row, index.shape), low, axis=1, mode="promise_in_bounds"
        )
        out = jnp.where(high == r, got, out)
    return out


def pack_blocks(route, old, *rest):
    outs, table = rest[:-1], rest[-1]
    me = lax.axis_index("box")
    capacity = outs[0].shape[0]
    for m in range(len(outs) * capacity):
        table[m] = 0
    routes = [route[i] for i in range(old.shape[0])]
    for i, target in enumerate(routes):
        order = jnp.int32(0)
        for earlier in routes[:i]:
            order = order + (earlier == target).astype(I32)
        table[(target ^ me) * capacity + order] = i
    for k, out in enumerate(outs):
        for s in range(capacity):
            out[s] = old[table[k * capacity + s]]


def mark_places(target, column, high, low):
    low_iota = iota((LANES, LANES), 0).astype(F32).astype(BF)
    low = jnp.broadcast_to(low, (LANES, LANES)).astype(BF)
    match = jnp.where(low_iota == low, jnp.ones_like(low), jnp.zeros_like(low))
    lanes = slice(column * LANES, (column + 1) * LANES)
    for g in range(target.shape[0] // LANES):
        here = jnp.broadcast_to(jnp.where(high == g, 1.0, 0.0), (LANES, LANES)).astype(BF)
        target[g * LANES : (g + 1) * LANES, lanes] = match * here


def sort_rows(owner_route, owner_slot, sorter, positions, table, high_rows, low_rows, starts):
    dom_total = positions.shape[0]
    row_groups = owner_route.shape[0]
    rows = row_groups * LANES
    me = lax.axis_index("dom")
    route = owner_route[...]
    picks = jnp.concatenate([as_onehot(route == d) for d in range(dom_total)], axis=0)
    span = dom_total * row_groups
    ahead = as_onehot(iota((LANES, LANES), 0) < iota((LANES, LANES), 1))
    within = jnp.dot(picks, ahead, preferred_element_type=F32)
    totals = jnp.dot(picks, jnp.ones((LANES, LANES), BF), preferred_element_type=F32).astype(BF)
    before = as_onehot(iota((span, span), 1) < iota((span, span), 0))
    base = jnp.dot(before, totals, preferred_element_type=F32)
    ranked = within + base
    place = jnp.zeros((row_groups, LANES), F32)
    for d in range(dom_total):
        place = jnp.where(route == d, ranked[d * row_groups : (d + 1) * row_groups], place)
        starts[d] = jnp.max(base[d * row_groups : d * row_groups + 1]).astype(I32)
    starts[dom_total] = rows
    place = place.astype(I32)
    high = (place >> 7).astype(F32)
    low = (place & (LANES - 1)).astype(F32)
    for g in range(row_groups):
        mark_places(sorter, g, high[g : g + 1], low[g : g + 1])
    spot = owner_slot[...]
    which = iota((POS_ROWS, rows), 0)
    parts = jnp.where(which == 0, spot >> 7, jnp.where(which == 1, spot & (LANES - 1), 0))
    ordered = lax.dot_general(
        parts.astype(F32).astype(BF), sorter[...], NT_DIMS, preferred_element_type=F32
    )
    for g in range(row_groups):
        high_rows[g : g + 1] = ordered[0:1, g * LANES : (g + 1) * LANES]
        low_rows[g : g + 1] = ordered[1:2, g * LANES : (g + 1) * LANES]
    which = iota((POS_ROWS, LANES), 0)
    for k in range(dom_total):
        owner = me ^ k
        start = starts[owner]
        held = starts[owner + 1] - start
        block = jnp.zeros((POS_ROWS, LANES), F32)
        for j in range(2):
            chunk = jnp.minimum(start // LANES + j, row_groups - 1)
            table[2 * k + j] = chunk
            high = jnp.where(held > j * LANES, high_rows[pl.ds(chunk, 1)], NOWHERE)
            block = jnp.where(which == j, high, block)
            block = jnp.where(which == 2 + j, low_rows[pl.ds(chunk, 1)], block)
        positions[k] = block.astype(BF)


def mask_weights(capacity, slot, count, weights, masked, mass_inv, blocks):
    targets = weights.shape[0]
    entries = weights.shape[1] // LANES
    box = lax.axis_index("box")
    for t in range(targets):
        total = jnp.zeros((1, LANES), F32)
        for l in range(entries):
            live = l < count[t]
            span = slice(l * LANES, (l + 1) * LANES)
            part = weights[t, span, :]
            part = jnp.where(live, part, jnp.zeros_like(part))
            masked[t, span, :] = part
            total = total + jnp.sum(part.astype(F32), axis=0, keepdims=True)
            entry = jnp.where(live, slot[l, t], slot[0, t])
            source = lax.div(entry, capacity) ^ box
            blocks[t * entries + l] = source * capacity + lax.rem(entry, capacity)
        mass_inv[t : t + 1] = 1.0 / total


def element_parts(connectivity, motion, size, couple, readout, shared, drive, base, onehot,
                  chosen, inverse, strain, elastic, wide):
    elements = connectivity.shape[1]
    corners = connectivity.shape[0]
    groups = motion.shape[1] // LANES
    corner = iota((corners, LANES), 0)
    signs = [(2 * ((corner >> c) & 1) - 1).astype(F32) for c in range(3)]
    low_iota = iota((LANES, LANES), 0)
    lane_iota = iota((LANES, LANES), 1).astype(F32)
    strain[...] = jnp.zeros_like(strain)
    elastic[...] = jnp.zeros_like(elastic)
    for j in range(elements // LANES):
        lanes = slice(j * LANES, (j + 1) * LANES)
        nodes = connectivity[:, lanes]
        scale = 1.0 / (4.0 * size[:, lanes])
        grad = []
        for i in range(3):
            moved = lookup(
                [motion[i : i + 1, r * LANES : (r + 1) * LANES] for r in range(groups)], nodes
            )
            grad.append(
                [jnp.sum(moved * signs[c], axis=0, keepdims=True) * scale for c in range(3)]
            )
        rows = [
            grad[0][0],
            grad[1][1],
            grad[2][2],
            grad[0][1] + grad[1][0],
            grad[1][2] + grad[2][1],
            grad[2][0] + grad[0][2],
        ]
        volume = 1.2 * (rows[0] + rows[1] + rows[2])
        for c in range(6):
            strain[c : c + 1, lanes] = rows[c]
            elastic[c : c + 1, lanes] = volume + 1.6 * rows[c] if c < 3 else 0.8 * rows[c]
        turned = (nodes & (LANES - 1)).astype(F32).T
        for a in range(corners):
            onehot[a, lanes, :] = as_onehot(lane_iota == turned[:, a : a + 1])
    wide[...] = jnp.zeros_like(wide)
    wide[0, 0:6] = couple[...]
    wide[1, 0:6] = readout[...]
    drive[...] = lax.dot_general(
        strain[...], wide[0], TN_DIMS, preferred_element_type=F32, precision=HIGHEST
    )
    base[...] = elastic[...] + lax.dot_general(
        wide[1], drive[...], NT_DIMS, preferred_element_type=F32, precision=HIGHEST
    )
    odd_dom = lax.axis_index("dom") & 1
    odd_box = lax.axis_index("box") & 1
    chosen[...] = jnp.zeros_like(chosen)
    chosen[0:1] = shared[pl.ds(1 - odd_dom, 1)]
    chosen[1:2] = shared[pl.ds(odd_dom, 1)]
    chosen[2:3] = shared[pl.ds(3 - odd_box, 1)]
    chosen[3:4] = shared[pl.ds(2 + odd_box, 1)]
    group = iota((groups, LANES), 0)
    lane = iota((groups, LANES), 1)
    total = jnp.zeros((2 * groups, LANES), F32)
    for m in range(4):
        axis = "dom" if m < 2 else "box"
        here = lax.axis_index(axis)
        partner = here + (1 - 2 * (here & 1)) * (1 if m % 2 == 0 else -1)
        paired = (partner >= 0) & (partner < lax.axis_size(axis))
        nodes = jnp.where(paired, chosen[m : m + 1], groups * LANES)
        here = group == (nodes >> 7)
        marks = jnp.concatenate(
            [jnp.where(here, m + 1, 0), jnp.where(here, lane, 0)], axis=0
        ).astype(F32)
        total = total + lax.dot_general(
            marks.astype(BF),
            as_onehot(low_iota == (nodes & (LANES - 1))),
            NT_DIMS,
            preferred_element_type=F32,
        )
    total = total.astype(I32)
    inverse[0] = total[:groups] - 1
    inverse[1] = total[groups:]


def project_rows(table, blocks, masked, mass_inv, sorter, positions, *rest):
    dom_total = positions.shape[0]
    box_total = lax.axis_size("box")
    received = rest[:box_total]
    outs = rest[box_total : box_total + dom_total]
    held, turned, ordered = rest[box_total + dom_total :]
    capacity = received[0].shape[0]
    for k, block in enumerate(received):
        for s in range(capacity):
            held[k * capacity + s] = block[s]
    targets = masked.shape[0]
    entries = masked.shape[1] // LANES
    for t in range(targets):
        picked = [held[blocks[t * entries + l]] for l in range(entries)]
        numerator = jnp.dot(
            jnp.concatenate(picked, axis=1), masked[t], preferred_element_type=F32
        )
        turned[:, t * LANES : (t + 1) * LANES] = (numerator * mass_inv[t : t + 1]).astype(BF)
    sort = lax.dot_general(sorter[...], turned[...], NT_DIMS, preferred_element_type=F32)
    for g in range(ordered.shape[0]):
        ordered[g] = sort[g * LANES : (g + 1) * LANES].astype(BF)
    for k, out in enumerate(outs):
        for j in range(2):
            out[j * LANES : (j + 1) * LANES] = ordered[table[2 * k + j]]
        out[2 * LANES :] = positions[k]


def place(payloads, placing, rows):
    for k, payload in enumerate(payloads):
        rows[k * 2 * LANES : (k + 1) * 2 * LANES] = payload[: 2 * LANES]
        where = payload[2 * LANES :].astype(F32)
        for j in range(2):
            mark_places(placing, 2 * k + j, where[j : j + 1], where[2 + j : 3 + j])
    return jnp.dot(placing[...], rows[...], preferred_element_type=F32)


def place_early(count, *refs):
    out, placing, rows = refs[count:]
    out[...] = place(refs[:count], placing, rows)


def finish(placed, count, *refs):
    payloads = refs[:count]
    early, base, size, connectivity, onehot, decay, readout, chosen = refs[count : count + 8]
    settled, local = refs[count + 8 : count + 10]
    exports = refs[count + 10 : count + 14]
    scratch = refs[count + 14 :]
    elements = base.shape[1]
    if placed:
        arrived = early[...]
    else:
        arrived = (early[...] + place(payloads, *scratch)).astype(BF)
    settled[...] = arrived
    taken = readout[...] * decay[...]
    taken = jnp.concatenate([taken, jnp.zeros((SUBS - 6, LANES), F32)], axis=0)
    share = lax.dot_general(
        jnp.concatenate(pieces(taken, 3), axis=0), arrived, NT_DIMS, preferred_element_type=F32
    )
    stress = base[...] + (share[0:SUBS] + share[SUBS : 2 * SUBS] + share[2 * SUBS : 3 * SUBS])
    row = iota((3 * SUBS, 2 * SUBS), 0)
    column = iota((3 * SUBS, 2 * SUBS), 1) & (SUBS - 1)
    spread = jnp.zeros(row.shape, I32)
    for i in range(3):
        for c in range(3):
            spread = jnp.where(
                ((row >> 3) == i) & (column == TENSOR[i][c]),
                2 * ((row >> c) & 1) - 1,
                spread,
            )
    forces = jnp.dot(
        spread.astype(F32).astype(BF),
        jnp.concatenate(pieces(stress, 2), axis=0),
        preferred_element_type=F32,
    )
    edge = size[...]
    forces = forces * (edge * edge * 0.25)
    group = iota((SUBS, elements), 0)
    halves = [jnp.zeros((6 * SUBS, LANES), F32) for _ in range(2)]
    for a in range(SUBS):
        here = group == (connectivity[a : a + 1] >> 7)
        highs, lows = [], []
        for i in range(3):
            value = jnp.where(here, forces[i * SUBS + a : i * SUBS + a + 1], 0.0)
            high, low = pieces(value, 2)
            highs.append(high)
            lows.append(low)
        halves[a % 2] = halves[a % 2] + jnp.dot(
            jnp.concatenate(highs + lows, axis=0), onehot[a], preferred_element_type=F32
        )
    total = halves[0] + halves[1]
    nodes = chosen[...]
    for i in range(3):
        summed = (
            total[i * SUBS : (i + 1) * SUBS] + total[(3 + i) * SUBS : (4 + i) * SUBS]
        )
        local[i] = summed
        got = lookup([summed[r : r + 1] for r in range(SUBS)], nodes)
        for m, out in enumerate(exports):
            out[i : i + 1] = got[m : m + 1]


def relax(arrived, drive, decay, history):
    history[...] = (arrived[...].astype(F32) * decay[...] + drive[...]).astype(BF)


def add_shared(local, inverse, *rest):
    received, force = rest[:-1], rest[-1]
    row, column = inverse[0], inverse[1]
    for i in range(local.shape[0]):
        total = local[i]
        for m, got in enumerate(received):
            share = jnp.take_along_axis(
                jnp.broadcast_to(got[i : i + 1], column.shape),
                column,
                axis=1,
                mode="promise_in_bounds",
            )
            total = total + jnp.where(row == m, share, 0.0)
        for r in range(local.shape[1]):
            force[i : i + 1, r * LANES : (r + 1) * LANES] = total[r : r + 1]


VMEM = pl.BlockSpec(memory_space=pltpu.VMEM)
SMEM = pl.BlockSpec(memory_space=pltpu.SMEM)


def call(kernel, ins, outs, scratch, args, cost=2_000_000_000, out_specs=None):
    single = not isinstance(outs, (list, tuple))
    return pl.pallas_call(
        kernel,
        out_shape=outs,
        in_specs=ins,
        out_specs=out_specs or (VMEM if single else [VMEM] * len(outs)),
        scratch_shapes=scratch,
        cost_estimate=pl.CostEstimate(flops=cost, bytes_accessed=100_000, transcendentals=0),
        compiler_params=pltpu.CompilerParams(vmem_limit_bytes=24 * 1024 * 1024),
    )(*args)


def swaps(axis, first):
    total = lax.axis_size(axis)
    pairs = [(i, i + 1) for i in range(first, total - 1, 2)]
    left = sorted(set(range(total)) - {i for pair in pairs for i in pair})
    pairs += [(left[0], left[-1])] if left else []
    return [(a, b) for a, b in pairs] + [(b, a) for a, b in pairs if a != b]


def arrays(shape, dtype):
    return jax.ShapeDtypeStruct(shape, dtype)


def exclusive_order(targets, choice_total):
    one_hot = (targets[:, None] == jnp.arange(choice_total, dtype=I32)[None, :]).astype(I32)
    return jnp.sum((jnp.cumsum(one_hot, axis=0) - one_hot) * one_hot, axis=1)


def spread_rows(received, entry_slot, entry_count, weights, owner_route, owner_slot):
    targets, entries = entry_slot.shape
    block_size = weights.shape[-1]
    capacity, width, _ = received[0].shape
    me = lax.axis_index("box")
    stacked = jnp.concatenate(received, axis=0)
    held = ((entry_slot // capacity) ^ me) * capacity + entry_slot % capacity
    live = (jnp.arange(entries, dtype=I32)[None, :] < entry_count[:, None]).astype(BF)
    mass = jnp.einsum("tl,tlij->tj", live, weights, preferred_element_type=F32)
    picked = stacked[held] * live[:, :, None, None]
    numerator = jnp.einsum("tlhi,tlij->tjh", picked, weights, preferred_element_type=F32)
    projected = (numerator / mass[:, :, None]).astype(BF).reshape(targets * block_size, width)
    total = projected.shape[0]
    dom_total = lax.axis_size("dom")
    owner_capacity = 2 * (total // dom_total)
    place = owner_route * owner_capacity + exclusive_order(owner_route, dom_total)
    rows = jnp.zeros((dom_total * owner_capacity, width), BF).at[place].set(projected)
    spots = jnp.full((dom_total * owner_capacity,), total, I32).at[place].set(owner_slot)
    rows = lax.all_to_all(
        rows.reshape(dom_total, owner_capacity, width), "dom", 0, 0, tiled=True
    )
    spots = lax.all_to_all(spots.reshape(dom_total, owner_capacity), "dom", 0, 0, tiled=True)
    return (
        jnp.zeros((total, width), BF)
        .at[spots.reshape(-1)]
        .set(rows.reshape(-1, width), mode="drop")
    )


def body(old_history, box_route, entry_slot, entry_count, weights, owner_route, owner_slot,
         connectivity, shared_nodes, node_motion, elem_size, decay, couple, readout):
    blocks, width, block_size = old_history.shape
    targets, entries = entry_slot.shape
    box_total = lax.axis_size("box")
    dom_total = lax.axis_size("dom")
    capacity = blocks // 2
    rows = targets * block_size
    row_groups = rows // LANES
    elements = connectivity.shape[1]
    nodes = node_motion.shape[1]

    packed = call(
        pack_blocks, [SMEM, VMEM],
        [arrays((capacity, width, block_size), BF)] * box_total,
        [pltpu.SMEM((box_total * capacity,), I32)],
        (box_route, old_history),
    )
    received = {0: packed[0]}
    for k in [k for k in range(2, box_total)] + [1]:
        received[k] = lax.ppermute(packed[k], "box", [(i, i ^ k) for i in range(box_total)])
    received = [received[k] for k in range(box_total)]
    flat_weights = weights.reshape(targets, entries * block_size, block_size)
    edge = elem_size.reshape(1, elements)
    drive, base, onehot, chosen, inverse = call(
        element_parts, [VMEM] * 6,
        [
            arrays((elements, width), F32),
            arrays((SUBS, elements), F32),
            arrays((connectivity.shape[0], elements, LANES), BF),
            arrays((SUBS, shared_nodes.shape[1]), I32),
            arrays((2, nodes // LANES, LANES), I32),
        ],
        [
            pltpu.VMEM((SUBS, elements), F32),
            pltpu.VMEM((SUBS, elements), F32),
            pltpu.VMEM((2, SUBS, width), F32),
        ],
        (connectivity, node_motion, edge, couple.T, readout.T, shared_nodes),
    )
    usual = rows // dom_total
    relaxing = decay.reshape(1, width)
    if usual == LANES:
        sorter, positions, table = call(
            sort_rows, [VMEM, VMEM],
            [
                arrays((rows, rows), BF),
                arrays((dom_total, POS_ROWS, LANES), BF),
                arrays((2 * dom_total,), I32),
            ],
            [
                pltpu.VMEM((row_groups, LANES), F32),
                pltpu.VMEM((row_groups, LANES), F32),
                pltpu.SMEM((dom_total + 1,), I32),
            ],
            (owner_route.reshape(row_groups, LANES), owner_slot.reshape(1, rows)),
            out_specs=[VMEM, VMEM, SMEM],
        )
        masked, mass_inv, block_of = call(
            functools.partial(mask_weights, capacity), [SMEM, SMEM, VMEM],
            [
                arrays(flat_weights.shape, BF),
                arrays((targets, block_size), F32),
                arrays((targets * entries,), I32),
            ],
            [],
            (entry_slot.T, entry_count, flat_weights),
            out_specs=[VMEM, VMEM, SMEM],
        )
        payload = arrays((2 * usual + POS_ROWS, width), BF)
        outgoing = call(
            project_rows, [SMEM, SMEM] + [VMEM] * (4 + box_total),
            [payload] * dom_total,
            [
                pltpu.VMEM((box_total * capacity, width, block_size), BF),
                pltpu.VMEM((width, rows), BF),
                pltpu.VMEM((row_groups, LANES, width), BF),
            ],
            (table, block_of, masked, mass_inv, sorter, positions, *received),
        )
        far = dom_total // 2
        payloads = {0: outgoing[0]}
        for k in range(1, dom_total):
            payloads[k] = lax.ppermute(outgoing[k], "dom", [(i, i ^ k) for i in range(dom_total)])
        soon = [0, *range(dom_total - 1, far - 1, -1)]
        late = [payloads[k] for k in range(far - 1, 0, -1)]

        def placing(count):
            return [
                pltpu.VMEM((elements, count * 2 * usual), BF),
                pltpu.VMEM((count * 2 * usual, width), BF),
            ]

        early = call(
            functools.partial(place_early, len(soon)), [VMEM] * len(soon),
            arrays((elements, width), F32), placing(len(soon)), [payloads[k] for k in soon],
        )
        placed, scratch = False, placing(len(late))
    else:
        early = spread_rows(received, entry_slot, entry_count, weights, owner_route, owner_slot)
        late = []
        placed, scratch = True, []
    export = arrays((3, shared_nodes.shape[1]), F32)
    arrived, local, *exports = call(
        functools.partial(finish, placed, len(late)),
        [VMEM] * (len(late) + 8),
        [arrays((elements, width), BF), arrays((3, nodes // LANES, LANES), F32)] + [export] * 4,
        scratch,
        (*late, early, base, edge, connectivity, onehot, relaxing, readout.T, chosen),
    )
    history = call(relax, [VMEM] * 3, arrays((elements, width), BF), [], (arrived, drive, relaxing))
    halo = [None] * 4
    for m, axis, first in ((3, "box", 1), (1, "dom", 1), (0, "dom", 0), (2, "box", 0)):
        halo[m] = lax.ppermute(exports[m], axis, swaps(axis, first))
    force = call(
        add_shared, [VMEM] * (2 + len(halo)), arrays((3, nodes), F32), [],
        (local, inverse, *halo),
    )
    return history, force


def solution(mesh):
    return jax.shard_map(
        body,
        mesh=mesh,
        in_specs=(
            P(("dom", "box"), None, None),
            P(("dom", "box")),
            P(("dom", "box"), None),
            P(("dom", "box")),
            P(("dom", "box"), None, None, None),
            P(("dom", "box")),
            P(("dom", "box")),
            P(None, ("dom", "box")),
            P(None, ("dom", "box")),
            P(None, ("dom", "box")),
            P(("dom", "box")),
            P(),
            P(),
            P(),
        ),
        out_specs=(P(("dom", "box"), None), P(None, ("dom", "box"))),
        check_vma=False,
    )
```

```python
import functools

import jax
import jax.numpy as jnp
from jax import lax
from jax.experimental import pallas as pl
from jax.experimental.pallas import tpu as pltpu
from jax.sharding import PartitionSpec as P


BF = jnp.bfloat16
F32 = jnp.float32
I32 = jnp.int32
LANES = 128
SUBS = 8
POS_ROWS = 16
NOWHERE = 16.0
TENSOR = ((0, 3, 5), (3, 1, 4), (5, 4, 2))
NT_DIMS = (((1,), (1,)), ((), ()))
TN_DIMS = (((0,), (0,)), ((), ()))
HIGHEST = lax.Precision.HIGHEST


def iota(shape, dim):
    return lax.broadcasted_iota(I32, shape, dim)


def pieces(x, count):
    out = []
    for _ in range(count - 1):
        high = x.astype(BF)
        out.append(high)
        x = x - high.astype(F32)
    out.append(x.astype(BF))
    return out


def as_onehot(mask):
    return jnp.where(mask, 1.0, 0.0).astype(BF)


def lookup(rows, index):
    low = index & (LANES - 1)
    high = index >> 7
    out = jnp.zeros(index.shape, F32)
    for r, row in enumerate(rows):
        got = jnp.take_along_axis(
            jnp.broadcast_to(row, index.shape), low, axis=1, mode="promise_in_bounds"
        )
        out = jnp.where(high == r, got, out)
    return out


def pack_blocks(route, old, *rest):
    outs, table = rest[:-1], rest[-1]
    me = lax.axis_index("box")
    capacity = outs[0].shape[0]
    for m in range(len(outs) * capacity):
        table[m] = 0
    routes = [route[i] for i in range(old.shape[0])]
    for i, target in enumerate(routes):
        order = jnp.int32(0)
        for earlier in routes[:i]:
            order = order + (earlier == target).astype(I32)
        table[(target ^ me) * capacity + order] = i
    for k, out in enumerate(outs):
        for s in range(capacity):
            out[s] = old[table[k * capacity + s]]


def mark_places(target, column, high, low):
    low_iota = iota((LANES, LANES), 0).astype(F32).astype(BF)
    low = jnp.broadcast_to(low, (LANES, LANES)).astype(BF)
    match = jnp.where(low_iota == low, jnp.ones_like(low), jnp.zeros_like(low))
    lanes = slice(column * LANES, (column + 1) * LANES)
    for g in range(target.shape[0] // LANES):
        here = jnp.broadcast_to(jnp.where(high == g, 1.0, 0.0), (LANES, LANES)).astype(BF)
        target[g * LANES : (g + 1) * LANES, lanes] = match * here


def sort_rows(owner_route, owner_slot, sorter, positions, table, high_rows, low_rows, starts):
    dom_total = positions.shape[0]
    row_groups = owner_route.shape[0]
    rows = row_groups * LANES
    me = lax.axis_index("dom")
    route = owner_route[...]
    picks = jnp.concatenate([as_onehot(route == d) for d in range(dom_total)], axis=0)
    span = dom_total * row_groups
    ahead = as_onehot(iota((LANES, LANES), 0) < iota((LANES, LANES), 1))
    within = jnp.dot(picks, ahead, preferred_element_type=F32)
    totals = jnp.dot(picks, jnp.ones((LANES, LANES), BF), preferred_element_type=F32).astype(BF)
    before = as_onehot(iota((span, span), 1) < iota((span, span), 0))
    base = jnp.dot(before, totals, preferred_element_type=F32)
    ranked = within + base
    place = jnp.zeros((row_groups, LANES), F32)
    for d in range(dom_total):
        place = jnp.where(route == d, ranked[d * row_groups : (d + 1) * row_groups], place)
        starts[d] = jnp.max(base[d * row_groups : d * row_groups + 1]).astype(I32)
    starts[dom_total] = rows
    place = place.astype(I32)
    high = (place >> 7).astype(F32)
    low = (place & (LANES - 1)).astype(F32)
    for g in range(row_groups):
        mark_places(sorter, g, high[g : g + 1], low[g : g + 1])
    spot = owner_slot[...]
    which = iota((POS_ROWS, rows), 0)
    parts = jnp.where(which == 0, spot >> 7, jnp.where(which == 1, spot & (LANES - 1), 0))
    ordered = lax.dot_general(
        parts.astype(F32).astype(BF), sorter[...], NT_DIMS, preferred_element_type=F32
    )
    for g in range(row_groups):
        high_rows[g : g + 1] = ordered[0:1, g * LANES : (g + 1) * LANES]
        low_rows[g : g + 1] = ordered[1:2, g * LANES : (g + 1) * LANES]
    which = iota((POS_ROWS, LANES), 0)
    for k in range(dom_total):
        owner = me ^ k
        start = starts[owner]
        held = starts[owner + 1] - start
        block = jnp.zeros((POS_ROWS, LANES), F32)
        for j in range(2):
            chunk = jnp.minimum(start // LANES + j, row_groups - 1)
            table[2 * k + j] = chunk
            high = jnp.where(held > j * LANES, high_rows[pl.ds(chunk, 1)], NOWHERE)
            block = jnp.where(which == j, high, block)
            block = jnp.where(which == 2 + j, low_rows[pl.ds(chunk, 1)], block)
        positions[k] = block.astype(BF)


def mask_weights(capacity, slot, count, weights, masked, mass_inv, blocks):
    targets = weights.shape[0]
    entries = weights.shape[1] // LANES
    box = lax.axis_index("box")
    for t in range(targets):
        total = jnp.zeros((1, LANES), F32)
        for l in range(entries):
            live = l < count[t]
            span = slice(l * LANES, (l + 1) * LANES)
            part = weights[t, span, :]
            part = jnp.where(live, part, jnp.zeros_like(part))
            masked[t, span, :] = part
            total = total + jnp.sum(part.astype(F32), axis=0, keepdims=True)
            entry = jnp.where(live, slot[l, t], slot[0, t])
            source = lax.div(entry, capacity) ^ box
            blocks[t * entries + l] = source * capacity + lax.rem(entry, capacity)
        mass_inv[t : t + 1] = 1.0 / total


def element_parts(connectivity, motion, size, couple, readout, shared, drive, base, onehot,
                  chosen, inverse, strain, elastic, wide):
    elements = connectivity.shape[1]
    corners = connectivity.shape[0]
    groups = motion.shape[1] // LANES
    corner = iota((corners, LANES), 0)
    signs = [(2 * ((corner >> c) & 1) - 1).astype(F32) for c in range(3)]
    low_iota = iota((LANES, LANES), 0)
    lane_iota = iota((LANES, LANES), 1).astype(F32)
    strain[...] = jnp.zeros_like(strain)
    elastic[...] = jnp.zeros_like(elastic)
    for j in range(elements // LANES):
        lanes = slice(j * LANES, (j + 1) * LANES)
        nodes = connectivity[:, lanes]
        scale = 1.0 / (4.0 * size[:, lanes])
        grad = []
        for i in range(3):
            moved = lookup(
                [motion[i : i + 1, r * LANES : (r + 1) * LANES] for r in range(groups)], nodes
            )
            grad.append(
                [jnp.sum(moved * signs[c], axis=0, keepdims=True) * scale for c in range(3)]
            )
        rows = [
            grad[0][0],
            grad[1][1],
            grad[2][2],
            grad[0][1] + grad[1][0],
            grad[1][2] + grad[2][1],
            grad[2][0] + grad[0][2],
        ]
        volume = 1.2 * (rows[0] + rows[1] + rows[2])
        for c in range(6):
            strain[c : c + 1, lanes] = rows[c]
            elastic[c : c + 1, lanes] = volume + 1.6 * rows[c] if c < 3 else 0.8 * rows[c]
        turned = (nodes & (LANES - 1)).astype(F32).T
        for a in range(corners):
            onehot[a, lanes, :] = as_onehot(lane_iota == turned[:, a : a + 1])
    wide[...] = jnp.zeros_like(wide)
    wide[0, 0:6] = couple[...]
    wide[1, 0:6] = readout[...]
    drive[...] = lax.dot_general(
        strain[...], wide[0], TN_DIMS, preferred_element_type=F32, precision=HIGHEST
    )
    base[...] = elastic[...] + lax.dot_general(
        wide[1], drive[...], NT_DIMS, preferred_element_type=F32, precision=HIGHEST
    )
    odd_dom = lax.axis_index("dom") & 1
    odd_box = lax.axis_index("box") & 1
    chosen[...] = jnp.zeros_like(chosen)
    chosen[0:1] = shared[pl.ds(1 - odd_dom, 1)]
    chosen[1:2] = shared[pl.ds(odd_dom, 1)]
    chosen[2:3] = shared[pl.ds(3 - odd_box, 1)]
    chosen[3:4] = shared[pl.ds(2 + odd_box, 1)]
    group = iota((groups, LANES), 0)
    lane = iota((groups, LANES), 1)
    total = jnp.zeros((2 * groups, LANES), F32)
    for m in range(4):
        axis = "dom" if m < 2 else "box"
        here = lax.axis_index(axis)
        partner = here + (1 - 2 * (here & 1)) * (1 if m % 2 == 0 else -1)
        paired = (partner >= 0) & (partner < lax.axis_size(axis))
        nodes = jnp.where(paired, chosen[m : m + 1], groups * LANES)
        here = group == (nodes >> 7)
        marks = jnp.concatenate(
            [jnp.where(here, m + 1, 0), jnp.where(here, lane, 0)], axis=0
        ).astype(F32)
        total = total + lax.dot_general(
            marks.astype(BF),
            as_onehot(low_iota == (nodes & (LANES - 1))),
            NT_DIMS,
            preferred_element_type=F32,
        )
    total = total.astype(I32)
    inverse[0] = total[:groups] - 1
    inverse[1] = total[groups:]


def project_rows(table, blocks, masked, mass_inv, sorter, positions, *rest):
    dom_total = positions.shape[0]
    box_total = lax.axis_size("box")
    received = rest[:box_total]
    outs = rest[box_total : box_total + dom_total]
    held, turned, ordered = rest[box_total + dom_total :]
    capacity = received[0].shape[0]
    for k, block in enumerate(received):
        for s in range(capacity):
            held[k * capacity + s] = block[s]
    targets = masked.shape[0]
    entries = masked.shape[1] // LANES
    for t in range(targets):
        picked = [held[blocks[t * entries + l]] for l in range(entries)]
        numerator = jnp.dot(
            jnp.concatenate(picked, axis=1), masked[t], preferred_element_type=F32
        )
        turned[:, t * LANES : (t + 1) * LANES] = (numerator * mass_inv[t : t + 1]).astype(BF)
    sort = lax.dot_general(sorter[...], turned[...], NT_DIMS, preferred_element_type=F32)
    for g in range(ordered.shape[0]):
        ordered[g] = sort[g * LANES : (g + 1) * LANES].astype(BF)
    for k, out in enumerate(outs):
        for j in range(2):
            out[j * LANES : (j + 1) * LANES] = ordered[table[2 * k + j]]
        out[2 * LANES :] = positions[k]


def place(payloads, placing, rows):
    for k, payload in enumerate(payloads):
        rows[k * 2 * LANES : (k + 1) * 2 * LANES] = payload[: 2 * LANES]
        where = payload[2 * LANES :].astype(F32)
        for j in range(2):
            mark_places(placing, 2 * k + j, where[j : j + 1], where[2 + j : 3 + j])
    return jnp.dot(placing[...], rows[...], preferred_element_type=F32)


def place_early(count, *refs):
    out, placing, rows = refs[count:]
    out[...] = place(refs[:count], placing, rows)


def finish(placed, count, *refs):
    payloads = refs[:count]
    early, base, size, connectivity, onehot, decay, readout, chosen = refs[count : count + 8]
    settled, local = refs[count + 8 : count + 10]
    exports = refs[count + 10 : count + 14]
    scratch = refs[count + 14 :]
    elements = base.shape[1]
    if placed:
        arrived = early[...]
    else:
        arrived = (early[...] + place(payloads, *scratch)).astype(BF)
    settled[...] = arrived
    taken = readout[...] * decay[...]
    taken = jnp.concatenate([taken, jnp.zeros((SUBS - 6, LANES), F32)], axis=0)
    share = lax.dot_general(
        jnp.concatenate(pieces(taken, 3), axis=0), arrived, NT_DIMS, preferred_element_type=F32
    )
    stress = base[...] + (share[0:SUBS] + share[SUBS : 2 * SUBS] + share[2 * SUBS : 3 * SUBS])
    row = iota((3 * SUBS, 2 * SUBS), 0)
    column = iota((3 * SUBS, 2 * SUBS), 1) & (SUBS - 1)
    spread = jnp.zeros(row.shape, I32)
    for i in range(3):
        for c in range(3):
            spread = jnp.where(
                ((row >> 3) == i) & (column == TENSOR[i][c]),
                2 * ((row >> c) & 1) - 1,
                spread,
            )
    forces = jnp.dot(
        spread.astype(F32).astype(BF),
        jnp.concatenate(pieces(stress, 2), axis=0),
        preferred_element_type=F32,
    )
    edge = size[...]
    forces = forces * (edge * edge * 0.25)
    group = iota((SUBS, elements), 0)
    halves = [jnp.zeros((6 * SUBS, LANES), F32) for _ in range(2)]
    for a in range(SUBS):
        here = group == (connectivity[a : a + 1] >> 7)
        highs, lows = [], []
        for i in range(3):
            value = jnp.where(here, forces[i * SUBS + a : i * SUBS + a + 1], 0.0)
            high, low = pieces(value, 2)
            highs.append(high)
            lows.append(low)
        halves[a % 2] = halves[a % 2] + jnp.dot(
            jnp.concatenate(highs + lows, axis=0), onehot[a], preferred_element_type=F32
        )
    total = halves[0] + halves[1]
    nodes = chosen[...]
    for i in range(3):
        summed = (
            total[i * SUBS : (i + 1) * SUBS] + total[(3 + i) * SUBS : (4 + i) * SUBS]
        )
        local[i] = summed
        got = lookup([summed[r : r + 1] for r in range(SUBS)], nodes)
        for m, out in enumerate(exports):
            out[i : i + 1] = got[m : m + 1]


def relax(arrived, drive, decay, history):
    history[...] = (arrived[...].astype(F32) * decay[...] + drive[...]).astype(BF)


def add_shared(local, inverse, *rest):
    received, force = rest[:-1], rest[-1]
    row, column = inverse[0], inverse[1]
    for i in range(local.shape[0]):
        total = local[i]
        for m, got in enumerate(received):
            share = jnp.take_along_axis(
                jnp.broadcast_to(got[i : i + 1], column.shape),
                column,
                axis=1,
                mode="promise_in_bounds",
            )
            total = total + jnp.where(row == m, share, 0.0)
        for r in range(local.shape[1]):
            force[i : i + 1, r * LANES : (r + 1) * LANES] = total[r : r + 1]


VMEM = pl.BlockSpec(memory_space=pltpu.VMEM)
SMEM = pl.BlockSpec(memory_space=pltpu.SMEM)


def call(kernel, ins, outs, scratch, args, cost=2_000_000_000, out_specs=None):
    single = not isinstance(outs, (list, tuple))
    return pl.pallas_call(
        kernel,
        out_shape=outs,
        in_specs=ins,
        out_specs=out_specs or (VMEM if single else [VMEM] * len(outs)),
        scratch_shapes=scratch,
        cost_estimate=pl.CostEstimate(flops=cost, bytes_accessed=100_000, transcendentals=0),
        compiler_params=pltpu.CompilerParams(vmem_limit_bytes=24 * 1024 * 1024),
    )(*args)


def swaps(axis, first):
    total = lax.axis_size(axis)
    pairs = [(i, i + 1) for i in range(first, total - 1, 2)]
    left = sorted(set(range(total)) - {i for pair in pairs for i in pair})
    pairs += [(left[0], left[-1])] if left else []
    return [(a, b) for a, b in pairs] + [(b, a) for a, b in pairs if a != b]


def arrays(shape, dtype):
    return jax.ShapeDtypeStruct(shape, dtype)


def exclusive_order(targets, choice_total):
    one_hot = (targets[:, None] == jnp.arange(choice_total, dtype=I32)[None, :]).astype(I32)
    return jnp.sum((jnp.cumsum(one_hot, axis=0) - one_hot) * one_hot, axis=1)


def spread_rows(received, entry_slot, entry_count, weights, owner_route, owner_slot):
    targets, entries = entry_slot.shape
    block_size = weights.shape[-1]
    capacity, width, _ = received[0].shape
    me = lax.axis_index("box")
    stacked = jnp.concatenate(received, axis=0)
    held = ((entry_slot // capacity) ^ me) * capacity + entry_slot % capacity
    live = (jnp.arange(entries, dtype=I32)[None, :] < entry_count[:, None]).astype(BF)
    mass = jnp.einsum("tl,tlij->tj", live, weights, preferred_element_type=F32)
    picked = stacked[held] * live[:, :, None, None]
    numerator = jnp.einsum("tlhi,tlij->tjh", picked, weights, preferred_element_type=F32)
    projected = (numerator / mass[:, :, None]).astype(BF).reshape(targets * block_size, width)
    total = projected.shape[0]
    dom_total = lax.axis_size("dom")
    owner_capacity = 2 * (total // dom_total)
    place = owner_route * owner_capacity + exclusive_order(owner_route, dom_total)
    rows = jnp.zeros((dom_total * owner_capacity, width), BF).at[place].set(projected)
    spots = jnp.full((dom_total * owner_capacity,), total, I32).at[place].set(owner_slot)
    rows = lax.all_to_all(
        rows.reshape(dom_total, owner_capacity, width), "dom", 0, 0, tiled=True
    )
    spots = lax.all_to_all(spots.reshape(dom_total, owner_capacity), "dom", 0, 0, tiled=True)
    return (
        jnp.zeros((total, width), BF)
        .at[spots.reshape(-1)]
        .set(rows.reshape(-1, width), mode="drop")
    )


def body(old_history, box_route, entry_slot, entry_count, weights, owner_route, owner_slot,
         connectivity, shared_nodes, node_motion, elem_size, decay, couple, readout):
    blocks, width, block_size = old_history.shape
    targets, entries = entry_slot.shape
    box_total = lax.axis_size("box")
    dom_total = lax.axis_size("dom")
    capacity = blocks // 2
    rows = targets * block_size
    row_groups = rows // LANES
    elements = connectivity.shape[1]
    nodes = node_motion.shape[1]

    packed = call(
        pack_blocks, [SMEM, VMEM],
        [arrays((capacity, width, block_size), BF)] * box_total,
        [pltpu.SMEM((box_total * capacity,), I32)],
        (box_route, old_history),
    )
    received = {0: packed[0]}
    for k in [k for k in range(2, box_total)] + [1]:
        received[k] = lax.ppermute(packed[k], "box", [(i, i ^ k) for i in range(box_total)])
    received = [received[k] for k in range(box_total)]
    flat_weights = weights.reshape(targets, entries * block_size, block_size)
    edge = elem_size.reshape(1, elements)
    drive, base, onehot, chosen, inverse = call(
        element_parts, [VMEM] * 6,
        [
            arrays((elements, width), F32),
            arrays((SUBS, elements), F32),
            arrays((connectivity.shape[0], elements, LANES), BF),
            arrays((SUBS, shared_nodes.shape[1]), I32),
            arrays((2, nodes // LANES, LANES), I32),
        ],
        [
            pltpu.VMEM((SUBS, elements), F32),
            pltpu.VMEM((SUBS, elements), F32),
            pltpu.VMEM((2, SUBS, width), F32),
        ],
        (connectivity, node_motion, edge, couple.T, readout.T, shared_nodes),
        cost=1000,
    )
    usual = rows // dom_total
    relaxing = decay.reshape(1, width)
    if usual == LANES:
        sorter, positions, table = call(
            sort_rows, [VMEM, VMEM],
            [
                arrays((rows, rows), BF),
                arrays((dom_total, POS_ROWS, LANES), BF),
                arrays((2 * dom_total,), I32),
            ],
            [
                pltpu.VMEM((row_groups, LANES), F32),
                pltpu.VMEM((row_groups, LANES), F32),
                pltpu.SMEM((dom_total + 1,), I32),
            ],
            (owner_route.reshape(row_groups, LANES), owner_slot.reshape(1, rows)),
            out_specs=[VMEM, VMEM, SMEM],
        )
        masked, mass_inv, block_of = call(
            functools.partial(mask_weights, capacity), [SMEM, SMEM, VMEM],
            [
                arrays(flat_weights.shape, BF),
                arrays((targets, block_size), F32),
                arrays((targets * entries,), I32),
            ],
            [],
            (entry_slot.T, entry_count, flat_weights),
            out_specs=[VMEM, VMEM, SMEM],
        )
        payload = arrays((2 * usual + POS_ROWS, width), BF)
        outgoing = call(
            project_rows, [SMEM, SMEM] + [VMEM] * (4 + box_total),
            [payload] * dom_total,
            [
                pltpu.VMEM((box_total * capacity, width, block_size), BF),
                pltpu.VMEM((width, rows), BF),
                pltpu.VMEM((row_groups, LANES, width), BF),
            ],
            (table, block_of, masked, mass_inv, sorter, positions, *received),
        )
        far = dom_total // 2
        payloads = {0: outgoing[0]}
        for k in range(1, dom_total):
            payloads[k] = lax.ppermute(outgoing[k], "dom", [(i, i ^ k) for i in range(dom_total)])
        soon = [0, *range(dom_total - 1, far - 1, -1), 1]
        late = [payloads[k] for k in range(far - 1, 1, -1)]

        def placing(count):
            return [
                pltpu.VMEM((elements, count * 2 * usual), BF),
                pltpu.VMEM((count * 2 * usual, width), BF),
            ]

        early = call(
            functools.partial(place_early, len(soon)), [VMEM] * len(soon),
            arrays((elements, width), F32), placing(len(soon)), [payloads[k] for k in soon],
        )
        placed, scratch = False, placing(len(late))
    else:
        early = spread_rows(received, entry_slot, entry_count, weights, owner_route, owner_slot)
        late = []
        placed, scratch = True, []
    export = arrays((3, shared_nodes.shape[1]), F32)
    arrived, local, *exports = call(
        functools.partial(finish, placed, len(late)),
        [VMEM] * (len(late) + 8),
        [arrays((elements, width), BF), arrays((3, nodes // LANES, LANES), F32)] + [export] * 4,
        scratch,
        (*late, early, base, edge, connectivity, onehot, relaxing, readout.T, chosen),
    )
    history = call(relax, [VMEM] * 3, arrays((elements, width), BF), [], (arrived, drive, relaxing))
    halo = [None] * 4
    for m, axis, first in ((3, "box", 1), (1, "dom", 1), (0, "dom", 0), (2, "box", 0)):
        halo[m] = lax.ppermute(exports[m], axis, swaps(axis, first))
    force = call(
        add_shared, [VMEM] * (2 + len(halo)), arrays((3, nodes), F32), [],
        (local, inverse, *halo),
    )
    return history, force


def solution(mesh):
    return jax.shard_map(
        body,
        mesh=mesh,
        in_specs=(
            P(("dom", "box"), None, None),
            P(("dom", "box")),
            P(("dom", "box"), None),
            P(("dom", "box")),
            P(("dom", "box"), None, None, None),
            P(("dom", "box")),
            P(("dom", "box")),
            P(None, ("dom", "box")),
            P(None, ("dom", "box")),
            P(None, ("dom", "box")),
            P(("dom", "box")),
            P(),
            P(),
            P(),
        ),
        out_specs=(P(("dom", "box"), None), P(None, ("dom", "box"))),
        check_vma=False,
    )
```

```python
import functools

import jax
import jax.numpy as jnp
from jax import lax
from jax.experimental import pallas as pl
from jax.experimental.pallas import tpu as pltpu
from jax.sharding import PartitionSpec as P


BF = jnp.bfloat16
F32 = jnp.float32
I32 = jnp.int32
LANES = 128
SUBS = 8
META = 8
PARTS = 16
NOWHERE = 16.0
TENSOR = ((0, 3, 5), (3, 1, 4), (5, 4, 2))
NT_DIMS = (((1,), (1,)), ((), ()))
TN_DIMS = (((0,), (0,)), ((), ()))
HIGHEST = lax.Precision.HIGHEST


def iota(shape, dim):
    return lax.broadcasted_iota(I32, shape, dim)


def pieces(x, count):
    out = []
    for _ in range(count - 1):
        high = x.astype(BF)
        out.append(high)
        x = x - high.astype(F32)
    out.append(x.astype(BF))
    return out


def as_onehot(mask):
    return jnp.where(mask, 1.0, 0.0).astype(BF)


def lookup(rows, index):
    low = index & (LANES - 1)
    high = index >> 7
    out = jnp.zeros(index.shape, F32)
    for r, row in enumerate(rows):
        got = jnp.take_along_axis(
            jnp.broadcast_to(row, index.shape), low, axis=1, mode="promise_in_bounds"
        )
        out = jnp.where(high == r, got, out)
    return out


def pack_blocks(route, old, *rest):
    outs, table = rest[:-1], rest[-1]
    me = lax.axis_index("box")
    capacity = outs[0].shape[0]
    for m in range(len(outs) * capacity):
        table[m] = 0
    routes = [route[i] for i in range(old.shape[0])]
    for i, target in enumerate(routes):
        order = jnp.int32(0)
        for earlier in routes[:i]:
            order = order + (earlier == target).astype(I32)
        table[(target ^ me) * capacity + order] = i
    for k, out in enumerate(outs):
        for s in range(capacity):
            out[s] = old[table[k * capacity + s]]


def mark_places(target, column, high, low):
    low_iota = iota((LANES, LANES), 0).astype(F32).astype(BF)
    low = jnp.broadcast_to(low, (LANES, LANES)).astype(BF)
    match = jnp.where(low_iota == low, jnp.ones_like(low), jnp.zeros_like(low))
    lanes = slice(column * LANES, (column + 1) * LANES)
    for g in range(target.shape[0] // LANES):
        here = jnp.broadcast_to(jnp.where(high == g, 1.0, 0.0), (LANES, LANES)).astype(BF)
        target[g * LANES : (g + 1) * LANES, lanes] = match * here


def sort_rows(owner_route, owner_slot, sorter, positions, table, high_rows, low_rows, starts):
    dom_total = positions.shape[0]
    row_groups = owner_route.shape[0]
    rows = row_groups * LANES
    me = lax.axis_index("dom")
    route = owner_route[...]
    picks = jnp.concatenate([as_onehot(route == d) for d in range(dom_total)], axis=0)
    span = dom_total * row_groups
    ahead = as_onehot(iota((LANES, LANES), 0) < iota((LANES, LANES), 1))
    within = jnp.dot(picks, ahead, preferred_element_type=F32)
    totals = jnp.dot(picks, jnp.ones((LANES, LANES), BF), preferred_element_type=F32).astype(BF)
    before = as_onehot(iota((span, span), 1) < iota((span, span), 0))
    base = jnp.dot(before, totals, preferred_element_type=F32)
    ranked = within + base
    place = jnp.zeros((row_groups, LANES), F32)
    for d in range(dom_total):
        place = jnp.where(route == d, ranked[d * row_groups : (d + 1) * row_groups], place)
        starts[d] = jnp.max(base[d * row_groups : d * row_groups + 1]).astype(I32)
    starts[dom_total] = rows
    place = place.astype(I32)
    high = (place >> 7).astype(F32)
    low = (place & (LANES - 1)).astype(F32)
    for g in range(row_groups):
        mark_places(sorter, g, high[g : g + 1], low[g : g + 1])
    spot = owner_slot[...]
    which = iota((PARTS, rows), 0)
    parts = jnp.where(which == 0, spot >> 7, jnp.where(which == 1, spot & (LANES - 1), 0))
    ordered = lax.dot_general(
        parts.astype(F32).astype(BF), sorter[...], NT_DIMS, preferred_element_type=F32
    )
    for g in range(row_groups):
        high_rows[g : g + 1] = ordered[0:1, g * LANES : (g + 1) * LANES]
        low_rows[g : g + 1] = ordered[1:2, g * LANES : (g + 1) * LANES]
    which = iota((META, LANES), 0)
    far = dom_total // 2
    extra, tag = jnp.int32(0), jnp.float32(NOWHERE)
    for k in reversed(range(dom_total)):
        owner = me ^ k
        start = starts[owner]
        held = starts[owner + 1] - start
        block = jnp.full((META, LANES), NOWHERE, F32)
        for j in range(2 if k < far else 1):
            chunk = jnp.minimum(start // LANES + j, row_groups - 1)
            table[2 * k + j] = chunk
            high = jnp.where(held > j * LANES, high_rows[pl.ds(chunk, 1)], NOWHERE)
            block = jnp.where(which == 2 * j, high, block)
            block = jnp.where(which == 2 * j + 1, low_rows[pl.ds(chunk, 1)], block)
        if k >= far:
            more = held > LANES
            extra = jnp.where(more, jnp.minimum(start // LANES + 1, row_groups - 1), extra)
            tag = jnp.where(more, jnp.float32(k ^ far), tag)
        if k == far:
            table[2 * k + 1] = extra
            block = jnp.where(which == 2, high_rows[pl.ds(extra, 1)], block)
            block = jnp.where(which == 3, low_rows[pl.ds(extra, 1)], block)
            block = jnp.where(which == 4, tag, block)
        positions[k] = block.astype(BF)


def mask_weights(capacity, slot, count, weights, masked, mass_inv, blocks):
    targets = weights.shape[0]
    entries = weights.shape[1] // LANES
    box = lax.axis_index("box")
    for t in range(targets):
        total = jnp.zeros((1, LANES), F32)
        for l in range(entries):
            live = l < count[t]
            span = slice(l * LANES, (l + 1) * LANES)
            part = weights[t, span, :]
            part = jnp.where(live, part, jnp.zeros_like(part))
            masked[t, span, :] = part
            total = total + jnp.sum(part.astype(F32), axis=0, keepdims=True)
            entry = jnp.where(live, slot[l, t], slot[0, t])
            source = lax.div(entry, capacity) ^ box
            blocks[t * entries + l] = source * capacity + lax.rem(entry, capacity)
        mass_inv[t : t + 1] = 1.0 / total


def element_parts(connectivity, motion, size, couple, readout, shared, drive, base, onehot,
                  chosen, inverse, strain, elastic, wide):
    elements = connectivity.shape[1]
    corners = connectivity.shape[0]
    groups = motion.shape[1] // LANES
    corner = iota((corners, LANES), 0)
    signs = [(2 * ((corner >> c) & 1) - 1).astype(F32) for c in range(3)]
    low_iota = iota((LANES, LANES), 0)
    lane_iota = iota((LANES, LANES), 1).astype(F32)
    strain[...] = jnp.zeros_like(strain)
    elastic[...] = jnp.zeros_like(elastic)
    for j in range(elements // LANES):
        lanes = slice(j * LANES, (j + 1) * LANES)
        nodes = connectivity[:, lanes]
        scale = 1.0 / (4.0 * size[:, lanes])
        grad = []
        for i in range(3):
            moved = lookup(
                [motion[i : i + 1, r * LANES : (r + 1) * LANES] for r in range(groups)], nodes
            )
            grad.append(
                [jnp.sum(moved * signs[c], axis=0, keepdims=True) * scale for c in range(3)]
            )
        rows = [
            grad[0][0],
            grad[1][1],
            grad[2][2],
            grad[0][1] + grad[1][0],
            grad[1][2] + grad[2][1],
            grad[2][0] + grad[0][2],
        ]
        volume = 1.2 * (rows[0] + rows[1] + rows[2])
        for c in range(6):
            strain[c : c + 1, lanes] = rows[c]
            elastic[c : c + 1, lanes] = volume + 1.6 * rows[c] if c < 3 else 0.8 * rows[c]
        turned = (nodes & (LANES - 1)).astype(F32).T
        for a in range(corners):
            onehot[a, lanes, :] = as_onehot(lane_iota == turned[:, a : a + 1])
    wide[...] = jnp.zeros_like(wide)
    wide[0, 0:6] = couple[...]
    wide[1, 0:6] = readout[...]
    drive[...] = lax.dot_general(
        strain[...], wide[0], TN_DIMS, preferred_element_type=F32, precision=HIGHEST
    )
    base[...] = elastic[...] + lax.dot_general(
        wide[1], drive[...], NT_DIMS, preferred_element_type=F32, precision=HIGHEST
    )
    odd_dom = lax.axis_index("dom") & 1
    odd_box = lax.axis_index("box") & 1
    chosen[...] = jnp.zeros_like(chosen)
    chosen[0:1] = shared[pl.ds(1 - odd_dom, 1)]
    chosen[1:2] = shared[pl.ds(odd_dom, 1)]
    chosen[2:3] = shared[pl.ds(3 - odd_box, 1)]
    chosen[3:4] = shared[pl.ds(2 + odd_box, 1)]
    group = iota((groups, LANES), 0)
    lane = iota((groups, LANES), 1)
    total = jnp.zeros((2 * groups, LANES), F32)
    for m in range(4):
        axis = "dom" if m < 2 else "box"
        here = lax.axis_index(axis)
        partner = here + (1 - 2 * (here & 1)) * (1 if m % 2 == 0 else -1)
        paired = (partner >= 0) & (partner < lax.axis_size(axis))
        nodes = jnp.where(paired, chosen[m : m + 1], groups * LANES)
        here = group == (nodes >> 7)
        marks = jnp.concatenate(
            [jnp.where(here, m + 1, 0), jnp.where(here, lane, 0)], axis=0
        ).astype(F32)
        total = total + lax.dot_general(
            marks.astype(BF),
            as_onehot(low_iota == (nodes & (LANES - 1))),
            NT_DIMS,
            preferred_element_type=F32,
        )
    total = total.astype(I32)
    inverse[0] = total[:groups] - 1
    inverse[1] = total[groups:]


def project_rows(table, blocks, masked, mass_inv, sorter, positions, *rest):
    dom_total = positions.shape[0]
    box_total = lax.axis_size("box")
    received = rest[:box_total]
    outs = rest[box_total : box_total + dom_total]
    held, turned, ordered = rest[box_total + dom_total :]
    capacity = received[0].shape[0]
    for k, block in enumerate(received):
        for s in range(capacity):
            held[k * capacity + s] = block[s]
    targets = masked.shape[0]
    entries = masked.shape[1] // LANES
    for t in range(targets):
        picked = [held[blocks[t * entries + l]] for l in range(entries)]
        numerator = jnp.dot(
            jnp.concatenate(picked, axis=1), masked[t], preferred_element_type=F32
        )
        turned[:, t * LANES : (t + 1) * LANES] = (numerator * mass_inv[t : t + 1]).astype(BF)
    sort = lax.dot_general(sorter[...], turned[...], NT_DIMS, preferred_element_type=F32)
    for g in range(ordered.shape[0]):
        ordered[g] = sort[g * LANES : (g + 1) * LANES].astype(BF)
    for k, out in enumerate(outs):
        for j in range(2 if k <= dom_total // 2 else 1):
            out[j * LANES : (j + 1) * LANES] = ordered[table[2 * k + j]]
        out[out.shape[0] - META :] = positions[k]


def pass_on(relayed, *refs):
    count = len(refs) // 2
    meta = relayed[2 * LANES :].astype(F32)
    which = iota((META, LANES), 0)
    for k, (held, out) in enumerate(zip(refs[:count], refs[count:]), 1):
        out[2 * LANES : 3 * LANES] = relayed[LANES : 2 * LANES]
        block = held[3 * LANES :].astype(F32)
        block = jnp.where(which == 4, jnp.where(meta[4:5] == k, meta[2:3], NOWHERE), block)
        block = jnp.where(which == 5, meta[3:4], block)
        out[3 * LANES :] = block.astype(BF)


def place(payloads, chunks, placing, rows):
    column = 0
    for payload, parts in zip(payloads, chunks):
        meta = payload[payload.shape[0] - META :].astype(F32)
        for j, tagged in parts:
            high, low = meta[2 * j : 2 * j + 1], meta[2 * j + 1 : 2 * j + 2]
            if tagged:
                high = jnp.where(meta[4:5] == 0, high, NOWHERE)
            rows[column * LANES : (column + 1) * LANES] = payload[j * LANES : (j + 1) * LANES]
            mark_places(placing, column, high, low)
            column += 1
    return jnp.dot(placing[...], rows[...], preferred_element_type=F32)


def place_early(chunks, *refs):
    count = len(chunks)
    out, placing, rows = refs[count:]
    out[...] = place(refs[:count], chunks, placing, rows)


def finish(placed, chunks, *refs):
    count = len(chunks)
    payloads = refs[:count]
    early, base, size, connectivity, onehot, decay, readout, chosen = refs[count : count + 8]
    settled, local = refs[count + 8 : count + 10]
    exports = refs[count + 10 : count + 14]
    scratch = refs[count + 14 :]
    elements = base.shape[1]
    if placed:
        arrived = early[...]
    else:
        arrived = (early[...] + place(payloads, chunks, *scratch)).astype(BF)
    settled[...] = arrived
    taken = readout[...] * decay[...]
    taken = jnp.concatenate([taken, jnp.zeros((SUBS - 6, LANES), F32)], axis=0)
    share = lax.dot_general(
        jnp.concatenate(pieces(taken, 3), axis=0), arrived, NT_DIMS, preferred_element_type=F32
    )
    stress = base[...] + (share[0:SUBS] + share[SUBS : 2 * SUBS] + share[2 * SUBS : 3 * SUBS])
    row = iota((3 * SUBS, 2 * SUBS), 0)
    column = iota((3 * SUBS, 2 * SUBS), 1) & (SUBS - 1)
    spread = jnp.zeros(row.shape, I32)
    for i in range(3):
        for c in range(3):
            spread = jnp.where(
                ((row >> 3) == i) & (column == TENSOR[i][c]),
                2 * ((row >> c) & 1) - 1,
                spread,
            )
    forces = jnp.dot(
        spread.astype(F32).astype(BF),
        jnp.concatenate(pieces(stress, 2), axis=0),
        preferred_element_type=F32,
    )
    edge = size[...]
    forces = forces * (edge * edge * 0.25)
    group = iota((SUBS, elements), 0)
    halves = [jnp.zeros((6 * SUBS, LANES), F32) for _ in range(2)]
    for a in range(SUBS):
        here = group == (connectivity[a : a + 1] >> 7)
        highs, lows = [], []
        for i in range(3):
            value = jnp.where(here, forces[i * SUBS + a : i * SUBS + a + 1], 0.0)
            high, low = pieces(value, 2)
            highs.append(high)
            lows.append(low)
        halves[a % 2] = halves[a % 2] + jnp.dot(
            jnp.concatenate(highs + lows, axis=0), onehot[a], preferred_element_type=F32
        )
    total = halves[0] + halves[1]
    nodes = chosen[...]
    for i in range(3):
        summed = (
            total[i * SUBS : (i + 1) * SUBS] + total[(3 + i) * SUBS : (4 + i) * SUBS]
        )
        local[i] = summed
        got = lookup([summed[r : r + 1] for r in range(SUBS)], nodes)
        for m, out in enumerate(exports):
            out[i : i + 1] = got[m : m + 1]


def relax(arrived, drive, decay, history):
    history[...] = (arrived[...].astype(F32) * decay[...] + drive[...]).astype(BF)


def add_shared(local, inverse, *rest):
    received, force = rest[:-1], rest[-1]
    row, column = inverse[0], inverse[1]
    for i in range(local.shape[0]):
        total = local[i]
        for m, got in enumerate(received):
            share = jnp.take_along_axis(
                jnp.broadcast_to(got[i : i + 1], column.shape),
                column,
                axis=1,
                mode="promise_in_bounds",
            )
            total = total + jnp.where(row == m, share, 0.0)
        for r in range(local.shape[1]):
            force[i : i + 1, r * LANES : (r + 1) * LANES] = total[r : r + 1]


VMEM = pl.BlockSpec(memory_space=pltpu.VMEM)
SMEM = pl.BlockSpec(memory_space=pltpu.SMEM)


def call(kernel, ins, outs, scratch, args, cost=2_000_000_000, out_specs=None, aliases=None):
    single = not isinstance(outs, (list, tuple))
    return pl.pallas_call(
        kernel,
        out_shape=outs,
        in_specs=ins,
        out_specs=out_specs or (VMEM if single else [VMEM] * len(outs)),
        scratch_shapes=scratch,
        input_output_aliases=aliases or {},
        cost_estimate=pl.CostEstimate(flops=cost, bytes_accessed=100_000, transcendentals=0),
        compiler_params=pltpu.CompilerParams(vmem_limit_bytes=24 * 1024 * 1024),
    )(*args)


def swaps(axis, first):
    total = lax.axis_size(axis)
    pairs = [(i, i + 1) for i in range(first, total - 1, 2)]
    left = sorted(set(range(total)) - {i for pair in pairs for i in pair})
    pairs += [(left[0], left[-1])] if left else []
    return [(a, b) for a, b in pairs] + [(b, a) for a, b in pairs if a != b]


def arrays(shape, dtype):
    return jax.ShapeDtypeStruct(shape, dtype)


def exclusive_order(targets, choice_total):
    one_hot = (targets[:, None] == jnp.arange(choice_total, dtype=I32)[None, :]).astype(I32)
    return jnp.sum((jnp.cumsum(one_hot, axis=0) - one_hot) * one_hot, axis=1)


def spread_rows(received, entry_slot, entry_count, weights, owner_route, owner_slot):
    targets, entries = entry_slot.shape
    block_size = weights.shape[-1]
    capacity, width, _ = received[0].shape
    me = lax.axis_index("box")
    stacked = jnp.concatenate(received, axis=0)
    held = ((entry_slot // capacity) ^ me) * capacity + entry_slot % capacity
    live = (jnp.arange(entries, dtype=I32)[None, :] < entry_count[:, None]).astype(BF)
    mass = jnp.einsum("tl,tlij->tj", live, weights, preferred_element_type=F32)
    picked = stacked[held] * live[:, :, None, None]
    numerator = jnp.einsum("tlhi,tlij->tjh", picked, weights, preferred_element_type=F32)
    projected = (numerator / mass[:, :, None]).astype(BF).reshape(targets * block_size, width)
    total = projected.shape[0]
    dom_total = lax.axis_size("dom")
    owner_capacity = 2 * (total // dom_total)
    place = owner_route * owner_capacity + exclusive_order(owner_route, dom_total)
    rows = jnp.zeros((dom_total * owner_capacity, width), BF).at[place].set(projected)
    spots = jnp.full((dom_total * owner_capacity,), total, I32).at[place].set(owner_slot)
    rows = lax.all_to_all(
        rows.reshape(dom_total, owner_capacity, width), "dom", 0, 0, tiled=True
    )
    spots = lax.all_to_all(spots.reshape(dom_total, owner_capacity), "dom", 0, 0, tiled=True)
    return (
        jnp.zeros((total, width), BF)
        .at[spots.reshape(-1)]
        .set(rows.reshape(-1, width), mode="drop")
    )


def body(old_history, box_route, entry_slot, entry_count, weights, owner_route, owner_slot,
         connectivity, shared_nodes, node_motion, elem_size, decay, couple, readout):
    blocks, width, block_size = old_history.shape
    targets, entries = entry_slot.shape
    box_total = lax.axis_size("box")
    dom_total = lax.axis_size("dom")
    capacity = blocks // 2
    rows = targets * block_size
    row_groups = rows // LANES
    elements = connectivity.shape[1]
    nodes = node_motion.shape[1]

    packed = call(
        pack_blocks, [SMEM, VMEM],
        [arrays((capacity, width, block_size), BF)] * box_total,
        [pltpu.SMEM((box_total * capacity,), I32)],
        (box_route, old_history),
    )
    received = {0: packed[0]}
    for k in [k for k in range(2, box_total)] + [1]:
        received[k] = lax.ppermute(packed[k], "box", [(i, i ^ k) for i in range(box_total)])
    received = [received[k] for k in range(box_total)]
    flat_weights = weights.reshape(targets, entries * block_size, block_size)
    edge = elem_size.reshape(1, elements)
    drive, base, onehot, chosen, inverse = call(
        element_parts, [VMEM] * 6,
        [
            arrays((elements, width), F32),
            arrays((SUBS, elements), F32),
            arrays((connectivity.shape[0], elements, LANES), BF),
            arrays((SUBS, shared_nodes.shape[1]), I32),
            arrays((2, nodes // LANES, LANES), I32),
        ],
        [
            pltpu.VMEM((SUBS, elements), F32),
            pltpu.VMEM((SUBS, elements), F32),
            pltpu.VMEM((2, SUBS, width), F32),
        ],
        (connectivity, node_motion, edge, couple.T, readout.T, shared_nodes),
        cost=1000,
    )
    usual = rows // dom_total
    relaxing = decay.reshape(1, width)
    if usual == LANES:
        sorter, positions, table = call(
            sort_rows, [VMEM, VMEM],
            [
                arrays((rows, rows), BF),
                arrays((dom_total, META, LANES), BF),
                arrays((2 * dom_total,), I32),
            ],
            [
                pltpu.VMEM((row_groups, LANES), F32),
                pltpu.VMEM((row_groups, LANES), F32),
                pltpu.SMEM((dom_total + 1,), I32),
            ],
            (owner_route.reshape(row_groups, LANES), owner_slot.reshape(1, rows)),
            out_specs=[VMEM, VMEM, SMEM],
        )
        masked, mass_inv, block_of = call(
            functools.partial(mask_weights, capacity), [SMEM, SMEM, VMEM],
            [
                arrays(flat_weights.shape, BF),
                arrays((targets, block_size), F32),
                arrays((targets * entries,), I32),
            ],
            [],
            (entry_slot.T, entry_count, flat_weights),
            out_specs=[VMEM, VMEM, SMEM],
        )
        far = dom_total // 2
        lengths = [2] + [3] * (far - 1) + [2] + [1] * (far - 1)
        outgoing = list(
            call(
                project_rows, [SMEM, SMEM] + [VMEM] * (4 + box_total),
                [arrays((n * LANES + META, width), BF) for n in lengths],
                [
                    pltpu.VMEM((box_total * capacity, width, block_size), BF),
                    pltpu.VMEM((width, rows), BF),
                    pltpu.VMEM((row_groups, LANES, width), BF),
                ],
                (table, block_of, masked, mass_inv, sorter, positions, *received),
            )
        )
        payloads = {0: outgoing[0]}

        def swap(k):
            payloads[k] = lax.ppermute(outgoing[k], "dom", [(i, i ^ k) for i in range(dom_total)])

        for k in range(far, dom_total):
            swap(k)
        near = list(range(1, far))
        outgoing[1:far] = call(
            pass_on, [VMEM] * far, [arrays(outgoing[k].shape, BF) for k in near], [],
            (payloads[far], *outgoing[1:far]), cost=1000, aliases={k: k - 1 for k in near},
        )
        for k in near:
            swap(k)
        parts = [[(0, False), (1, False)]] + [[(0, False), (1, False), (2, False)]] * (far - 1)
        parts += [[(0, False), (1, True)]] + [[(0, False)]] * (far - 1)
        soon = [0, *range(far, dom_total), 1]
        last = list(range(far - 1, 1, -1))
        late = [payloads[k] for k in last]
        chunks = [parts[k] for k in last]

        def placing(chosen):
            total = LANES * sum(len(part) for part in chosen)
            return [pltpu.VMEM((elements, total), BF), pltpu.VMEM((total, width), BF)]

        first = [parts[k] for k in soon]
        early = call(
            functools.partial(place_early, first), [VMEM] * len(soon),
            arrays((elements, width), F32), placing(first), [payloads[k] for k in soon],
        )
        placed, scratch = False, placing(chunks)
    else:
        early = spread_rows(received, entry_slot, entry_count, weights, owner_route, owner_slot)
        late, chunks = [], []
        placed, scratch = True, []
    export = arrays((3, shared_nodes.shape[1]), F32)
    arrived, local, *exports = call(
        functools.partial(finish, placed, chunks),
        [VMEM] * (len(late) + 8),
        [arrays((elements, width), BF), arrays((3, nodes // LANES, LANES), F32)] + [export] * 4,
        scratch,
        (*late, early, base, edge, connectivity, onehot, relaxing, readout.T, chosen),
    )
    history = call(relax, [VMEM] * 3, arrays((elements, width), BF), [], (arrived, drive, relaxing))
    halo = [None] * 4
    for m, axis, first in ((3, "box", 1), (1, "dom", 1), (0, "dom", 0), (2, "box", 0)):
        halo[m] = lax.ppermute(exports[m], axis, swaps(axis, first))
    force = call(
        add_shared, [VMEM] * (2 + len(halo)), arrays((3, nodes), F32), [],
        (local, inverse, *halo),
    )
    return history, force


def solution(mesh):
    return jax.shard_map(
        body,
        mesh=mesh,
        in_specs=(
            P(("dom", "box"), None, None),
            P(("dom", "box")),
            P(("dom", "box"), None),
            P(("dom", "box")),
            P(("dom", "box"), None, None, None),
            P(("dom", "box")),
            P(("dom", "box")),
            P(None, ("dom", "box")),
            P(None, ("dom", "box")),
            P(None, ("dom", "box")),
            P(("dom", "box")),
            P(),
            P(),
            P(),
        ),
        out_specs=(P(("dom", "box"), None), P(None, ("dom", "box"))),
        check_vma=False,
    )
```

```python
import functools

import jax
import jax.numpy as jnp
from jax import lax
from jax.experimental import pallas as pl
from jax.experimental.pallas import tpu as pltpu
from jax.sharding import PartitionSpec as P


BF = jnp.bfloat16
F32 = jnp.float32
I32 = jnp.int32
LANES = 128
SUBS = 8
META = 8
PARTS = 16
NOWHERE = 16.0
TENSOR = ((0, 3, 5), (3, 1, 4), (5, 4, 2))
NT_DIMS = (((1,), (1,)), ((), ()))
TN_DIMS = (((0,), (0,)), ((), ()))
HIGHEST = lax.Precision.HIGHEST


def iota(shape, dim):
    return lax.broadcasted_iota(I32, shape, dim)


def pieces(x, count):
    out = []
    for _ in range(count - 1):
        high = x.astype(BF)
        out.append(high)
        x = x - high.astype(F32)
    out.append(x.astype(BF))
    return out


def as_onehot(mask):
    return jnp.where(mask, 1.0, 0.0).astype(BF)


def lookup(rows, index):
    low = index & (LANES - 1)
    high = index >> 7
    out = jnp.zeros(index.shape, F32)
    for r, row in enumerate(rows):
        got = jnp.take_along_axis(
            jnp.broadcast_to(row, index.shape), low, axis=1, mode="promise_in_bounds"
        )
        out = jnp.where(high == r, got, out)
    return out


def pack_blocks(route_hbm, old_hbm, *rest):
    outs = rest[:-4]
    table, route, old, sems = rest[-4:]
    find = pltpu.make_async_copy(route_hbm, route, sems.at[0])
    take = pltpu.make_async_copy(old_hbm, old, sems.at[1])
    find.start()
    take.start()
    find.wait()
    me = lax.axis_index("box")
    capacity = outs[0].shape[0]
    for m in range(len(outs) * capacity):
        table[m] = 0
    routes = [route[i] for i in range(old.shape[0])]
    for i, target in enumerate(routes):
        order = jnp.int32(0)
        for earlier in routes[:i]:
            order = order + (earlier == target).astype(I32)
        table[(target ^ me) * capacity + order] = i
    take.wait()
    for k, out in enumerate(outs):
        for s in range(capacity):
            out[s] = old[table[k * capacity + s]]


def mark_places(target, column, high, low):
    low_iota = iota((LANES, LANES), 0).astype(F32).astype(BF)
    low = jnp.broadcast_to(low, (LANES, LANES)).astype(BF)
    match = jnp.where(low_iota == low, jnp.ones_like(low), jnp.zeros_like(low))
    lanes = slice(column * LANES, (column + 1) * LANES)
    for g in range(target.shape[0] // LANES):
        here = jnp.broadcast_to(jnp.where(high == g, 1.0, 0.0), (LANES, LANES)).astype(BF)
        target[g * LANES : (g + 1) * LANES, lanes] = match * here


def sort_rows(owner_route, owner_slot, sorter, positions, table, high_rows, low_rows, starts):
    dom_total = positions.shape[0]
    row_groups = owner_route.shape[0]
    rows = row_groups * LANES
    me = lax.axis_index("dom")
    route = owner_route[...]
    picks = jnp.concatenate([as_onehot(route == d) for d in range(dom_total)], axis=0)
    span = dom_total * row_groups
    ahead = as_onehot(iota((LANES, LANES), 0) < iota((LANES, LANES), 1))
    within = jnp.dot(picks, ahead, preferred_element_type=F32)
    totals = jnp.dot(picks, jnp.ones((LANES, LANES), BF), preferred_element_type=F32).astype(BF)
    before = as_onehot(iota((span, span), 1) < iota((span, span), 0))
    base = jnp.dot(before, totals, preferred_element_type=F32)
    ranked = within + base
    place = jnp.zeros((row_groups, LANES), F32)
    for d in range(dom_total):
        place = jnp.where(route == d, ranked[d * row_groups : (d + 1) * row_groups], place)
        starts[d] = jnp.max(base[d * row_groups : d * row_groups + 1]).astype(I32)
    starts[dom_total] = rows
    place = place.astype(I32)
    high = (place >> 7).astype(F32)
    low = (place & (LANES - 1)).astype(F32)
    for g in range(row_groups):
        mark_places(sorter, g, high[g : g + 1], low[g : g + 1])
    spot = owner_slot[...]
    which = iota((PARTS, rows), 0)
    parts = jnp.where(which == 0, spot >> 7, jnp.where(which == 1, spot & (LANES - 1), 0))
    ordered = lax.dot_general(
        parts.astype(F32).astype(BF), sorter[...], NT_DIMS, preferred_element_type=F32
    )
    for g in range(row_groups):
        high_rows[g : g + 1] = ordered[0:1, g * LANES : (g + 1) * LANES]
        low_rows[g : g + 1] = ordered[1:2, g * LANES : (g + 1) * LANES]
    which = iota((META, LANES), 0)
    for k in range(dom_total):
        owner = me ^ k
        start = starts[owner]
        held = starts[owner + 1] - start
        block = jnp.zeros((META, LANES), F32)
        for j in range(2):
            chunk = jnp.minimum(start // LANES + j, row_groups - 1)
            table[2 * k + j] = chunk
            high = jnp.where(held > j * LANES, high_rows[pl.ds(chunk, 1)], NOWHERE)
            block = jnp.where(which == j, high, block)
            block = jnp.where(which == 2 + j, low_rows[pl.ds(chunk, 1)], block)
        positions[k] = block.astype(BF)


def mask_weights(capacity, slot, count, weights, masked, mass_inv, blocks):
    targets = weights.shape[0]
    entries = weights.shape[1] // LANES
    box = lax.axis_index("box")
    for t in range(targets):
        total = jnp.zeros((1, LANES), F32)
        for l in range(entries):
            live = l < count[t]
            span = slice(l * LANES, (l + 1) * LANES)
            part = weights[t, span, :]
            part = jnp.where(live, part, jnp.zeros_like(part))
            masked[t, span, :] = part
            total = total + jnp.sum(part.astype(F32), axis=0, keepdims=True)
            entry = jnp.where(live, slot[l, t], slot[0, t])
            source = lax.div(entry, capacity) ^ box
            blocks[t * entries + l] = source * capacity + lax.rem(entry, capacity)
        mass_inv[t : t + 1] = 1.0 / total


def element_parts(connectivity, motion, size, couple, readout, shared, drive, base, onehot,
                  chosen, inverse, strain, elastic, wide):
    elements = connectivity.shape[1]
    corners = connectivity.shape[0]
    groups = motion.shape[1] // LANES
    corner = iota((corners, LANES), 0)
    signs = [(2 * ((corner >> c) & 1) - 1).astype(F32) for c in range(3)]
    low_iota = iota((LANES, LANES), 0)
    lane_iota = iota((LANES, LANES), 1).astype(F32)
    strain[...] = jnp.zeros_like(strain)
    elastic[...] = jnp.zeros_like(elastic)
    for j in range(elements // LANES):
        lanes = slice(j * LANES, (j + 1) * LANES)
        nodes = connectivity[:, lanes]
        scale = 1.0 / (4.0 * size[:, lanes])
        grad = []
        for i in range(3):
            moved = lookup(
                [motion[i : i + 1, r * LANES : (r + 1) * LANES] for r in range(groups)], nodes
            )
            grad.append(
                [jnp.sum(moved * signs[c], axis=0, keepdims=True) * scale for c in range(3)]
            )
        rows = [
            grad[0][0],
            grad[1][1],
            grad[2][2],
            grad[0][1] + grad[1][0],
            grad[1][2] + grad[2][1],
            grad[2][0] + grad[0][2],
        ]
        volume = 1.2 * (rows[0] + rows[1] + rows[2])
        for c in range(6):
            strain[c : c + 1, lanes] = rows[c]
            elastic[c : c + 1, lanes] = volume + 1.6 * rows[c] if c < 3 else 0.8 * rows[c]
        turned = (nodes & (LANES - 1)).astype(F32).T
        for a in range(corners):
            onehot[a, lanes, :] = as_onehot(lane_iota == turned[:, a : a + 1])
    wide[...] = jnp.zeros_like(wide)
    wide[0, 0:6] = couple[...]
    wide[1, 0:6] = readout[...]
    drive[...] = lax.dot_general(
        strain[...], wide[0], TN_DIMS, preferred_element_type=F32, precision=HIGHEST
    )
    base[...] = elastic[...] + lax.dot_general(
        wide[1], drive[...], NT_DIMS, preferred_element_type=F32, precision=HIGHEST
    )
    odd_dom = lax.axis_index("dom") & 1
    odd_box = lax.axis_index("box") & 1
    chosen[...] = jnp.zeros_like(chosen)
    chosen[0:1] = shared[pl.ds(1 - odd_dom, 1)]
    chosen[1:2] = shared[pl.ds(odd_dom, 1)]
    chosen[2:3] = shared[pl.ds(3 - odd_box, 1)]
    chosen[3:4] = shared[pl.ds(2 + odd_box, 1)]
    group = iota((groups, LANES), 0)
    lane = iota((groups, LANES), 1)
    total = jnp.zeros((2 * groups, LANES), F32)
    for m in range(4):
        axis = "dom" if m < 2 else "box"
        here = lax.axis_index(axis)
        partner = here + (1 - 2 * (here & 1)) * (1 if m % 2 == 0 else -1)
        paired = (partner >= 0) & (partner < lax.axis_size(axis))
        nodes = jnp.where(paired, chosen[m : m + 1], groups * LANES)
        here = group == (nodes >> 7)
        marks = jnp.concatenate(
            [jnp.where(here, m + 1, 0), jnp.where(here, lane, 0)], axis=0
        ).astype(F32)
        total = total + lax.dot_general(
            marks.astype(BF),
            as_onehot(low_iota == (nodes & (LANES - 1))),
            NT_DIMS,
            preferred_element_type=F32,
        )
    total = total.astype(I32)
    inverse[0] = total[:groups] - 1
    inverse[1] = total[groups:]


def project_rows(table, blocks, masked, mass_inv, sorter, positions, *rest):
    dom_total = positions.shape[0]
    box_total = lax.axis_size("box")
    received = rest[:box_total]
    outs = rest[box_total : box_total + dom_total]
    held, turned, ordered = rest[box_total + dom_total :]
    capacity = received[0].shape[0]
    for k, block in enumerate(received):
        for s in range(capacity):
            held[k * capacity + s] = block[s]
    targets = masked.shape[0]
    entries = masked.shape[1] // LANES
    for t in range(targets):
        picked = [held[blocks[t * entries + l]] for l in range(entries)]
        numerator = jnp.dot(
            jnp.concatenate(picked, axis=1), masked[t], preferred_element_type=F32
        )
        turned[:, t * LANES : (t + 1) * LANES] = (numerator * mass_inv[t : t + 1]).astype(BF)
    sort = lax.dot_general(sorter[...], turned[...], NT_DIMS, preferred_element_type=F32)
    for g in range(ordered.shape[0]):
        ordered[g] = sort[g * LANES : (g + 1) * LANES].astype(BF)
    for k, out in enumerate(outs):
        for j in range(2):
            out[j * LANES : (j + 1) * LANES] = ordered[table[2 * k + j]]
        out[2 * LANES :] = positions[k]


def place(payloads, placing, rows):
    for k, payload in enumerate(payloads):
        rows[k * 2 * LANES : (k + 1) * 2 * LANES] = payload[: 2 * LANES]
        where = payload[2 * LANES :].astype(F32)
        for j in range(2):
            mark_places(placing, 2 * k + j, where[j : j + 1], where[2 + j : 3 + j])
    return jnp.dot(placing[...], rows[...], preferred_element_type=F32)


def place_more(count, *refs):
    before, (out, placing, rows) = refs[count:-3], refs[-3:]
    placed = place(refs[:count], placing, rows)
    for held in before:
        placed = placed + held[...]
    out[...] = placed


def finish(placed, count, *refs):
    payloads = refs[:count]
    early, base, size, connectivity, onehot, decay, readout, chosen = refs[count : count + 8]
    settled, local = refs[count + 8 : count + 10]
    exports = refs[count + 10 : count + 14]
    scratch = refs[count + 14 :]
    elements = base.shape[1]
    if placed:
        arrived = early[...]
    else:
        arrived = (early[...] + place(payloads, *scratch)).astype(BF)
    settled[...] = arrived
    taken = readout[...] * decay[...]
    taken = jnp.concatenate([taken, jnp.zeros((SUBS - 6, LANES), F32)], axis=0)
    share = lax.dot_general(
        jnp.concatenate(pieces(taken, 3), axis=0), arrived, NT_DIMS, preferred_element_type=F32
    )
    stress = base[...] + (share[0:SUBS] + share[SUBS : 2 * SUBS] + share[2 * SUBS : 3 * SUBS])
    row = iota((3 * SUBS, 2 * SUBS), 0)
    column = iota((3 * SUBS, 2 * SUBS), 1) & (SUBS - 1)
    spread = jnp.zeros(row.shape, I32)
    for i in range(3):
        for c in range(3):
            spread = jnp.where(
                ((row >> 3) == i) & (column == TENSOR[i][c]),
                2 * ((row >> c) & 1) - 1,
                spread,
            )
    forces = jnp.dot(
        spread.astype(F32).astype(BF),
        jnp.concatenate(pieces(stress, 2), axis=0),
        preferred_element_type=F32,
    )
    edge = size[...]
    forces = forces * (edge * edge * 0.25)
    group = iota((SUBS, elements), 0)
    halves = [jnp.zeros((6 * SUBS, LANES), F32) for _ in range(2)]
    for a in range(SUBS):
        here = group == (connectivity[a : a + 1] >> 7)
        highs, lows = [], []
        for i in range(3):
            value = jnp.where(here, forces[i * SUBS + a : i * SUBS + a + 1], 0.0)
            high, low = pieces(value, 2)
            highs.append(high)
            lows.append(low)
        halves[a % 2] = halves[a % 2] + jnp.dot(
            jnp.concatenate(highs + lows, axis=0), onehot[a], preferred_element_type=F32
        )
    total = halves[0] + halves[1]
    nodes = chosen[...]
    for i in range(3):
        summed = (
            total[i * SUBS : (i + 1) * SUBS] + total[(3 + i) * SUBS : (4 + i) * SUBS]
        )
        local[i] = summed
        got = lookup([summed[r : r + 1] for r in range(SUBS)], nodes)
        for m, out in enumerate(exports):
            out[i : i + 1] = got[m : m + 1]


def relax(arrived, drive, decay, history):
    history[...] = (arrived[...].astype(F32) * decay[...] + drive[...]).astype(BF)


def add_shared(local, inverse, *rest):
    received, force = rest[:-1], rest[-1]
    row, column = inverse[0], inverse[1]
    for i in range(local.shape[0]):
        total = local[i]
        for m, got in enumerate(received):
            share = jnp.take_along_axis(
                jnp.broadcast_to(got[i : i + 1], column.shape),
                column,
                axis=1,
                mode="promise_in_bounds",
            )
            total = total + jnp.where(row == m, share, 0.0)
        for r in range(local.shape[1]):
            force[i : i + 1, r * LANES : (r + 1) * LANES] = total[r : r + 1]


VMEM = pl.BlockSpec(memory_space=pltpu.VMEM)
SMEM = pl.BlockSpec(memory_space=pltpu.SMEM)
HBM = pl.BlockSpec(memory_space=pltpu.HBM)


def call(kernel, ins, outs, scratch, args, cost=2_000_000_000, out_specs=None):
    single = not isinstance(outs, (list, tuple))
    return pl.pallas_call(
        kernel,
        out_shape=outs,
        in_specs=ins,
        out_specs=out_specs or (VMEM if single else [VMEM] * len(outs)),
        scratch_shapes=scratch,
        cost_estimate=pl.CostEstimate(flops=cost, bytes_accessed=100_000, transcendentals=0),
        compiler_params=pltpu.CompilerParams(vmem_limit_bytes=24 * 1024 * 1024),
    )(*args)


def swaps(axis, first):
    total = lax.axis_size(axis)
    pairs = [(i, i + 1) for i in range(first, total - 1, 2)]
    left = sorted(set(range(total)) - {i for pair in pairs for i in pair})
    pairs += [(left[0], left[-1])] if left else []
    return [(a, b) for a, b in pairs] + [(b, a) for a, b in pairs if a != b]


def arrays(shape, dtype):
    return jax.ShapeDtypeStruct(shape, dtype)


def exclusive_order(targets, choice_total):
    one_hot = (targets[:, None] == jnp.arange(choice_total, dtype=I32)[None, :]).astype(I32)
    return jnp.sum((jnp.cumsum(one_hot, axis=0) - one_hot) * one_hot, axis=1)


def spread_rows(received, entry_slot, entry_count, weights, owner_route, owner_slot):
    targets, entries = entry_slot.shape
    block_size = weights.shape[-1]
    capacity, width, _ = received[0].shape
    me = lax.axis_index("box")
    stacked = jnp.concatenate(received, axis=0)
    held = ((entry_slot // capacity) ^ me) * capacity + entry_slot % capacity
    live = (jnp.arange(entries, dtype=I32)[None, :] < entry_count[:, None]).astype(BF)
    mass = jnp.einsum("tl,tlij->tj", live, weights, preferred_element_type=F32)
    picked = stacked[held] * live[:, :, None, None]
    numerator = jnp.einsum("tlhi,tlij->tjh", picked, weights, preferred_element_type=F32)
    projected = (numerator / mass[:, :, None]).astype(BF).reshape(targets * block_size, width)
    total = projected.shape[0]
    dom_total = lax.axis_size("dom")
    owner_capacity = 2 * (total // dom_total)
    place = owner_route * owner_capacity + exclusive_order(owner_route, dom_total)
    rows = jnp.zeros((dom_total * owner_capacity, width), BF).at[place].set(projected)
    spots = jnp.full((dom_total * owner_capacity,), total, I32).at[place].set(owner_slot)
    rows = lax.all_to_all(
        rows.reshape(dom_total, owner_capacity, width), "dom", 0, 0, tiled=True
    )
    spots = lax.all_to_all(spots.reshape(dom_total, owner_capacity), "dom", 0, 0, tiled=True)
    return (
        jnp.zeros((total, width), BF)
        .at[spots.reshape(-1)]
        .set(rows.reshape(-1, width), mode="drop")
    )


def body(old_history, box_route, entry_slot, entry_count, weights, owner_route, owner_slot,
         connectivity, shared_nodes, node_motion, elem_size, decay, couple, readout):
    blocks, width, block_size = old_history.shape
    targets, entries = entry_slot.shape
    box_total = lax.axis_size("box")
    dom_total = lax.axis_size("dom")
    capacity = blocks // 2
    rows = targets * block_size
    row_groups = rows // LANES
    elements = connectivity.shape[1]
    nodes = node_motion.shape[1]

    packed = call(
        pack_blocks, [HBM, HBM],
        [arrays((capacity, width, block_size), BF)] * box_total,
        [
            pltpu.SMEM((box_total * capacity,), I32),
            pltpu.SMEM((blocks,), I32),
            pltpu.VMEM(old_history.shape, BF),
            pltpu.SemaphoreType.DMA((2,)),
        ],
        (
            pltpu.with_memory_space_constraint(box_route, pltpu.HBM),
            pltpu.with_memory_space_constraint(old_history, pltpu.HBM),
        ),
    )
    received = {0: packed[0]}
    for k in [k for k in range(2, box_total)] + [1]:
        received[k] = lax.ppermute(packed[k], "box", [(i, i ^ k) for i in range(box_total)])
    received = [received[k] for k in range(box_total)]
    flat_weights = weights.reshape(targets, entries * block_size, block_size)
    edge = elem_size.reshape(1, elements)
    drive, base, onehot, chosen, inverse = call(
        element_parts, [VMEM] * 6,
        [
            arrays((elements, width), F32),
            arrays((SUBS, elements), F32),
            arrays((connectivity.shape[0], elements, LANES), BF),
            arrays((SUBS, shared_nodes.shape[1]), I32),
            arrays((2, nodes // LANES, LANES), I32),
        ],
        [
            pltpu.VMEM((SUBS, elements), F32),
            pltpu.VMEM((SUBS, elements), F32),
            pltpu.VMEM((2, SUBS, width), F32),
        ],
        (connectivity, node_motion, edge, couple.T, readout.T, shared_nodes),
        cost=1000,
    )
    usual = rows // dom_total
    relaxing = decay.reshape(1, width)
    if usual == LANES:
        sorter, positions, table = call(
            sort_rows, [VMEM, VMEM],
            [
                arrays((rows, rows), BF),
                arrays((dom_total, META, LANES), BF),
                arrays((2 * dom_total,), I32),
            ],
            [
                pltpu.VMEM((row_groups, LANES), F32),
                pltpu.VMEM((row_groups, LANES), F32),
                pltpu.SMEM((dom_total + 1,), I32),
            ],
            (owner_route.reshape(row_groups, LANES), owner_slot.reshape(1, rows)),
            out_specs=[VMEM, VMEM, SMEM],
        )
        masked, mass_inv, block_of = call(
            functools.partial(mask_weights, capacity), [SMEM, SMEM, VMEM],
            [
                arrays(flat_weights.shape, BF),
                arrays((targets, block_size), F32),
                arrays((targets * entries,), I32),
            ],
            [],
            (entry_slot.T, entry_count, flat_weights),
            out_specs=[VMEM, VMEM, SMEM],
        )
        payload = arrays((2 * usual + META, width), BF)
        outgoing = call(
            project_rows, [SMEM, SMEM] + [VMEM] * (4 + box_total),
            [payload] * dom_total,
            [
                pltpu.VMEM((box_total * capacity, width, block_size), BF),
                pltpu.VMEM((width, rows), BF),
                pltpu.VMEM((row_groups, LANES, width), BF),
            ],
            (table, block_of, masked, mass_inv, sorter, positions, *received),
        )
        payloads = {0: outgoing[0]}
        for k in range(1, dom_total):
            payloads[k] = lax.ppermute(outgoing[k], "dom", [(i, i ^ k) for i in range(dom_total)])
        order = arrival(dom_total)
        stages = [[0, *order[0]], *order[1:]]

        def placing(count):
            return [
                pltpu.VMEM((elements, count * 2 * usual), BF),
                pltpu.VMEM((count * 2 * usual, width), BF),
            ]

        early = []
        for stage in stages[:-1]:
            count = len(stage)
            early = [
                call(
                    functools.partial(place_more, count),
                    [VMEM] * (count + len(early)), arrays((elements, width), F32),
                    placing(count), [*[payloads[k] for k in stage], *early], cost=1000,
                )
            ]
        early = early[0]
        late = [payloads[k] for k in stages[-1]]
        placed, scratch = False, placing(len(late))
    else:
        early = spread_rows(received, entry_slot, entry_count, weights, owner_route, owner_slot)
        late = []
        placed, scratch = True, []
    export = arrays((3, shared_nodes.shape[1]), F32)
    arrived, local, *exports = call(
        functools.partial(finish, placed, len(late)),
        [VMEM] * (len(late) + 8),
        [arrays((elements, width), BF), arrays((3, nodes // LANES, LANES), F32)] + [export] * 4,
        scratch,
        (*late, early, base, edge, connectivity, onehot, relaxing, readout.T, chosen),
    )
    history = call(relax, [VMEM] * 3, arrays((elements, width), BF), [], (arrived, drive, relaxing))
    halo = [None] * 4
    for m, axis, first in ((3, "box", 1), (1, "dom", 1), (0, "dom", 0), (2, "box", 0)):
        halo[m] = lax.ppermute(exports[m], axis, swaps(axis, first))
    force = call(
        add_shared, [VMEM] * (2 + len(halo)), arrays((3, nodes), F32), [],
        (local, inverse, *halo),
    )
    return history, force


def arrival(dom_total):
    far = dom_total // 2
    return [
        [dom_total - 1, *range(far + 1, dom_total - 2), 1],
        [dom_total - 2, far - 1],
        [far, *range(far - 2, 1, -1)],
    ]


def solution(mesh):
    return jax.shard_map(
        body,
        mesh=mesh,
        in_specs=(
            P(("dom", "box"), None, None),
            P(("dom", "box")),
            P(("dom", "box"), None),
            P(("dom", "box")),
            P(("dom", "box"), None, None, None),
            P(("dom", "box")),
            P(("dom", "box")),
            P(None, ("dom", "box")),
            P(None, ("dom", "box")),
            P(None, ("dom", "box")),
            P(("dom", "box")),
            P(),
            P(),
            P(),
        ),
        out_specs=(P(("dom", "box"), None), P(None, ("dom", "box"))),
        check_vma=False,
    )
```

```python
import functools

import jax
import jax.numpy as jnp
from jax import lax
from jax.experimental import pallas as pl
from jax.experimental.pallas import tpu as pltpu
from jax.sharding import PartitionSpec as P


BF = jnp.bfloat16
F32 = jnp.float32
I32 = jnp.int32
LANES = 128
SUBS = 8
META = 8
PARTS = 16
NOWHERE = 16.0
TENSOR = ((0, 3, 5), (3, 1, 4), (5, 4, 2))
NT_DIMS = (((1,), (1,)), ((), ()))
TN_DIMS = (((0,), (0,)), ((), ()))
HIGHEST = lax.Precision.HIGHEST


def iota(shape, dim):
    return lax.broadcasted_iota(I32, shape, dim)


def pieces(x, count):
    out = []
    for _ in range(count - 1):
        high = x.astype(BF)
        out.append(high)
        x = x - high.astype(F32)
    out.append(x.astype(BF))
    return out


def as_onehot(mask):
    return jnp.where(mask, 1.0, 0.0).astype(BF)


def lookup(rows, index):
    low = index & (LANES - 1)
    high = index >> 7
    out = jnp.zeros(index.shape, F32)
    for r, row in enumerate(rows):
        got = jnp.take_along_axis(
            jnp.broadcast_to(row, index.shape), low, axis=1, mode="promise_in_bounds"
        )
        out = jnp.where(high == r, got, out)
    return out


def pack_blocks(route_hbm, old_hbm, *rest):
    outs = rest[:-4]
    table, route, old, sems = rest[-4:]
    find = pltpu.make_async_copy(route_hbm, route, sems.at[0])
    take = pltpu.make_async_copy(old_hbm, old, sems.at[1])
    find.start()
    take.start()
    find.wait()
    me = lax.axis_index("box")
    capacity = outs[0].shape[0]
    for m in range(len(outs) * capacity):
        table[m] = 0
    routes = [route[i] for i in range(old.shape[0])]
    for i, target in enumerate(routes):
        order = jnp.int32(0)
        for earlier in routes[:i]:
            order = order + (earlier == target).astype(I32)
        table[(target ^ me) * capacity + order] = i
    take.wait()
    for k, out in enumerate(outs):
        for s in range(capacity):
            out[s] = old[table[k * capacity + s]]


def marks(high, low, rows):
    shape = (LANES, high.shape[1])
    low = jnp.broadcast_to(low, shape).astype(BF)
    low_iota = iota(shape, 0).astype(F32).astype(BF)
    match = jnp.where(low_iota == low, jnp.ones_like(low), jnp.zeros_like(low))
    return jnp.concatenate(
        [
            match * jnp.broadcast_to(jnp.where(high == g, 1.0, 0.0), shape).astype(BF)
            for g in range(rows // LANES)
        ],
        axis=0,
    )


def side_by_side(x, first, count):
    return jnp.concatenate([x[first + i : first + i + 1] for i in range(count)], axis=1)


def sort_rows(owner_route, owner_slot, spots, positions, table, high_rows, low_rows, starts):
    dom_total = positions.shape[0]
    row_groups = owner_route.shape[0]
    rows = row_groups * LANES
    me = lax.axis_index("dom")
    route = owner_route[...]
    picks = jnp.concatenate([as_onehot(route == d) for d in range(dom_total)], axis=0)
    span = dom_total * row_groups
    ahead = as_onehot(iota((LANES, LANES), 0) < iota((LANES, LANES), 1))
    within = jnp.dot(picks, ahead, preferred_element_type=F32)
    totals = jnp.dot(picks, jnp.ones((LANES, LANES), BF), preferred_element_type=F32).astype(BF)
    before = as_onehot(iota((span, span), 1) < iota((span, span), 0))
    base = jnp.dot(before, totals, preferred_element_type=F32)
    ranked = within + base
    place = jnp.zeros((row_groups, LANES), F32)
    for d in range(dom_total):
        place = jnp.where(route == d, ranked[d * row_groups : (d + 1) * row_groups], place)
        starts[d] = jnp.max(base[d * row_groups : d * row_groups + 1]).astype(I32)
    starts[dom_total] = rows
    place = place.astype(I32)
    high = (place >> 7).astype(F32)
    low = (place & (LANES - 1)).astype(F32)
    spots[0] = high
    spots[1] = low
    spot = owner_slot[...]
    which = iota((PARTS, rows), 0)
    parts = jnp.where(which == 0, spot >> 7, jnp.where(which == 1, spot & (LANES - 1), 0))
    parts = parts.astype(F32).astype(BF)
    ordered = jnp.zeros((PARTS, rows), F32)
    for g in range(0, row_groups, 2):
        ordered = ordered + lax.dot_general(
            parts[:, g * LANES : (g + 2) * LANES],
            marks(side_by_side(high, g, 2), side_by_side(low, g, 2), rows),
            NT_DIMS,
            preferred_element_type=F32,
        )
    for g in range(row_groups):
        high_rows[g : g + 1] = ordered[0:1, g * LANES : (g + 1) * LANES]
        low_rows[g : g + 1] = ordered[1:2, g * LANES : (g + 1) * LANES]
    which = iota((META, LANES), 0)
    for k in range(dom_total):
        owner = me ^ k
        start = starts[owner]
        held = starts[owner + 1] - start
        block = jnp.zeros((META, LANES), F32)
        for j in range(2):
            chunk = jnp.minimum(start // LANES + j, row_groups - 1)
            table[2 * k + j] = chunk
            high = jnp.where(held > j * LANES, high_rows[pl.ds(chunk, 1)], NOWHERE)
            block = jnp.where(which == j, high, block)
            block = jnp.where(which == 2 + j, low_rows[pl.ds(chunk, 1)], block)
        positions[k] = block.astype(BF)


def mask_weights(capacity, slot, count, weights, masked, mass_inv, blocks):
    targets = weights.shape[0]
    entries = weights.shape[1] // LANES
    box = lax.axis_index("box")
    for t in range(targets):
        total = jnp.zeros((1, LANES), F32)
        for l in range(entries):
            live = l < count[t]
            span = slice(l * LANES, (l + 1) * LANES)
            part = weights[t, span, :]
            part = jnp.where(live, part, jnp.zeros_like(part))
            masked[t, span, :] = part
            total = total + jnp.sum(part.astype(F32), axis=0, keepdims=True)
            entry = jnp.where(live, slot[l, t], slot[0, t])
            source = lax.div(entry, capacity) ^ box
            blocks[t * entries + l] = source * capacity + lax.rem(entry, capacity)
        mass_inv[t : t + 1] = 1.0 / total


def element_parts(connectivity, motion, size, couple, readout, shared, drive, base, onehot,
                  grouped, quarter, chosen, inverse, strain, elastic, wide):
    elements = connectivity.shape[1]
    corners = connectivity.shape[0]
    groups = motion.shape[1] // LANES
    corner = iota((corners, LANES), 0)
    signs = [(2 * ((corner >> c) & 1) - 1).astype(F32) for c in range(3)]
    low_iota = iota((LANES, LANES), 0)
    lane_iota = iota((LANES, LANES), 1).astype(F32)
    eighth = iota((groups, LANES), 0)
    strain[...] = jnp.zeros_like(strain)
    elastic[...] = jnp.zeros_like(elastic)
    for j in range(elements // LANES):
        lanes = slice(j * LANES, (j + 1) * LANES)
        nodes = connectivity[:, lanes]
        edge = size[:, lanes]
        scale = 1.0 / (4.0 * edge)
        quarter[:, lanes] = edge * edge * 0.25
        grad = []
        for i in range(3):
            moved = lookup(
                [motion[i : i + 1, r * LANES : (r + 1) * LANES] for r in range(groups)], nodes
            )
            grad.append(
                [jnp.sum(moved * signs[c], axis=0, keepdims=True) * scale for c in range(3)]
            )
        rows = [
            grad[0][0],
            grad[1][1],
            grad[2][2],
            grad[0][1] + grad[1][0],
            grad[1][2] + grad[2][1],
            grad[2][0] + grad[0][2],
        ]
        volume = 1.2 * (rows[0] + rows[1] + rows[2])
        for c in range(6):
            strain[c : c + 1, lanes] = rows[c]
            elastic[c : c + 1, lanes] = volume + 1.6 * rows[c] if c < 3 else 0.8 * rows[c]
        turned = (nodes & (LANES - 1)).astype(F32).T
        for a in range(corners):
            here = as_onehot(eighth == (nodes[a : a + 1] >> 7))
            grouped[a, :, lanes] = jnp.concatenate([here, here], axis=0)
            onehot[a, lanes, :] = as_onehot(lane_iota == turned[:, a : a + 1])
    wide[...] = jnp.zeros_like(wide)
    wide[0, 0:6] = couple[...]
    wide[1, 0:6] = readout[...]
    drive[...] = lax.dot_general(
        strain[...], wide[0], TN_DIMS, preferred_element_type=F32, precision=HIGHEST
    )
    base[...] = elastic[...] + lax.dot_general(
        wide[1], drive[...], NT_DIMS, preferred_element_type=F32, precision=HIGHEST
    )
    odd_dom = lax.axis_index("dom") & 1
    odd_box = lax.axis_index("box") & 1
    chosen[...] = jnp.zeros_like(chosen)
    chosen[0:1] = shared[pl.ds(1 - odd_dom, 1)]
    chosen[1:2] = shared[pl.ds(odd_dom, 1)]
    chosen[2:3] = shared[pl.ds(3 - odd_box, 1)]
    chosen[3:4] = shared[pl.ds(2 + odd_box, 1)]
    group = iota((groups, LANES), 0)
    lane = iota((groups, LANES), 1)
    total = jnp.zeros((2 * groups, LANES), F32)
    for m in range(4):
        axis = "dom" if m < 2 else "box"
        here = lax.axis_index(axis)
        partner = here + (1 - 2 * (here & 1)) * (1 if m % 2 == 0 else -1)
        paired = (partner >= 0) & (partner < lax.axis_size(axis))
        nodes = jnp.where(paired, chosen[m : m + 1], groups * LANES)
        here = group == (nodes >> 7)
        marks = jnp.concatenate(
            [jnp.where(here, m + 1, 0), jnp.where(here, lane, 0)], axis=0
        ).astype(F32)
        total = total + lax.dot_general(
            marks.astype(BF),
            as_onehot(low_iota == (nodes & (LANES - 1))),
            NT_DIMS,
            preferred_element_type=F32,
        )
    total = total.astype(I32)
    inverse[0] = total[:groups] - 1
    inverse[1] = total[groups:]


def project_rows(table, blocks, masked, mass_inv, spots, positions, *rest):
    dom_total = positions.shape[0]
    box_total = lax.axis_size("box")
    received = rest[:box_total]
    outs = rest[box_total : box_total + dom_total]
    held, turned, ordered = rest[box_total + dom_total :]
    capacity = received[0].shape[0]
    for k, block in enumerate(received):
        for s in range(capacity):
            held[k * capacity + s] = block[s]
    targets = masked.shape[0]
    entries = masked.shape[1] // LANES
    for t in range(targets):
        picked = [held[blocks[t * entries + l]] for l in range(entries)]
        numerator = jnp.dot(
            jnp.concatenate(picked, axis=1), masked[t], preferred_element_type=F32
        )
        turned[:, t * LANES : (t + 1) * LANES] = (numerator * mass_inv[t : t + 1]).astype(BF)
    high, low = spots[0], spots[1]
    rows = turned.shape[1]
    sort = jnp.zeros((rows, LANES), F32)
    for g in range(0, rows // LANES, 2):
        sort = sort + lax.dot_general(
            marks(side_by_side(high, g, 2), side_by_side(low, g, 2), rows),
            turned[:, g * LANES : (g + 2) * LANES],
            NT_DIMS,
            preferred_element_type=F32,
        )
    for g in range(ordered.shape[0]):
        ordered[g] = sort[g * LANES : (g + 1) * LANES].astype(BF)
    for k, out in enumerate(outs):
        for j in range(2):
            out[j * LANES : (j + 1) * LANES] = ordered[table[2 * k + j]]
        out[2 * LANES :] = positions[k]


def place(payloads, elements):
    total = None
    for payload in payloads:
        where = payload[2 * LANES :].astype(F32)
        part = jnp.dot(
            marks(side_by_side(where, 0, 2), side_by_side(where, 2, 2), elements),
            payload[: 2 * LANES],
            preferred_element_type=F32,
        )
        total = part if total is None else total + part
    return total


def place_more(count, *refs):
    before, out = refs[count:-1], refs[-1]
    placed = place(refs[:count], out.shape[0])
    for held in before:
        placed = placed + held[...]
    out[...] = placed


def finish(placed, count, *refs):
    payloads = refs[:count]
    early, base, quarter, grouped, onehot, decay, readout, chosen = refs[count : count + 8]
    settled, local = refs[count + 8 : count + 10]
    exports = refs[count + 10 : count + 14]
    (spread_forces,) = refs[count + 14 :]
    elements = base.shape[1]
    if placed:
        arrived = early[...]
    else:
        arrived = (early[...] + place(payloads, elements)).astype(BF)
    settled[...] = arrived
    taken = readout[...] * decay[...]
    taken = jnp.concatenate([taken, jnp.zeros((SUBS - 6, LANES), F32)], axis=0)
    share = lax.dot_general(
        jnp.concatenate(pieces(taken, 3), axis=0), arrived, NT_DIMS, preferred_element_type=F32
    )
    stress = base[...] + (share[0:SUBS] + share[SUBS : 2 * SUBS] + share[2 * SUBS : 3 * SUBS])
    row = iota((3 * SUBS, 2 * SUBS), 0)
    column = iota((3 * SUBS, 2 * SUBS), 1) & (SUBS - 1)
    spread = jnp.zeros(row.shape, I32)
    for i in range(3):
        for c in range(3):
            spread = jnp.where(
                ((row >> 3) == i) & (column == TENSOR[i][c]),
                2 * ((row >> c) & 1) - 1,
                spread,
            )
    forces = jnp.dot(
        spread.astype(F32).astype(BF),
        jnp.concatenate(pieces(stress, 2), axis=0),
        preferred_element_type=F32,
    )
    forces = forces * quarter[...]
    high = forces.astype(BF).astype(F32)
    spread_forces[: 3 * SUBS] = high
    spread_forces[3 * SUBS :] = forces - high
    halves = [jnp.zeros((6 * SUBS, LANES), F32) for _ in range(2)]
    for a in range(SUBS):
        mask = grouped[a]
        values = []
        for i in range(3):
            both = [
                spread_forces[pl.ds(n * 3 * SUBS + i * SUBS + a, SUBS, stride=0), :]
                for n in range(2)
            ]
            values.append(jnp.concatenate(both, axis=0).astype(BF) * mask)
        halves[a % 2] = halves[a % 2] + jnp.dot(
            jnp.concatenate(values, axis=0), onehot[a], preferred_element_type=F32
        )
    total = halves[0] + halves[1]
    nodes = chosen[...]
    for i in range(3):
        summed = (
            total[2 * i * SUBS : (2 * i + 1) * SUBS]
            + total[(2 * i + 1) * SUBS : (2 * i + 2) * SUBS]
        )
        local[i] = summed
        got = lookup([summed[r : r + 1] for r in range(SUBS)], nodes)
        for m, out in enumerate(exports):
            out[i : i + 1] = got[m : m + 1]


def relax(arrived, drive, decay, history):
    history[...] = (arrived[...].astype(F32) * decay[...] + drive[...]).astype(BF)


def add_shared(local, inverse, *rest):
    received, force = rest[:-1], rest[-1]
    row, column = inverse[0], inverse[1]
    for i in range(local.shape[0]):
        total = local[i]
        for m, got in enumerate(received):
            share = jnp.take_along_axis(
                jnp.broadcast_to(got[i : i + 1], column.shape),
                column,
                axis=1,
                mode="promise_in_bounds",
            )
            total = total + jnp.where(row == m, share, 0.0)
        for r in range(local.shape[1]):
            force[i : i + 1, r * LANES : (r + 1) * LANES] = total[r : r + 1]


VMEM = pl.BlockSpec(memory_space=pltpu.VMEM)
SMEM = pl.BlockSpec(memory_space=pltpu.SMEM)
HBM = pl.BlockSpec(memory_space=pltpu.HBM)


def call(kernel, ins, outs, scratch, args, cost=2_000_000_000, out_specs=None):
    single = not isinstance(outs, (list, tuple))
    return pl.pallas_call(
        kernel,
        out_shape=outs,
        in_specs=ins,
        out_specs=out_specs or (VMEM if single else [VMEM] * len(outs)),
        scratch_shapes=scratch,
        cost_estimate=pl.CostEstimate(flops=cost, bytes_accessed=100_000, transcendentals=0),
        compiler_params=pltpu.CompilerParams(vmem_limit_bytes=24 * 1024 * 1024),
    )(*args)


def swaps(axis, first):
    total = lax.axis_size(axis)
    pairs = [(i, i + 1) for i in range(first, total - 1, 2)]
    left = sorted(set(range(total)) - {i for pair in pairs for i in pair})
    pairs += [(left[0], left[-1])] if left else []
    return [(a, b) for a, b in pairs] + [(b, a) for a, b in pairs if a != b]


def arrays(shape, dtype):
    return jax.ShapeDtypeStruct(shape, dtype)


def exclusive_order(targets, choice_total):
    one_hot = (targets[:, None] == jnp.arange(choice_total, dtype=I32)[None, :]).astype(I32)
    return jnp.sum((jnp.cumsum(one_hot, axis=0) - one_hot) * one_hot, axis=1)


def spread_rows(received, entry_slot, entry_count, weights, owner_route, owner_slot):
    targets, entries = entry_slot.shape
    block_size = weights.shape[-1]
    capacity, width, _ = received[0].shape
    me = lax.axis_index("box")
    stacked = jnp.concatenate(received, axis=0)
    held = ((entry_slot // capacity) ^ me) * capacity + entry_slot % capacity
    live = (jnp.arange(entries, dtype=I32)[None, :] < entry_count[:, None]).astype(BF)
    mass = jnp.einsum("tl,tlij->tj", live, weights, preferred_element_type=F32)
    picked = stacked[held] * live[:, :, None, None]
    numerator = jnp.einsum("tlhi,tlij->tjh", picked, weights, preferred_element_type=F32)
    projected = (numerator / mass[:, :, None]).astype(BF).reshape(targets * block_size, width)
    total = projected.shape[0]
    dom_total = lax.axis_size("dom")
    owner_capacity = 2 * (total // dom_total)
    place = owner_route * owner_capacity + exclusive_order(owner_route, dom_total)
    rows = jnp.zeros((dom_total * owner_capacity, width), BF).at[place].set(projected)
    spots = jnp.full((dom_total * owner_capacity,), total, I32).at[place].set(owner_slot)
    rows = lax.all_to_all(
        rows.reshape(dom_total, owner_capacity, width), "dom", 0, 0, tiled=True
    )
    spots = lax.all_to_all(spots.reshape(dom_total, owner_capacity), "dom", 0, 0, tiled=True)
    return (
        jnp.zeros((total, width), BF)
        .at[spots.reshape(-1)]
        .set(rows.reshape(-1, width), mode="drop")
    )


def body(old_history, box_route, entry_slot, entry_count, weights, owner_route, owner_slot,
         connectivity, shared_nodes, node_motion, elem_size, decay, couple, readout):
    blocks, width, block_size = old_history.shape
    targets, entries = entry_slot.shape
    box_total = lax.axis_size("box")
    dom_total = lax.axis_size("dom")
    capacity = blocks // 2
    rows = targets * block_size
    row_groups = rows // LANES
    elements = connectivity.shape[1]
    nodes = node_motion.shape[1]

    packed = call(
        pack_blocks, [HBM, HBM],
        [arrays((capacity, width, block_size), BF)] * box_total,
        [
            pltpu.SMEM((box_total * capacity,), I32),
            pltpu.SMEM((blocks,), I32),
            pltpu.VMEM(old_history.shape, BF),
            pltpu.SemaphoreType.DMA((2,)),
        ],
        (
            pltpu.with_memory_space_constraint(box_route, pltpu.HBM),
            pltpu.with_memory_space_constraint(old_history, pltpu.HBM),
        ),
    )
    received = {0: packed[0]}
    for k in [k for k in range(2, box_total)] + [1]:
        received[k] = lax.ppermute(packed[k], "box", [(i, i ^ k) for i in range(box_total)])
    received = [received[k] for k in range(box_total)]
    flat_weights = weights.reshape(targets, entries * block_size, block_size)
    edge = elem_size.reshape(1, elements)
    drive, base, onehot, grouped, quarter, chosen, inverse = call(
        element_parts, [VMEM] * 6,
        [
            arrays((elements, width), F32),
            arrays((SUBS, elements), F32),
            arrays((connectivity.shape[0], elements, LANES), BF),
            arrays((connectivity.shape[0], 2 * nodes // LANES, elements), BF),
            arrays((1, elements), F32),
            arrays((SUBS, shared_nodes.shape[1]), I32),
            arrays((2, nodes // LANES, LANES), I32),
        ],
        [
            pltpu.VMEM((SUBS, elements), F32),
            pltpu.VMEM((SUBS, elements), F32),
            pltpu.VMEM((2, SUBS, width), F32),
        ],
        (connectivity, node_motion, edge, couple.T, readout.T, shared_nodes),
        cost=1000,
    )
    usual = rows // dom_total
    relaxing = decay.reshape(1, width)
    if usual == LANES:
        spots, positions, table = call(
            sort_rows, [VMEM, VMEM],
            [
                arrays((2, row_groups, LANES), F32),
                arrays((dom_total, META, LANES), BF),
                arrays((2 * dom_total,), I32),
            ],
            [
                pltpu.VMEM((row_groups, LANES), F32),
                pltpu.VMEM((row_groups, LANES), F32),
                pltpu.SMEM((dom_total + 1,), I32),
            ],
            (owner_route.reshape(row_groups, LANES), owner_slot.reshape(1, rows)),
            out_specs=[VMEM, VMEM, SMEM],
        )
        masked, mass_inv, block_of = call(
            functools.partial(mask_weights, capacity), [SMEM, SMEM, VMEM],
            [
                arrays(flat_weights.shape, BF),
                arrays((targets, block_size), F32),
                arrays((targets * entries,), I32),
            ],
            [],
            (entry_slot.T, entry_count, flat_weights),
            out_specs=[VMEM, VMEM, SMEM],
        )
        payload = arrays((2 * usual + META, width), BF)
        outgoing = call(
            project_rows, [SMEM, SMEM] + [VMEM] * (4 + box_total),
            [payload] * dom_total,
            [
                pltpu.VMEM((box_total * capacity, width, block_size), BF),
                pltpu.VMEM((width, rows), BF),
                pltpu.VMEM((row_groups, LANES, width), BF),
            ],
            (table, block_of, masked, mass_inv, spots, positions, *received),
        )
        payloads = {0: outgoing[0]}
        for k in range(1, dom_total):
            payloads[k] = lax.ppermute(outgoing[k], "dom", [(i, i ^ k) for i in range(dom_total)])
        order = arrival(dom_total)
        stages = [[0, *order[0]], *order[1:]]

        early = []
        for stage in stages[:-1]:
            count = len(stage)
            early = [
                call(
                    functools.partial(place_more, count),
                    [VMEM] * (count + len(early)), arrays((elements, width), F32),
                    [], [*[payloads[k] for k in stage], *early], cost=1000,
                )
            ]
        early = early[0]
        late = [payloads[k] for k in stages[-1]]
        placed = False
    else:
        early = spread_rows(received, entry_slot, entry_count, weights, owner_route, owner_slot)
        late = []
        placed = True
    export = arrays((3, shared_nodes.shape[1]), F32)
    arrived, local, *exports = call(
        functools.partial(finish, placed, len(late)),
        [VMEM] * (len(late) + 8),
        [arrays((elements, width), BF), arrays((3, nodes // LANES, LANES), F32)] + [export] * 4,
        [pltpu.VMEM((6 * SUBS, elements), F32)],
        (*late, early, base, quarter, grouped, onehot, relaxing, readout.T, chosen),
    )
    history = call(relax, [VMEM] * 3, arrays((elements, width), BF), [], (arrived, drive, relaxing))
    halo = [None] * 4
    for m, axis, first in ((3, "box", 1), (1, "dom", 1), (0, "dom", 0), (2, "box", 0)):
        halo[m] = lax.ppermute(exports[m], axis, swaps(axis, first))
    force = call(
        add_shared, [VMEM] * (2 + len(halo)), arrays((3, nodes), F32), [],
        (local, inverse, *halo),
    )
    return history, force


def arrival(dom_total):
    far = dom_total // 2
    return [
        [dom_total - 1, *range(far + 1, dom_total - 2), 1],
        [dom_total - 2, far - 1],
        [far, *range(far - 2, 1, -1)],
    ]


def solution(mesh):
    return jax.shard_map(
        body,
        mesh=mesh,
        in_specs=(
            P(("dom", "box"), None, None),
            P(("dom", "box")),
            P(("dom", "box"), None),
            P(("dom", "box")),
            P(("dom", "box"), None, None, None),
            P(("dom", "box")),
            P(("dom", "box")),
            P(None, ("dom", "box")),
            P(None, ("dom", "box")),
            P(None, ("dom", "box")),
            P(("dom", "box")),
            P(),
            P(),
            P(),
        ),
        out_specs=(P(("dom", "box"), None), P(None, ("dom", "box"))),
        check_vma=False,
    )
```

```python
import functools

import jax
import jax.numpy as jnp
from jax import lax
from jax.experimental import pallas as pl
from jax.experimental.pallas import tpu as pltpu
from jax.sharding import PartitionSpec as P


BF = jnp.bfloat16
F32 = jnp.float32
I32 = jnp.int32
LANES = 128
SUBS = 8
META = 8
PARTS = 16
NOWHERE = 16.0
TENSOR = ((0, 3, 5), (3, 1, 4), (5, 4, 2))
NT_DIMS = (((1,), (1,)), ((), ()))
TN_DIMS = (((0,), (0,)), ((), ()))
HIGHEST = lax.Precision.HIGHEST


def iota(shape, dim):
    return lax.broadcasted_iota(I32, shape, dim)


def pieces(x, count):
    out = []
    for _ in range(count - 1):
        high = x.astype(BF)
        out.append(high)
        x = x - high.astype(F32)
    out.append(x.astype(BF))
    return out


def as_onehot(mask):
    return jnp.where(mask, 1.0, 0.0).astype(BF)


def lookup(rows, index):
    low = index & (LANES - 1)
    high = index >> 7
    out = jnp.zeros(index.shape, F32)
    for r, row in enumerate(rows):
        got = jnp.take_along_axis(
            jnp.broadcast_to(row, index.shape), low, axis=1, mode="promise_in_bounds"
        )
        out = jnp.where(high == r, got, out)
    return out


def pack_blocks(route_hbm, old_hbm, *rest):
    outs = rest[:-4]
    table, route, old, sems = rest[-4:]
    find = pltpu.make_async_copy(route_hbm, route, sems.at[0])
    take = pltpu.make_async_copy(old_hbm, old, sems.at[1])
    find.start()
    take.start()
    find.wait()
    me = lax.axis_index("box")
    capacity = outs[0].shape[0]
    for m in range(len(outs) * capacity):
        table[m] = 0
    routes = [route[i] for i in range(old.shape[0])]
    for i, target in enumerate(routes):
        order = jnp.int32(0)
        for earlier in routes[:i]:
            order = order + (earlier == target).astype(I32)
        table[(target ^ me) * capacity + order] = i
    take.wait()
    for k, out in enumerate(outs):
        for s in range(capacity):
            out[s] = old[table[k * capacity + s]]


def marks(high, low, rows):
    shape = (LANES, high.shape[1])
    low = jnp.broadcast_to(low, shape).astype(BF)
    low_iota = iota(shape, 0).astype(F32).astype(BF)
    match = jnp.where(low_iota == low, jnp.ones_like(low), jnp.zeros_like(low))
    return jnp.concatenate(
        [
            match * jnp.broadcast_to(jnp.where(high == g, 1.0, 0.0), shape).astype(BF)
            for g in range(rows // LANES)
        ],
        axis=0,
    )


def side_by_side(x, first, count):
    return jnp.concatenate([x[first + i : first + i + 1] for i in range(count)], axis=1)


def sort_rows(owner_route, owner_slot, spots, positions, table, high_rows, low_rows, starts):
    dom_total = positions.shape[0]
    row_groups = owner_route.shape[0]
    rows = row_groups * LANES
    me = lax.axis_index("dom")
    route = owner_route[...]
    picks = jnp.concatenate([as_onehot(route == d) for d in range(dom_total)], axis=0)
    span = dom_total * row_groups
    ahead = as_onehot(iota((LANES, LANES), 0) < iota((LANES, LANES), 1))
    within = jnp.dot(picks, ahead, preferred_element_type=F32)
    totals = jnp.dot(picks, jnp.ones((LANES, LANES), BF), preferred_element_type=F32).astype(BF)
    before = as_onehot(iota((span, span), 1) < iota((span, span), 0))
    base = jnp.dot(before, totals, preferred_element_type=F32)
    ranked = within + base
    place = jnp.zeros((row_groups, LANES), F32)
    for d in range(dom_total):
        place = jnp.where(route == d, ranked[d * row_groups : (d + 1) * row_groups], place)
        starts[d] = jnp.max(base[d * row_groups : d * row_groups + 1]).astype(I32)
    starts[dom_total] = rows
    place = place.astype(I32)
    high = (place >> 7).astype(F32)
    low = (place & (LANES - 1)).astype(F32)
    spots[0] = high
    spots[1] = low
    spot = owner_slot[...]
    which = iota((PARTS, rows), 0)
    parts = jnp.where(which == 0, spot >> 7, jnp.where(which == 1, spot & (LANES - 1), 0))
    parts = parts.astype(F32).astype(BF)
    ordered = jnp.zeros((PARTS, rows), F32)
    for g in range(0, row_groups, 2):
        ordered = ordered + lax.dot_general(
            parts[:, g * LANES : (g + 2) * LANES],
            marks(side_by_side(high, g, 2), side_by_side(low, g, 2), rows),
            NT_DIMS,
            preferred_element_type=F32,
        )
    for g in range(row_groups):
        high_rows[g : g + 1] = ordered[0:1, g * LANES : (g + 1) * LANES]
        low_rows[g : g + 1] = ordered[1:2, g * LANES : (g + 1) * LANES]
    which = iota((META, LANES), 0)
    for k in range(dom_total):
        owner = me ^ k
        start = starts[owner]
        held = starts[owner + 1] - start
        block = jnp.zeros((META, LANES), F32)
        for j in range(2):
            chunk = jnp.minimum(start // LANES + j, row_groups - 1)
            table[2 * k + j] = chunk
            high = jnp.where(held > j * LANES, high_rows[pl.ds(chunk, 1)], NOWHERE)
            block = jnp.where(which == j, high, block)
            block = jnp.where(which == 2 + j, low_rows[pl.ds(chunk, 1)], block)
        positions[k] = block.astype(BF)


def mask_weights(capacity, slot, count, weights, masked, mass_inv, blocks):
    targets = weights.shape[0]
    entries = weights.shape[1] // LANES
    box = lax.axis_index("box")
    for t in range(targets):
        total = jnp.zeros((1, LANES), F32)
        for l in range(entries):
            live = l < count[t]
            span = slice(l * LANES, (l + 1) * LANES)
            part = weights[t, span, :]
            part = jnp.where(live, part, jnp.zeros_like(part))
            masked[t, span, :] = part
            total = total + jnp.sum(part.astype(F32), axis=0, keepdims=True)
            entry = jnp.where(live, slot[l, t], slot[0, t])
            source = lax.div(entry, capacity) ^ box
            blocks[t * entries + l] = source * capacity + lax.rem(entry, capacity)
        mass_inv[t : t + 1] = 1.0 / total


def element_parts(connectivity, motion, size, couple, readout, shared, drive, base, onehot,
                  grouped, quarter, chosen, inverse, strain, elastic, wide):
    elements = connectivity.shape[1]
    corners = connectivity.shape[0]
    groups = motion.shape[1] // LANES
    corner = iota((corners, LANES), 0)
    signs = [(2 * ((corner >> c) & 1) - 1).astype(F32) for c in range(3)]
    low_iota = iota((LANES, LANES), 0)
    lane_iota = iota((LANES, LANES), 1).astype(F32)
    eighth = iota((groups, LANES), 0)
    strain[...] = jnp.zeros_like(strain)
    elastic[...] = jnp.zeros_like(elastic)
    for j in range(elements // LANES):
        lanes = slice(j * LANES, (j + 1) * LANES)
        nodes = connectivity[:, lanes]
        edge = size[:, lanes]
        scale = 1.0 / (4.0 * edge)
        quarter[:, lanes] = edge * edge * 0.25
        grad = []
        for i in range(3):
            moved = lookup(
                [motion[i : i + 1, r * LANES : (r + 1) * LANES] for r in range(groups)], nodes
            )
            grad.append(
                [jnp.sum(moved * signs[c], axis=0, keepdims=True) * scale for c in range(3)]
            )
        rows = [
            grad[0][0],
            grad[1][1],
            grad[2][2],
            grad[0][1] + grad[1][0],
            grad[1][2] + grad[2][1],
            grad[2][0] + grad[0][2],
        ]
        volume = 1.2 * (rows[0] + rows[1] + rows[2])
        for c in range(6):
            strain[c : c + 1, lanes] = rows[c]
            elastic[c : c + 1, lanes] = volume + 1.6 * rows[c] if c < 3 else 0.8 * rows[c]
        turned = (nodes & (LANES - 1)).astype(F32).T
        for a in range(corners):
            here = as_onehot(eighth == (nodes[a : a + 1] >> 7))
            grouped[a, :, lanes] = jnp.concatenate([here, here], axis=0)
            onehot[a, lanes, :] = as_onehot(lane_iota == turned[:, a : a + 1])
    wide[...] = jnp.zeros_like(wide)
    wide[0, 0:6] = couple[...]
    wide[1, 0:6] = readout[...]
    drive[...] = lax.dot_general(
        strain[...], wide[0], TN_DIMS, preferred_element_type=F32, precision=HIGHEST
    )
    base[...] = elastic[...] + lax.dot_general(
        wide[1], drive[...], NT_DIMS, preferred_element_type=F32, precision=HIGHEST
    )
    odd_dom = lax.axis_index("dom") & 1
    odd_box = lax.axis_index("box") & 1
    chosen[...] = jnp.zeros_like(chosen)
    chosen[0:1] = shared[pl.ds(1 - odd_dom, 1)]
    chosen[1:2] = shared[pl.ds(odd_dom, 1)]
    chosen[2:3] = shared[pl.ds(3 - odd_box, 1)]
    chosen[3:4] = shared[pl.ds(2 + odd_box, 1)]
    group = iota((groups, LANES), 0)
    lane = iota((groups, LANES), 1)
    total = jnp.zeros((2 * groups, LANES), F32)
    for m in range(4):
        axis = "dom" if m < 2 else "box"
        here = lax.axis_index(axis)
        partner = here + (1 - 2 * (here & 1)) * (1 if m % 2 == 0 else -1)
        paired = (partner >= 0) & (partner < lax.axis_size(axis))
        nodes = jnp.where(paired, chosen[m : m + 1], groups * LANES)
        here = group == (nodes >> 7)
        marks = jnp.concatenate(
            [jnp.where(here, m + 1, 0), jnp.where(here, lane, 0)], axis=0
        ).astype(F32)
        total = total + lax.dot_general(
            marks.astype(BF),
            as_onehot(low_iota == (nodes & (LANES - 1))),
            NT_DIMS,
            preferred_element_type=F32,
        )
    total = total.astype(I32)
    inverse[0] = total[:groups] - 1
    inverse[1] = total[groups:]


def project_rows(table_in, blocks_in, masked, mass_inv, spots, positions, *rest):
    dom_total = positions.shape[0]
    box_total = lax.axis_size("box")
    received = rest[:box_total]
    outs = rest[box_total : box_total + dom_total]
    held, turned, ordered, table, blocks, sems = rest[box_total + dom_total :]
    capacity = received[0].shape[0]
    copies = [
        pltpu.make_async_copy(source, target, sems.at[i])
        for i, (source, target) in enumerate([(table_in, table), (blocks_in, blocks)])
    ]
    for copy in copies:
        copy.start()
    for k, block in enumerate(received):
        for s in range(capacity):
            held[k * capacity + s] = block[s]
    for copy in copies:
        copy.wait()
    targets = masked.shape[0]
    entries = masked.shape[1] // LANES
    for t in range(targets):
        picked = [held[blocks[t * entries + l]] for l in range(entries)]
        numerator = jnp.dot(
            jnp.concatenate(picked, axis=1), masked[t], preferred_element_type=F32
        )
        turned[:, t * LANES : (t + 1) * LANES] = (numerator * mass_inv[t : t + 1]).astype(BF)
    high, low = spots[0], spots[1]
    rows = turned.shape[1]
    sort = jnp.zeros((rows, LANES), F32)
    for g in range(0, rows // LANES, 2):
        sort = sort + lax.dot_general(
            marks(side_by_side(high, g, 2), side_by_side(low, g, 2), rows),
            turned[:, g * LANES : (g + 2) * LANES],
            NT_DIMS,
            preferred_element_type=F32,
        )
    for g in range(ordered.shape[0]):
        ordered[g] = sort[g * LANES : (g + 1) * LANES].astype(BF)
    for k, out in enumerate(outs):
        for j in range(2):
            out[j * LANES : (j + 1) * LANES] = ordered[table[2 * k + j]]
        out[2 * LANES :] = positions[k]


def place(payloads, elements):
    total = None
    for payload in payloads:
        where = payload[2 * LANES :].astype(F32)
        part = jnp.dot(
            marks(side_by_side(where, 0, 2), side_by_side(where, 2, 2), elements),
            payload[: 2 * LANES],
            preferred_element_type=F32,
        )
        total = part if total is None else total + part
    return total


def place_more(count, *refs):
    before, out = refs[count:-1], refs[-1]
    placed = place(refs[:count], out.shape[0])
    for held in before:
        placed = placed + held[...]
    out[...] = placed


def finish(placed, count, *refs):
    payloads = refs[:count]
    early, base, quarter, grouped, onehot, decay, readout, chosen = refs[count : count + 8]
    settled, local = refs[count + 8 : count + 10]
    exports = refs[count + 10 : count + 14]
    (spread_forces,) = refs[count + 14 :]
    elements = base.shape[1]
    if placed:
        arrived = early[...]
    else:
        arrived = (early[...] + place(payloads, elements)).astype(BF)
    settled[...] = arrived
    taken = readout[...] * decay[...]
    taken = jnp.concatenate([taken, jnp.zeros((SUBS - 6, LANES), F32)], axis=0)
    share = lax.dot_general(
        jnp.concatenate(pieces(taken, 3), axis=0), arrived, NT_DIMS, preferred_element_type=F32
    )
    stress = base[...] + (share[0:SUBS] + share[SUBS : 2 * SUBS] + share[2 * SUBS : 3 * SUBS])
    row = iota((3 * SUBS, 2 * SUBS), 0)
    column = iota((3 * SUBS, 2 * SUBS), 1) & (SUBS - 1)
    spread = jnp.zeros(row.shape, I32)
    for i in range(3):
        for c in range(3):
            spread = jnp.where(
                ((row >> 3) == i) & (column == TENSOR[i][c]),
                2 * ((row >> c) & 1) - 1,
                spread,
            )
    forces = jnp.dot(
        spread.astype(F32).astype(BF),
        jnp.concatenate(pieces(stress, 2), axis=0),
        preferred_element_type=F32,
    )
    forces = forces * quarter[...]
    high = forces.astype(BF).astype(F32)
    spread_forces[: 3 * SUBS] = high
    spread_forces[3 * SUBS :] = forces - high
    halves = [jnp.zeros((6 * SUBS, LANES), F32) for _ in range(2)]
    for a in range(SUBS):
        mask = grouped[a]
        values = []
        for i in range(3):
            both = [
                spread_forces[pl.ds(n * 3 * SUBS + i * SUBS + a, SUBS, stride=0), :]
                for n in range(2)
            ]
            values.append(jnp.concatenate(both, axis=0).astype(BF) * mask)
        halves[a % 2] = halves[a % 2] + jnp.dot(
            jnp.concatenate(values, axis=0), onehot[a], preferred_element_type=F32
        )
    total = halves[0] + halves[1]
    nodes = chosen[...]
    for i in range(3):
        summed = (
            total[2 * i * SUBS : (2 * i + 1) * SUBS]
            + total[(2 * i + 1) * SUBS : (2 * i + 2) * SUBS]
        )
        local[i] = summed
        got = lookup([summed[r : r + 1] for r in range(SUBS)], nodes)
        for m, out in enumerate(exports):
            out[i : i + 1] = got[m : m + 1]


def relax(arrived, drive, decay, history):
    history[...] = (arrived[...].astype(F32) * decay[...] + drive[...]).astype(BF)


def add_shared(local, inverse, *rest):
    received, force = rest[:-1], rest[-1]
    row, column = inverse[0], inverse[1]
    for i in range(local.shape[0]):
        total = local[i]
        for m, got in enumerate(received):
            share = jnp.take_along_axis(
                jnp.broadcast_to(got[i : i + 1], column.shape),
                column,
                axis=1,
                mode="promise_in_bounds",
            )
            total = total + jnp.where(row == m, share, 0.0)
        for r in range(local.shape[1]):
            force[i : i + 1, r * LANES : (r + 1) * LANES] = total[r : r + 1]


VMEM = pl.BlockSpec(memory_space=pltpu.VMEM)
SMEM = pl.BlockSpec(memory_space=pltpu.SMEM)
HBM = pl.BlockSpec(memory_space=pltpu.HBM)


def call(kernel, ins, outs, scratch, args, cost=2_000_000_000, out_specs=None):
    single = not isinstance(outs, (list, tuple))
    return pl.pallas_call(
        kernel,
        out_shape=outs,
        in_specs=ins,
        out_specs=out_specs or (VMEM if single else [VMEM] * len(outs)),
        scratch_shapes=scratch,
        cost_estimate=pl.CostEstimate(flops=cost, bytes_accessed=100_000, transcendentals=0),
        compiler_params=pltpu.CompilerParams(vmem_limit_bytes=24 * 1024 * 1024),
    )(*args)


def swaps(which):
    dom_total, box_total = lax.axis_size("dom"), lax.axis_size("box")
    pairs = []
    for d in range(dom_total):
        for b in range(box_total):
            here, total = (d, dom_total) if which < 2 else (b, box_total)
            other = here + (1 - 2 * (here & 1)) * (1 if which % 2 == 0 else -1)
            if not 0 <= other < total:
                partner = (d, b ^ 1 if which < 2 else box_total - 1 - b)
            else:
                partner = (other, b) if which < 2 else (d, other)
            pairs.append((d * box_total + b, partner[0] * box_total + partner[1]))
    return pairs


def arrays(shape, dtype):
    return jax.ShapeDtypeStruct(shape, dtype)


def exclusive_order(targets, choice_total):
    one_hot = (targets[:, None] == jnp.arange(choice_total, dtype=I32)[None, :]).astype(I32)
    return jnp.sum((jnp.cumsum(one_hot, axis=0) - one_hot) * one_hot, axis=1)


def spread_rows(received, entry_slot, entry_count, weights, owner_route, owner_slot):
    targets, entries = entry_slot.shape
    block_size = weights.shape[-1]
    capacity, width, _ = received[0].shape
    me = lax.axis_index("box")
    stacked = jnp.concatenate(received, axis=0)
    held = ((entry_slot // capacity) ^ me) * capacity + entry_slot % capacity
    live = (jnp.arange(entries, dtype=I32)[None, :] < entry_count[:, None]).astype(BF)
    mass = jnp.einsum("tl,tlij->tj", live, weights, preferred_element_type=F32)
    picked = stacked[held] * live[:, :, None, None]
    numerator = jnp.einsum("tlhi,tlij->tjh", picked, weights, preferred_element_type=F32)
    projected = (numerator / mass[:, :, None]).astype(BF).reshape(targets * block_size, width)
    total = projected.shape[0]
    dom_total = lax.axis_size("dom")
    owner_capacity = 2 * (total // dom_total)
    place = owner_route * owner_capacity + exclusive_order(owner_route, dom_total)
    rows = jnp.zeros((dom_total * owner_capacity, width), BF).at[place].set(projected)
    spots = jnp.full((dom_total * owner_capacity,), total, I32).at[place].set(owner_slot)
    rows = lax.all_to_all(
        rows.reshape(dom_total, owner_capacity, width), "dom", 0, 0, tiled=True
    )
    spots = lax.all_to_all(spots.reshape(dom_total, owner_capacity), "dom", 0, 0, tiled=True)
    return (
        jnp.zeros((total, width), BF)
        .at[spots.reshape(-1)]
        .set(rows.reshape(-1, width), mode="drop")
    )


def body(old_history, box_route, entry_slot, entry_count, weights, owner_route, owner_slot,
         connectivity, shared_nodes, node_motion, elem_size, decay, couple, readout):
    blocks, width, block_size = old_history.shape
    targets, entries = entry_slot.shape
    box_total = lax.axis_size("box")
    dom_total = lax.axis_size("dom")
    capacity = blocks // 2
    rows = targets * block_size
    row_groups = rows // LANES
    elements = connectivity.shape[1]
    nodes = node_motion.shape[1]

    packed = call(
        pack_blocks, [HBM, HBM],
        [arrays((capacity, width, block_size), BF)] * box_total,
        [
            pltpu.SMEM((box_total * capacity,), I32),
            pltpu.SMEM((blocks,), I32),
            pltpu.VMEM(old_history.shape, BF),
            pltpu.SemaphoreType.DMA((2,)),
        ],
        (
            pltpu.with_memory_space_constraint(box_route, pltpu.HBM),
            pltpu.with_memory_space_constraint(old_history, pltpu.HBM),
        ),
    )
    received = {0: packed[0]}
    for k in [k for k in range(2, box_total)] + [1]:
        received[k] = lax.ppermute(packed[k], "box", [(i, i ^ k) for i in range(box_total)])
    received = [received[k] for k in range(box_total)]
    flat_weights = weights.reshape(targets, entries * block_size, block_size)
    edge = elem_size.reshape(1, elements)
    drive, base, onehot, grouped, quarter, chosen, inverse = call(
        element_parts, [VMEM] * 6,
        [
            arrays((elements, width), F32),
            arrays((SUBS, elements), F32),
            arrays((connectivity.shape[0], elements, LANES), BF),
            arrays((connectivity.shape[0], 2 * nodes // LANES, elements), BF),
            arrays((1, elements), F32),
            arrays((SUBS, shared_nodes.shape[1]), I32),
            arrays((2, nodes // LANES, LANES), I32),
        ],
        [
            pltpu.VMEM((SUBS, elements), F32),
            pltpu.VMEM((SUBS, elements), F32),
            pltpu.VMEM((2, SUBS, width), F32),
        ],
        (connectivity, node_motion, edge, couple.T, readout.T, shared_nodes),
        cost=1000,
    )
    usual = rows // dom_total
    relaxing = decay.reshape(1, width)
    if usual == LANES:
        spots, positions, table = call(
            sort_rows, [VMEM, VMEM],
            [
                arrays((2, row_groups, LANES), F32),
                arrays((dom_total, META, LANES), BF),
                arrays((2 * dom_total,), I32),
            ],
            [
                pltpu.VMEM((row_groups, LANES), F32),
                pltpu.VMEM((row_groups, LANES), F32),
                pltpu.SMEM((dom_total + 1,), I32),
            ],
            (owner_route.reshape(row_groups, LANES), owner_slot.reshape(1, rows)),
            out_specs=[VMEM, VMEM, SMEM],
        )
        masked, mass_inv, block_of = call(
            functools.partial(mask_weights, capacity), [SMEM, SMEM, VMEM],
            [
                arrays(flat_weights.shape, BF),
                arrays((targets, block_size), F32),
                arrays((targets * entries,), I32),
            ],
            [],
            (entry_slot.T, entry_count, flat_weights),
            out_specs=[VMEM, VMEM, SMEM],
        )
        payload = arrays((2 * usual + META, width), BF)
        outgoing = call(
            project_rows, [VMEM] * (6 + box_total),
            [payload] * dom_total,
            [
                pltpu.VMEM((box_total * capacity, width, block_size), BF),
                pltpu.VMEM((width, rows), BF),
                pltpu.VMEM((row_groups, LANES, width), BF),
                pltpu.SMEM(table.shape, I32),
                pltpu.SMEM(block_of.shape, I32),
                pltpu.SemaphoreType.DMA((2,)),
            ],
            (table, block_of, masked, mass_inv, spots, positions, *received),
        )
        payloads = {0: outgoing[0]}
        for k in range(1, dom_total):
            payloads[k] = lax.ppermute(outgoing[k], "dom", [(i, i ^ k) for i in range(dom_total)])
        order = arrival(dom_total)
        stages = [[0, *order[0]], *order[1:]]

        early = []
        for stage in stages[:-1]:
            count = len(stage)
            early = [
                call(
                    functools.partial(place_more, count),
                    [VMEM] * (count + len(early)), arrays((elements, width), F32),
                    [], [*[payloads[k] for k in stage], *early], cost=1000,
                )
            ]
        early = early[0]
        late = [payloads[k] for k in stages[-1]]
        placed = False
    else:
        early = spread_rows(received, entry_slot, entry_count, weights, owner_route, owner_slot)
        late = []
        placed = True
    export = arrays((3, shared_nodes.shape[1]), F32)
    arrived, local, *exports = call(
        functools.partial(finish, placed, len(late)),
        [VMEM] * (len(late) + 8),
        [arrays((elements, width), BF), arrays((3, nodes // LANES, LANES), F32)] + [export] * 4,
        [pltpu.VMEM((6 * SUBS, elements), F32)],
        (*late, early, base, quarter, grouped, onehot, relaxing, readout.T, chosen),
    )
    history = call(relax, [VMEM] * 3, arrays((elements, width), BF), [], (arrived, drive, relaxing))
    halo = [None] * 4
    for m in (1, 0, 3, 2):
        halo[m] = lax.ppermute(exports[m], ("dom", "box"), swaps(m))
    force = call(
        add_shared, [VMEM] * (2 + len(halo)), arrays((3, nodes), F32), [],
        (local, inverse, *halo),
    )
    return history, force


def arrival(dom_total):
    far = dom_total // 2
    return [
        [dom_total - 1, *range(far + 1, dom_total - 2), 1],
        list(range(far - 1, 1, -1)),
        [dom_total - 2, far],
    ]


def solution(mesh):
    return jax.shard_map(
        body,
        mesh=mesh,
        in_specs=(
            P(("dom", "box"), None, None),
            P(("dom", "box")),
            P(("dom", "box"), None),
            P(("dom", "box")),
            P(("dom", "box"), None, None, None),
            P(("dom", "box")),
            P(("dom", "box")),
            P(None, ("dom", "box")),
            P(None, ("dom", "box")),
            P(None, ("dom", "box")),
            P(("dom", "box")),
            P(),
            P(),
            P(),
        ),
        out_specs=(P(("dom", "box"), None), P(None, ("dom", "box"))),
        check_vma=False,
    )
```

```python
import functools

import jax
import jax.numpy as jnp
from jax import lax
from jax.experimental import pallas as pl
from jax.experimental.pallas import tpu as pltpu
from jax.sharding import PartitionSpec as P


BF = jnp.bfloat16
F32 = jnp.float32
I32 = jnp.int32
LANES = 128
SUBS = 8
META = 8
PARTS = 16
NOWHERE = 16.0
TENSOR = ((0, 3, 5), (3, 1, 4), (5, 4, 2))
NT_DIMS = (((1,), (1,)), ((), ()))
TN_DIMS = (((0,), (0,)), ((), ()))
HIGHEST = lax.Precision.HIGHEST


def iota(shape, dim):
    return lax.broadcasted_iota(I32, shape, dim)


def pieces(x, count):
    out = []
    for _ in range(count - 1):
        high = x.astype(BF)
        out.append(high)
        x = x - high.astype(F32)
    out.append(x.astype(BF))
    return out


def as_onehot(mask):
    return jnp.where(mask, 1.0, 0.0).astype(BF)


def lookup(rows, index):
    low = index & (LANES - 1)
    high = index >> 7
    out = jnp.zeros(index.shape, F32)
    for r, row in enumerate(rows):
        got = jnp.take_along_axis(
            jnp.broadcast_to(row, index.shape), low, axis=1, mode="promise_in_bounds"
        )
        out = jnp.where(high == r, got, out)
    return out


def pack_blocks(route_hbm, old_hbm, *rest):
    outs = rest[:-4]
    table, route, old, sems = rest[-4:]
    find = pltpu.make_async_copy(route_hbm, route, sems.at[0])
    take = pltpu.make_async_copy(old_hbm, old, sems.at[1])
    find.start()
    take.start()
    find.wait()
    me = lax.axis_index("box")
    capacity = outs[0].shape[0]
    for m in range(len(outs) * capacity):
        table[m] = 0
    routes = [route[i] for i in range(old.shape[0])]
    for i, target in enumerate(routes):
        order = jnp.int32(0)
        for earlier in routes[:i]:
            order = order + (earlier == target).astype(I32)
        table[(target ^ me) * capacity + order] = i
    take.wait()
    for k, out in enumerate(outs):
        for s in range(capacity):
            out[s] = old[table[k * capacity + s]]


def marks(high, low, rows):
    shape = (LANES, high.shape[1])
    low = jnp.broadcast_to(low, shape).astype(BF)
    low_iota = iota(shape, 0).astype(F32).astype(BF)
    match = jnp.where(low_iota == low, jnp.ones_like(low), jnp.zeros_like(low))
    return jnp.concatenate(
        [
            match * jnp.broadcast_to(jnp.where(high == g, 1.0, 0.0), shape).astype(BF)
            for g in range(rows // LANES)
        ],
        axis=0,
    )


def side_by_side(x, first, count):
    return jnp.concatenate([x[first + i : first + i + 1] for i in range(count)], axis=1)


def sort_rows(owner_route, owner_slot, spots, positions, table, high_rows, low_rows, starts):
    dom_total = positions.shape[0]
    row_groups = owner_route.shape[0]
    rows = row_groups * LANES
    me = lax.axis_index("dom")
    route = owner_route[...]
    picks = jnp.concatenate([as_onehot(route == d) for d in range(dom_total)], axis=0)
    span = dom_total * row_groups
    ahead = as_onehot(iota((LANES, LANES), 0) < iota((LANES, LANES), 1))
    within = jnp.dot(picks, ahead, preferred_element_type=F32)
    totals = jnp.dot(picks, jnp.ones((LANES, LANES), BF), preferred_element_type=F32).astype(BF)
    before = as_onehot(iota((span, span), 1) < iota((span, span), 0))
    base = jnp.dot(before, totals, preferred_element_type=F32)
    ranked = within + base
    place = jnp.zeros((row_groups, LANES), F32)
    for d in range(dom_total):
        place = jnp.where(route == d, ranked[d * row_groups : (d + 1) * row_groups], place)
        starts[d] = jnp.max(base[d * row_groups : d * row_groups + 1]).astype(I32)
    starts[dom_total] = rows
    place = place.astype(I32)
    high = (place >> 7).astype(F32)
    low = (place & (LANES - 1)).astype(F32)
    spots[0] = high
    spots[1] = low
    spot = owner_slot[...]
    which = iota((PARTS, rows), 0)
    parts = jnp.where(which == 0, spot >> 7, jnp.where(which == 1, spot & (LANES - 1), 0))
    parts = parts.astype(F32).astype(BF)
    ordered = jnp.zeros((PARTS, rows), F32)
    for g in range(0, row_groups, 2):
        ordered = ordered + lax.dot_general(
            parts[:, g * LANES : (g + 2) * LANES],
            marks(side_by_side(high, g, 2), side_by_side(low, g, 2), rows),
            NT_DIMS,
            preferred_element_type=F32,
        )
    for g in range(row_groups):
        high_rows[g : g + 1] = ordered[0:1, g * LANES : (g + 1) * LANES]
        low_rows[g : g + 1] = ordered[1:2, g * LANES : (g + 1) * LANES]
    which = iota((META, LANES), 0)
    for k in range(dom_total):
        owner = me ^ k
        start = starts[owner]
        held = starts[owner + 1] - start
        block = jnp.zeros((META, LANES), F32)
        for j in range(2):
            chunk = jnp.minimum(start // LANES + j, row_groups - 1)
            table[2 * k + j] = chunk
            high = jnp.where(held > j * LANES, high_rows[pl.ds(chunk, 1)], NOWHERE)
            block = jnp.where(which == j, high, block)
            block = jnp.where(which == 2 + j, low_rows[pl.ds(chunk, 1)], block)
        positions[k] = block.astype(BF)


def mask_weights(capacity, slot, count, weights, masked, mass_inv, blocks):
    targets = weights.shape[0]
    entries = weights.shape[1] // LANES
    box = lax.axis_index("box")
    for t in range(targets):
        total = jnp.zeros((1, LANES), F32)
        for l in range(entries):
            live = l < count[t]
            span = slice(l * LANES, (l + 1) * LANES)
            part = weights[t, span, :]
            part = jnp.where(live, part, jnp.zeros_like(part))
            masked[t, span, :] = part
            total = total + jnp.sum(part.astype(F32), axis=0, keepdims=True)
            entry = jnp.where(live, slot[l, t], slot[0, t])
            source = lax.div(entry, capacity) ^ box
            blocks[t * entries + l] = source * capacity + lax.rem(entry, capacity)
        mass_inv[t : t + 1] = 1.0 / total


def element_parts(connectivity, motion, size, couple, readout, shared, drive, base, onehot,
                  grouped, quarter, chosen, inverse, strain, elastic, wide):
    elements = connectivity.shape[1]
    corners = connectivity.shape[0]
    groups = motion.shape[1] // LANES
    corner = iota((corners, LANES), 0)
    signs = [(2 * ((corner >> c) & 1) - 1).astype(F32) for c in range(3)]
    low_iota = iota((LANES, LANES), 0)
    lane_iota = iota((LANES, LANES), 1).astype(F32)
    eighth = iota((groups, LANES), 0)
    strain[...] = jnp.zeros_like(strain)
    elastic[...] = jnp.zeros_like(elastic)
    for j in range(elements // LANES):
        lanes = slice(j * LANES, (j + 1) * LANES)
        nodes = connectivity[:, lanes]
        edge = size[:, lanes]
        scale = 1.0 / (4.0 * edge)
        quarter[:, lanes] = edge * edge * 0.25
        grad = []
        for i in range(3):
            moved = lookup(
                [motion[i : i + 1, r * LANES : (r + 1) * LANES] for r in range(groups)], nodes
            )
            grad.append(
                [jnp.sum(moved * signs[c], axis=0, keepdims=True) * scale for c in range(3)]
            )
        rows = [
            grad[0][0],
            grad[1][1],
            grad[2][2],
            grad[0][1] + grad[1][0],
            grad[1][2] + grad[2][1],
            grad[2][0] + grad[0][2],
        ]
        volume = 1.2 * (rows[0] + rows[1] + rows[2])
        for c in range(6):
            strain[c : c + 1, lanes] = rows[c]
            elastic[c : c + 1, lanes] = volume + 1.6 * rows[c] if c < 3 else 0.8 * rows[c]
        turned = (nodes & (LANES - 1)).astype(F32).T
        for a in range(corners):
            here = as_onehot(eighth == (nodes[a : a + 1] >> 7))
            grouped[a, :, lanes] = jnp.concatenate([here, here], axis=0)
            onehot[a, lanes, :] = as_onehot(lane_iota == turned[:, a : a + 1])
    wide[...] = jnp.zeros_like(wide)
    wide[0, 0:6] = couple[...]
    wide[1, 0:6] = readout[...]
    drive[...] = lax.dot_general(
        strain[...], wide[0], TN_DIMS, preferred_element_type=F32, precision=HIGHEST
    )
    base[...] = elastic[...] + lax.dot_general(
        wide[1], drive[...], NT_DIMS, preferred_element_type=F32, precision=HIGHEST
    )
    odd_dom = lax.axis_index("dom") & 1
    odd_box = lax.axis_index("box") & 1
    chosen[...] = jnp.zeros_like(chosen)
    chosen[0:1] = shared[pl.ds(1 - odd_dom, 1)]
    chosen[1:2] = shared[pl.ds(odd_dom, 1)]
    chosen[2:3] = shared[pl.ds(3 - odd_box, 1)]
    chosen[3:4] = shared[pl.ds(2 + odd_box, 1)]
    group = iota((groups, LANES), 0)
    lane = iota((groups, LANES), 1)
    total = jnp.zeros((2 * groups, LANES), F32)
    for m in range(4):
        axis = "dom" if m < 2 else "box"
        here = lax.axis_index(axis)
        partner = here + (1 - 2 * (here & 1)) * (1 if m % 2 == 0 else -1)
        paired = (partner >= 0) & (partner < lax.axis_size(axis))
        nodes = jnp.where(paired, chosen[m : m + 1], groups * LANES)
        here = group == (nodes >> 7)
        marks = jnp.concatenate(
            [jnp.where(here, m + 1, 0), jnp.where(here, lane, 0)], axis=0
        ).astype(F32)
        total = total + lax.dot_general(
            marks.astype(BF),
            as_onehot(low_iota == (nodes & (LANES - 1))),
            NT_DIMS,
            preferred_element_type=F32,
        )
    total = total.astype(I32)
    inverse[0] = total[:groups] - 1
    inverse[1] = total[groups:]


def project_rows(table_in, blocks_in, masked, mass_inv, spots, positions, *rest):
    dom_total = positions.shape[0]
    box_total = lax.axis_size("box")
    received = rest[:box_total]
    outs = rest[box_total : box_total + dom_total]
    held, turned, ordered, table, blocks, sems = rest[box_total + dom_total :]
    capacity = received[0].shape[0]
    copies = [
        pltpu.make_async_copy(source, target, sems.at[i])
        for i, (source, target) in enumerate([(table_in, table), (blocks_in, blocks)])
    ]
    for copy in copies:
        copy.start()
    for k, block in enumerate(received):
        for s in range(capacity):
            held[k * capacity + s] = block[s]
    for copy in copies:
        copy.wait()
    targets = masked.shape[0]
    entries = masked.shape[1] // LANES
    for t in range(targets):
        picked = [held[blocks[t * entries + l]] for l in range(entries)]
        numerator = jnp.dot(
            jnp.concatenate(picked, axis=1), masked[t], preferred_element_type=F32
        )
        turned[:, t * LANES : (t + 1) * LANES] = (numerator * mass_inv[t : t + 1]).astype(BF)
    high, low = spots[0], spots[1]
    rows = turned.shape[1]
    sort = jnp.zeros((rows, LANES), F32)
    for g in range(rows // LANES):
        sort = sort + lax.dot_general(
            marks(high[g : g + 1], low[g : g + 1], rows),
            turned[:, g * LANES : (g + 1) * LANES],
            NT_DIMS,
            preferred_element_type=F32,
        )
    for g in range(ordered.shape[0]):
        ordered[g] = sort[g * LANES : (g + 1) * LANES].astype(BF)
    for k, out in enumerate(outs):
        for j in range(2):
            out[j * LANES : (j + 1) * LANES] = ordered[table[2 * k + j]]
        out[2 * LANES :] = positions[k]


def place(payloads, elements):
    total = None
    for payload in payloads:
        where = payload[2 * LANES :].astype(F32)
        part = jnp.dot(
            marks(side_by_side(where, 0, 2), side_by_side(where, 2, 2), elements),
            payload[: 2 * LANES],
            preferred_element_type=F32,
        )
        total = part if total is None else total + part
    return total


def place_more(count, *refs):
    before, out = refs[count:-1], refs[-1]
    placed = place(refs[:count], out.shape[0])
    for held in before:
        placed = placed + held[...]
    out[...] = placed


def finish(placed, count, *refs):
    payloads = refs[:count]
    early, base, quarter, grouped, onehot, decay, readout, chosen = refs[count : count + 8]
    settled, local = refs[count + 8 : count + 10]
    exports = refs[count + 10 : count + 14]
    (spread_forces,) = refs[count + 14 :]
    elements = base.shape[1]
    if placed:
        arrived = early[...]
    else:
        arrived = (early[...] + place(payloads, elements)).astype(BF)
    settled[...] = arrived
    taken = readout[...] * decay[...]
    taken = jnp.concatenate([taken, jnp.zeros((SUBS - 6, LANES), F32)], axis=0)
    share = lax.dot_general(
        jnp.concatenate(pieces(taken, 3), axis=0), arrived, NT_DIMS, preferred_element_type=F32
    )
    stress = base[...] + (share[0:SUBS] + share[SUBS : 2 * SUBS] + share[2 * SUBS : 3 * SUBS])
    row = iota((3 * SUBS, 2 * SUBS), 0)
    column = iota((3 * SUBS, 2 * SUBS), 1) & (SUBS - 1)
    spread = jnp.zeros(row.shape, I32)
    for i in range(3):
        for c in range(3):
            spread = jnp.where(
                ((row >> 3) == i) & (column == TENSOR[i][c]),
                2 * ((row >> c) & 1) - 1,
                spread,
            )
    forces = jnp.dot(
        spread.astype(F32).astype(BF),
        jnp.concatenate(pieces(stress, 2), axis=0),
        preferred_element_type=F32,
    )
    forces = forces * quarter[...]
    high = forces.astype(BF).astype(F32)
    spread_forces[: 3 * SUBS] = high
    spread_forces[3 * SUBS :] = forces - high
    halves = [jnp.zeros((6 * SUBS, LANES), F32) for _ in range(2)]
    for a in range(SUBS):
        mask = grouped[a]
        values = []
        for i in range(3):
            both = [
                spread_forces[pl.ds(n * 3 * SUBS + i * SUBS + a, SUBS, stride=0), :]
                for n in range(2)
            ]
            values.append(jnp.concatenate(both, axis=0).astype(BF) * mask)
        halves[a % 2] = halves[a % 2] + jnp.dot(
            jnp.concatenate(values, axis=0), onehot[a], preferred_element_type=F32
        )
    total = halves[0] + halves[1]
    nodes = chosen[...]
    for i in range(3):
        summed = (
            total[2 * i * SUBS : (2 * i + 1) * SUBS]
            + total[(2 * i + 1) * SUBS : (2 * i + 2) * SUBS]
        )
        local[i] = summed
        got = lookup([summed[r : r + 1] for r in range(SUBS)], nodes)
        for m, out in enumerate(exports):
            out[i : i + 1] = got[m : m + 1]


def relax(arrived, drive, decay, history):
    history[...] = (arrived[...].astype(F32) * decay[...] + drive[...]).astype(BF)


def add_shared(local, inverse, *rest):
    received, force = rest[:-1], rest[-1]
    row, column = inverse[0], inverse[1]
    for i in range(local.shape[0]):
        total = local[i]
        for m, got in enumerate(received):
            share = jnp.take_along_axis(
                jnp.broadcast_to(got[i : i + 1], column.shape),
                column,
                axis=1,
                mode="promise_in_bounds",
            )
            total = total + jnp.where(row == m, share, 0.0)
        for r in range(local.shape[1]):
            force[i : i + 1, r * LANES : (r + 1) * LANES] = total[r : r + 1]


VMEM = pl.BlockSpec(memory_space=pltpu.VMEM)
SMEM = pl.BlockSpec(memory_space=pltpu.SMEM)
HBM = pl.BlockSpec(memory_space=pltpu.HBM)


def call(kernel, ins, outs, scratch, args, cost=2_000_000_000, out_specs=None):
    single = not isinstance(outs, (list, tuple))
    return pl.pallas_call(
        kernel,
        out_shape=outs,
        in_specs=ins,
        out_specs=out_specs or (VMEM if single else [VMEM] * len(outs)),
        scratch_shapes=scratch,
        cost_estimate=pl.CostEstimate(flops=cost, bytes_accessed=100_000, transcendentals=0),
        compiler_params=pltpu.CompilerParams(vmem_limit_bytes=24 * 1024 * 1024),
    )(*args)


def swaps(which):
    dom_total, box_total = lax.axis_size("dom"), lax.axis_size("box")
    pairs = []
    for d in range(dom_total):
        for b in range(box_total):
            here, total = (d, dom_total) if which < 2 else (b, box_total)
            other = here + (1 - 2 * (here & 1)) * (1 if which % 2 == 0 else -1)
            if not 0 <= other < total:
                partner = (d, b ^ 1 if which < 2 else box_total - 1 - b)
            else:
                partner = (other, b) if which < 2 else (d, other)
            pairs.append((d * box_total + b, partner[0] * box_total + partner[1]))
    return pairs


def arrays(shape, dtype):
    return jax.ShapeDtypeStruct(shape, dtype)


def exclusive_order(targets, choice_total):
    one_hot = (targets[:, None] == jnp.arange(choice_total, dtype=I32)[None, :]).astype(I32)
    return jnp.sum((jnp.cumsum(one_hot, axis=0) - one_hot) * one_hot, axis=1)


def spread_rows(received, entry_slot, entry_count, weights, owner_route, owner_slot):
    targets, entries = entry_slot.shape
    block_size = weights.shape[-1]
    capacity, width, _ = received[0].shape
    me = lax.axis_index("box")
    stacked = jnp.concatenate(received, axis=0)
    held = ((entry_slot // capacity) ^ me) * capacity + entry_slot % capacity
    live = (jnp.arange(entries, dtype=I32)[None, :] < entry_count[:, None]).astype(BF)
    mass = jnp.einsum("tl,tlij->tj", live, weights, preferred_element_type=F32)
    picked = stacked[held] * live[:, :, None, None]
    numerator = jnp.einsum("tlhi,tlij->tjh", picked, weights, preferred_element_type=F32)
    projected = (numerator / mass[:, :, None]).astype(BF).reshape(targets * block_size, width)
    total = projected.shape[0]
    dom_total = lax.axis_size("dom")
    owner_capacity = 2 * (total // dom_total)
    place = owner_route * owner_capacity + exclusive_order(owner_route, dom_total)
    rows = jnp.zeros((dom_total * owner_capacity, width), BF).at[place].set(projected)
    spots = jnp.full((dom_total * owner_capacity,), total, I32).at[place].set(owner_slot)
    rows = lax.all_to_all(
        rows.reshape(dom_total, owner_capacity, width), "dom", 0, 0, tiled=True
    )
    spots = lax.all_to_all(spots.reshape(dom_total, owner_capacity), "dom", 0, 0, tiled=True)
    return (
        jnp.zeros((total, width), BF)
        .at[spots.reshape(-1)]
        .set(rows.reshape(-1, width), mode="drop")
    )


def body(old_history, box_route, entry_slot, entry_count, weights, owner_route, owner_slot,
         connectivity, shared_nodes, node_motion, elem_size, decay, couple, readout):
    blocks, width, block_size = old_history.shape
    targets, entries = entry_slot.shape
    box_total = lax.axis_size("box")
    dom_total = lax.axis_size("dom")
    capacity = blocks // 2
    rows = targets * block_size
    row_groups = rows // LANES
    elements = connectivity.shape[1]
    nodes = node_motion.shape[1]

    packed = call(
        pack_blocks, [HBM, HBM],
        [arrays((capacity, width, block_size), BF)] * box_total,
        [
            pltpu.SMEM((box_total * capacity,), I32),
            pltpu.SMEM((blocks,), I32),
            pltpu.VMEM(old_history.shape, BF),
            pltpu.SemaphoreType.DMA((2,)),
        ],
        (
            pltpu.with_memory_space_constraint(box_route, pltpu.HBM),
            pltpu.with_memory_space_constraint(old_history, pltpu.HBM),
        ),
    )
    received = {0: packed[0]}
    for k in [k for k in range(2, box_total)] + [1]:
        received[k] = lax.ppermute(packed[k], "box", [(i, i ^ k) for i in range(box_total)])
    received = [received[k] for k in range(box_total)]
    flat_weights = weights.reshape(targets, entries * block_size, block_size)
    edge = elem_size.reshape(1, elements)
    drive, base, onehot, grouped, quarter, chosen, inverse = call(
        element_parts, [VMEM] * 6,
        [
            arrays((elements, width), F32),
            arrays((SUBS, elements), F32),
            arrays((connectivity.shape[0], elements, LANES), BF),
            arrays((connectivity.shape[0], 2 * nodes // LANES, elements), BF),
            arrays((1, elements), F32),
            arrays((SUBS, shared_nodes.shape[1]), I32),
            arrays((2, nodes // LANES, LANES), I32),
        ],
        [
            pltpu.VMEM((SUBS, elements), F32),
            pltpu.VMEM((SUBS, elements), F32),
            pltpu.VMEM((2, SUBS, width), F32),
        ],
        (connectivity, node_motion, edge, couple.T, readout.T, shared_nodes),
        cost=1000,
    )
    usual = rows // dom_total
    relaxing = decay.reshape(1, width)
    if usual == LANES:
        spots, positions, table = call(
            sort_rows, [VMEM, VMEM],
            [
                arrays((2, row_groups, LANES), F32),
                arrays((dom_total, META, LANES), BF),
                arrays((2 * dom_total,), I32),
            ],
            [
                pltpu.VMEM((row_groups, LANES), F32),
                pltpu.VMEM((row_groups, LANES), F32),
                pltpu.SMEM((dom_total + 1,), I32),
            ],
            (owner_route.reshape(row_groups, LANES), owner_slot.reshape(1, rows)),
            out_specs=[VMEM, VMEM, SMEM],
        )
        masked, mass_inv, block_of = call(
            functools.partial(mask_weights, capacity), [SMEM, SMEM, VMEM],
            [
                arrays(flat_weights.shape, BF),
                arrays((targets, block_size), F32),
                arrays((targets * entries,), I32),
            ],
            [],
            (entry_slot.T, entry_count, flat_weights),
            out_specs=[VMEM, VMEM, SMEM],
        )
        payload = arrays((2 * usual + META, width), BF)
        outgoing = call(
            project_rows, [VMEM] * (6 + box_total),
            [payload] * dom_total,
            [
                pltpu.VMEM((box_total * capacity, width, block_size), BF),
                pltpu.VMEM((width, rows), BF),
                pltpu.VMEM((row_groups, LANES, width), BF),
                pltpu.SMEM(table.shape, I32),
                pltpu.SMEM(block_of.shape, I32),
                pltpu.SemaphoreType.DMA((2,)),
            ],
            (table, block_of, masked, mass_inv, spots, positions, *received),
        )
        payloads = {0: outgoing[0]}
        for k in range(1, dom_total):
            payloads[k] = lax.ppermute(outgoing[k], "dom", [(i, i ^ k) for i in range(dom_total)])
        order = arrival(dom_total)
        stages = [[0, *order[0]], *order[1:]]

        early = []
        for stage in stages[:-1]:
            count = len(stage)
            early = [
                call(
                    functools.partial(place_more, count),
                    [VMEM] * (count + len(early)), arrays((elements, width), F32),
                    [], [*[payloads[k] for k in stage], *early], cost=1000,
                )
            ]
        early = early[0]
        late = [payloads[k] for k in stages[-1]]
        placed = False
    else:
        early = spread_rows(received, entry_slot, entry_count, weights, owner_route, owner_slot)
        late = []
        placed = True
    export = arrays((3, shared_nodes.shape[1]), F32)
    arrived, local, *exports = call(
        functools.partial(finish, placed, len(late)),
        [VMEM] * (len(late) + 8),
        [arrays((elements, width), BF), arrays((3, nodes // LANES, LANES), F32)] + [export] * 4,
        [pltpu.VMEM((6 * SUBS, elements), F32)],
        (*late, early, base, quarter, grouped, onehot, relaxing, readout.T, chosen),
    )
    history = call(relax, [VMEM] * 3, arrays((elements, width), BF), [], (arrived, drive, relaxing))
    halo = [None] * 4
    for m in (1, 0, 3, 2):
        halo[m] = lax.ppermute(exports[m], ("dom", "box"), swaps(m))
    force = call(
        add_shared, [VMEM] * (2 + len(halo)), arrays((3, nodes), F32), [],
        (local, inverse, *halo),
    )
    return history, force


def arrival(dom_total):
    far, last = dom_total // 2, dom_total - 1
    return [
        [far, last, 1],
        [last - 1, far - 1],
        [*range(far + 1, last - 1), *range(2, far - 1)],
    ]


def solution(mesh):
    return jax.shard_map(
        body,
        mesh=mesh,
        in_specs=(
            P(("dom", "box"), None, None),
            P(("dom", "box")),
            P(("dom", "box"), None),
            P(("dom", "box")),
            P(("dom", "box"), None, None, None),
            P(("dom", "box")),
            P(("dom", "box")),
            P(None, ("dom", "box")),
            P(None, ("dom", "box")),
            P(None, ("dom", "box")),
            P(("dom", "box")),
            P(),
            P(),
            P(),
        ),
        out_specs=(P(("dom", "box"), None), P(None, ("dom", "box"))),
        check_vma=False,
    )
```

```python
import functools

import jax
import jax.numpy as jnp
from jax import lax
from jax.experimental import pallas as pl
from jax.experimental.pallas import tpu as pltpu
from jax.sharding import PartitionSpec as P


BF = jnp.bfloat16
F32 = jnp.float32
I32 = jnp.int32
LANES = 128
SUBS = 8
META = 8
PARTS = 16
NOWHERE = 16.0
TENSOR = ((0, 3, 5), (3, 1, 4), (5, 4, 2))
NT_DIMS = (((1,), (1,)), ((), ()))
TN_DIMS = (((0,), (0,)), ((), ()))
HIGHEST = lax.Precision.HIGHEST


def iota(shape, dim):
    return lax.broadcasted_iota(I32, shape, dim)


def pieces(x, count):
    out = []
    for _ in range(count - 1):
        high = x.astype(BF)
        out.append(high)
        x = x - high.astype(F32)
    out.append(x.astype(BF))
    return out


def as_onehot(mask):
    return jnp.where(mask, 1.0, 0.0).astype(BF)


def lookup(rows, index):
    low = index & (LANES - 1)
    high = index >> 7
    out = jnp.zeros(index.shape, F32)
    for r, row in enumerate(rows):
        got = jnp.take_along_axis(
            jnp.broadcast_to(row, index.shape), low, axis=1, mode="promise_in_bounds"
        )
        out = jnp.where(high == r, got, out)
    return out


def pack_blocks(route_hbm, old_hbm, *rest):
    outs = rest[:-4]
    table, route, old, sems = rest[-4:]
    find = pltpu.make_async_copy(route_hbm, route, sems.at[0])
    take = pltpu.make_async_copy(old_hbm, old, sems.at[1])
    find.start()
    take.start()
    find.wait()
    me = lax.axis_index("box")
    capacity = outs[0].shape[0]
    for m in range(len(outs) * capacity):
        table[m] = 0
    routes = [route[i] for i in range(old.shape[0])]
    for i, target in enumerate(routes):
        order = jnp.int32(0)
        for earlier in routes[:i]:
            order = order + (earlier == target).astype(I32)
        table[(target ^ me) * capacity + order] = i
    take.wait()
    for k, out in enumerate(outs):
        for s in range(capacity):
            out[s] = old[table[k * capacity + s]]


def marks(high, low, rows):
    shape = (LANES, high.shape[1])
    low = jnp.broadcast_to(low, shape).astype(BF)
    low_iota = iota(shape, 0).astype(F32).astype(BF)
    match = jnp.where(low_iota == low, jnp.ones_like(low), jnp.zeros_like(low))
    return jnp.concatenate(
        [
            match * jnp.broadcast_to(jnp.where(high == g, 1.0, 0.0), shape).astype(BF)
            for g in range(rows // LANES)
        ],
        axis=0,
    )


def side_by_side(x, first, count):
    return jnp.concatenate([x[first + i : first + i + 1] for i in range(count)], axis=1)


def sort_rows(owner_route, owner_slot, spots, positions, table, high_rows, low_rows, starts):
    dom_total = positions.shape[0]
    row_groups = owner_route.shape[0]
    rows = row_groups * LANES
    me = lax.axis_index("dom")
    route = owner_route[...]
    picks = jnp.concatenate([as_onehot(route == d) for d in range(dom_total)], axis=0)
    span = dom_total * row_groups
    ahead = as_onehot(iota((LANES, LANES), 0) < iota((LANES, LANES), 1))
    within = jnp.dot(picks, ahead, preferred_element_type=F32)
    totals = jnp.dot(picks, jnp.ones((LANES, LANES), BF), preferred_element_type=F32).astype(BF)
    before = as_onehot(iota((span, span), 1) < iota((span, span), 0))
    base = jnp.dot(before, totals, preferred_element_type=F32)
    ranked = within + base
    place = jnp.zeros((row_groups, LANES), F32)
    for d in range(dom_total):
        place = jnp.where(route == d, ranked[d * row_groups : (d + 1) * row_groups], place)
        starts[d] = jnp.max(base[d * row_groups : d * row_groups + 1]).astype(I32)
    starts[dom_total] = rows
    place = place.astype(I32)
    high = (place >> 7).astype(F32)
    low = (place & (LANES - 1)).astype(F32)
    spots[0] = high
    spots[1] = low
    spot = owner_slot[...]
    which = iota((PARTS, rows), 0)
    parts = jnp.where(which == 0, spot >> 7, jnp.where(which == 1, spot & (LANES - 1), 0))
    parts = parts.astype(F32).astype(BF)
    ordered = jnp.zeros((PARTS, rows), F32)
    for g in range(0, row_groups, 2):
        ordered = ordered + lax.dot_general(
            parts[:, g * LANES : (g + 2) * LANES],
            marks(side_by_side(high, g, 2), side_by_side(low, g, 2), rows),
            NT_DIMS,
            preferred_element_type=F32,
        )
    for g in range(row_groups):
        high_rows[g : g + 1] = ordered[0:1, g * LANES : (g + 1) * LANES]
        low_rows[g : g + 1] = ordered[1:2, g * LANES : (g + 1) * LANES]
    which = iota((META, LANES), 0)
    for k in range(dom_total):
        hop = jnp.int32(0)
        for b in range(lax.axis_size("box") if k else 0):
            here = lax.axis_index("box") == b
            hop = jnp.where(here, hops(dom_total, b)[k - 1], hop)
        owner = me ^ hop
        start = starts[owner]
        held = starts[owner + 1] - start
        block = jnp.zeros((META, LANES), F32)
        for j in range(2):
            chunk = jnp.minimum(start // LANES + j, row_groups - 1)
            table[2 * k + j] = chunk
            high = jnp.where(held > j * LANES, high_rows[pl.ds(chunk, 1)], NOWHERE)
            block = jnp.where(which == j, high, block)
            block = jnp.where(which == 2 + j, low_rows[pl.ds(chunk, 1)], block)
        positions[k] = block.astype(BF)


def mask_weights(capacity, slot, count, weights, masked, mass_inv, blocks):
    targets = weights.shape[0]
    entries = weights.shape[1] // LANES
    box = lax.axis_index("box")
    for t in range(targets):
        total = jnp.zeros((1, LANES), F32)
        for l in range(entries):
            live = l < count[t]
            span = slice(l * LANES, (l + 1) * LANES)
            part = weights[t, span, :]
            part = jnp.where(live, part, jnp.zeros_like(part))
            masked[t, span, :] = part
            total = total + jnp.sum(part.astype(F32), axis=0, keepdims=True)
            entry = jnp.where(live, slot[l, t], slot[0, t])
            source = lax.div(entry, capacity) ^ box
            blocks[t * entries + l] = source * capacity + lax.rem(entry, capacity)
        mass_inv[t : t + 1] = 1.0 / total


def element_parts(connectivity, motion, size, couple, readout, shared, drive, base, onehot,
                  grouped, quarter, chosen, inverse, strain, elastic, wide):
    elements = connectivity.shape[1]
    corners = connectivity.shape[0]
    groups = motion.shape[1] // LANES
    corner = iota((corners, LANES), 0)
    signs = [(2 * ((corner >> c) & 1) - 1).astype(F32) for c in range(3)]
    low_iota = iota((LANES, LANES), 0)
    lane_iota = iota((LANES, LANES), 1).astype(F32)
    eighth = iota((groups, LANES), 0)
    strain[...] = jnp.zeros_like(strain)
    elastic[...] = jnp.zeros_like(elastic)
    for j in range(elements // LANES):
        lanes = slice(j * LANES, (j + 1) * LANES)
        nodes = connectivity[:, lanes]
        edge = size[:, lanes]
        scale = 1.0 / (4.0 * edge)
        quarter[:, lanes] = edge * edge * 0.25
        grad = []
        for i in range(3):
            moved = lookup(
                [motion[i : i + 1, r * LANES : (r + 1) * LANES] for r in range(groups)], nodes
            )
            grad.append(
                [jnp.sum(moved * signs[c], axis=0, keepdims=True) * scale for c in range(3)]
            )
        rows = [
            grad[0][0],
            grad[1][1],
            grad[2][2],
            grad[0][1] + grad[1][0],
            grad[1][2] + grad[2][1],
            grad[2][0] + grad[0][2],
        ]
        volume = 1.2 * (rows[0] + rows[1] + rows[2])
        for c in range(6):
            strain[c : c + 1, lanes] = rows[c]
            elastic[c : c + 1, lanes] = volume + 1.6 * rows[c] if c < 3 else 0.8 * rows[c]
        turned = (nodes & (LANES - 1)).astype(F32).T
        for a in range(corners):
            here = as_onehot(eighth == (nodes[a : a + 1] >> 7))
            grouped[a, :, lanes] = jnp.concatenate([here, here], axis=0)
            onehot[a, lanes, :] = as_onehot(lane_iota == turned[:, a : a + 1])
    wide[...] = jnp.zeros_like(wide)
    wide[0, 0:6] = couple[...]
    wide[1, 0:6] = readout[...]
    drive[...] = lax.dot_general(
        strain[...], wide[0], TN_DIMS, preferred_element_type=F32, precision=HIGHEST
    )
    base[...] = elastic[...] + lax.dot_general(
        wide[1], drive[...], NT_DIMS, preferred_element_type=F32, precision=HIGHEST
    )
    odd_dom = lax.axis_index("dom") & 1
    odd_box = lax.axis_index("box") & 1
    chosen[...] = jnp.zeros_like(chosen)
    chosen[0:1] = shared[pl.ds(1 - odd_dom, 1)]
    chosen[1:2] = shared[pl.ds(odd_dom, 1)]
    chosen[2:3] = shared[pl.ds(3 - odd_box, 1)]
    chosen[3:4] = shared[pl.ds(2 + odd_box, 1)]
    group = iota((groups, LANES), 0)
    lane = iota((groups, LANES), 1)
    total = jnp.zeros((2 * groups, LANES), F32)
    for m in range(4):
        axis = "dom" if m < 2 else "box"
        here = lax.axis_index(axis)
        partner = here + (1 - 2 * (here & 1)) * (1 if m % 2 == 0 else -1)
        paired = (partner >= 0) & (partner < lax.axis_size(axis))
        nodes = jnp.where(paired, chosen[m : m + 1], groups * LANES)
        here = group == (nodes >> 7)
        marks = jnp.concatenate(
            [jnp.where(here, m + 1, 0), jnp.where(here, lane, 0)], axis=0
        ).astype(F32)
        total = total + lax.dot_general(
            marks.astype(BF),
            as_onehot(low_iota == (nodes & (LANES - 1))),
            NT_DIMS,
            preferred_element_type=F32,
        )
    total = total.astype(I32)
    inverse[0] = total[:groups] - 1
    inverse[1] = total[groups:]


def project_rows(table_in, blocks_in, masked, mass_inv, spots, positions, *rest):
    dom_total = positions.shape[0]
    box_total = lax.axis_size("box")
    received = rest[:box_total]
    outs = rest[box_total : box_total + dom_total]
    held, turned, ordered, table, blocks, sems = rest[box_total + dom_total :]
    capacity = received[0].shape[0]
    copies = [
        pltpu.make_async_copy(source, target, sems.at[i])
        for i, (source, target) in enumerate([(table_in, table), (blocks_in, blocks)])
    ]
    for copy in copies:
        copy.start()
    for k, block in enumerate(received):
        for s in range(capacity):
            held[k * capacity + s] = block[s]
    for copy in copies:
        copy.wait()
    targets = masked.shape[0]
    entries = masked.shape[1] // LANES
    for t in range(targets):
        picked = [held[blocks[t * entries + l]] for l in range(entries)]
        numerator = jnp.dot(
            jnp.concatenate(picked, axis=1), masked[t], preferred_element_type=F32
        )
        turned[:, t * LANES : (t + 1) * LANES] = (numerator * mass_inv[t : t + 1]).astype(BF)
    high, low = spots[0], spots[1]
    rows = turned.shape[1]
    sort = jnp.zeros((rows, LANES), F32)
    for g in range(rows // LANES):
        sort = sort + lax.dot_general(
            marks(high[g : g + 1], low[g : g + 1], rows),
            turned[:, g * LANES : (g + 1) * LANES],
            NT_DIMS,
            preferred_element_type=F32,
        )
    for g in range(ordered.shape[0]):
        ordered[g] = sort[g * LANES : (g + 1) * LANES].astype(BF)
    for k, out in enumerate(outs):
        for j in range(2):
            out[j * LANES : (j + 1) * LANES] = ordered[table[2 * k + j]]
        out[2 * LANES :] = positions[k]


def place(payloads, elements):
    total = None
    for payload in payloads:
        where = payload[2 * LANES :].astype(F32)
        part = jnp.dot(
            marks(side_by_side(where, 0, 2), side_by_side(where, 2, 2), elements),
            payload[: 2 * LANES],
            preferred_element_type=F32,
        )
        total = part if total is None else total + part
    return total


def place_more(count, *refs):
    before, out = refs[count:-1], refs[-1]
    placed = place(refs[:count], out.shape[0])
    for held in before:
        placed = placed + held[...]
    out[...] = placed


def finish(placed, count, *refs):
    payloads = refs[:count]
    early, base, quarter, grouped, onehot, decay, readout, chosen = refs[count : count + 8]
    settled, local = refs[count + 8 : count + 10]
    exports = refs[count + 10 : count + 14]
    (spread_forces,) = refs[count + 14 :]
    elements = base.shape[1]
    if placed:
        arrived = early[...]
    else:
        arrived = (early[...] + place(payloads, elements)).astype(BF)
    settled[...] = arrived
    taken = readout[...] * decay[...]
    taken = jnp.concatenate([taken, jnp.zeros((SUBS - 6, LANES), F32)], axis=0)
    share = lax.dot_general(
        jnp.concatenate(pieces(taken, 3), axis=0), arrived, NT_DIMS, preferred_element_type=F32
    )
    stress = base[...] + (share[0:SUBS] + share[SUBS : 2 * SUBS] + share[2 * SUBS : 3 * SUBS])
    row = iota((3 * SUBS, 2 * SUBS), 0)
    column = iota((3 * SUBS, 2 * SUBS), 1) & (SUBS - 1)
    spread = jnp.zeros(row.shape, I32)
    for i in range(3):
        for c in range(3):
            spread = jnp.where(
                ((row >> 3) == i) & (column == TENSOR[i][c]),
                2 * ((row >> c) & 1) - 1,
                spread,
            )
    forces = jnp.dot(
        spread.astype(F32).astype(BF),
        jnp.concatenate(pieces(stress, 2), axis=0),
        preferred_element_type=F32,
    )
    forces = forces * quarter[...]
    high = forces.astype(BF).astype(F32)
    spread_forces[: 3 * SUBS] = high
    spread_forces[3 * SUBS :] = forces - high
    halves = [jnp.zeros((6 * SUBS, LANES), F32) for _ in range(2)]
    for a in range(SUBS):
        mask = grouped[a]
        values = []
        for i in range(3):
            both = [
                spread_forces[pl.ds(n * 3 * SUBS + i * SUBS + a, SUBS, stride=0), :]
                for n in range(2)
            ]
            values.append(jnp.concatenate(both, axis=0).astype(BF) * mask)
        halves[a % 2] = halves[a % 2] + jnp.dot(
            jnp.concatenate(values, axis=0), onehot[a], preferred_element_type=F32
        )
    total = halves[0] + halves[1]
    nodes = chosen[...]
    for i in range(3):
        summed = (
            total[2 * i * SUBS : (2 * i + 1) * SUBS]
            + total[(2 * i + 1) * SUBS : (2 * i + 2) * SUBS]
        )
        local[i] = summed
        got = lookup([summed[r : r + 1] for r in range(SUBS)], nodes)
        for m, out in enumerate(exports):
            out[i : i + 1] = got[m : m + 1]


def relax(arrived, drive, decay, history):
    history[...] = (arrived[...].astype(F32) * decay[...] + drive[...]).astype(BF)


def add_shared(local, inverse, *rest):
    received, force = rest[:-1], rest[-1]
    row, column = inverse[0], inverse[1]
    for i in range(local.shape[0]):
        total = local[i]
        for m, got in enumerate(received):
            share = jnp.take_along_axis(
                jnp.broadcast_to(got[i : i + 1], column.shape),
                column,
                axis=1,
                mode="promise_in_bounds",
            )
            total = total + jnp.where(row == m, share, 0.0)
        for r in range(local.shape[1]):
            force[i : i + 1, r * LANES : (r + 1) * LANES] = total[r : r + 1]


VMEM = pl.BlockSpec(memory_space=pltpu.VMEM)
SMEM = pl.BlockSpec(memory_space=pltpu.SMEM)
HBM = pl.BlockSpec(memory_space=pltpu.HBM)


def call(kernel, ins, outs, scratch, args, cost=2_000_000_000, out_specs=None):
    single = not isinstance(outs, (list, tuple))
    return pl.pallas_call(
        kernel,
        out_shape=outs,
        in_specs=ins,
        out_specs=out_specs or (VMEM if single else [VMEM] * len(outs)),
        scratch_shapes=scratch,
        cost_estimate=pl.CostEstimate(flops=cost, bytes_accessed=100_000, transcendentals=0),
        compiler_params=pltpu.CompilerParams(vmem_limit_bytes=24 * 1024 * 1024),
    )(*args)


def swaps(which):
    dom_total, box_total = lax.axis_size("dom"), lax.axis_size("box")
    pairs = []
    for d in range(dom_total):
        for b in range(box_total):
            here, total = (d, dom_total) if which < 2 else (b, box_total)
            other = here + (1 - 2 * (here & 1)) * (1 if which % 2 == 0 else -1)
            if not 0 <= other < total:
                partner = (d, b ^ 1 if which < 2 else box_total - 1 - b)
            else:
                partner = (other, b) if which < 2 else (d, other)
            pairs.append((d * box_total + b, partner[0] * box_total + partner[1]))
    return pairs


def arrays(shape, dtype):
    return jax.ShapeDtypeStruct(shape, dtype)


def exclusive_order(targets, choice_total):
    one_hot = (targets[:, None] == jnp.arange(choice_total, dtype=I32)[None, :]).astype(I32)
    return jnp.sum((jnp.cumsum(one_hot, axis=0) - one_hot) * one_hot, axis=1)


def spread_rows(received, entry_slot, entry_count, weights, owner_route, owner_slot):
    targets, entries = entry_slot.shape
    block_size = weights.shape[-1]
    capacity, width, _ = received[0].shape
    me = lax.axis_index("box")
    stacked = jnp.concatenate(received, axis=0)
    held = ((entry_slot // capacity) ^ me) * capacity + entry_slot % capacity
    live = (jnp.arange(entries, dtype=I32)[None, :] < entry_count[:, None]).astype(BF)
    mass = jnp.einsum("tl,tlij->tj", live, weights, preferred_element_type=F32)
    picked = stacked[held] * live[:, :, None, None]
    numerator = jnp.einsum("tlhi,tlij->tjh", picked, weights, preferred_element_type=F32)
    projected = (numerator / mass[:, :, None]).astype(BF).reshape(targets * block_size, width)
    total = projected.shape[0]
    dom_total = lax.axis_size("dom")
    owner_capacity = 2 * (total // dom_total)
    place = owner_route * owner_capacity + exclusive_order(owner_route, dom_total)
    rows = jnp.zeros((dom_total * owner_capacity, width), BF).at[place].set(projected)
    spots = jnp.full((dom_total * owner_capacity,), total, I32).at[place].set(owner_slot)
    rows = lax.all_to_all(
        rows.reshape(dom_total, owner_capacity, width), "dom", 0, 0, tiled=True
    )
    spots = lax.all_to_all(spots.reshape(dom_total, owner_capacity), "dom", 0, 0, tiled=True)
    return (
        jnp.zeros((total, width), BF)
        .at[spots.reshape(-1)]
        .set(rows.reshape(-1, width), mode="drop")
    )


def body(old_history, box_route, entry_slot, entry_count, weights, owner_route, owner_slot,
         connectivity, shared_nodes, node_motion, elem_size, decay, couple, readout):
    blocks, width, block_size = old_history.shape
    targets, entries = entry_slot.shape
    box_total = lax.axis_size("box")
    dom_total = lax.axis_size("dom")
    capacity = blocks // 2
    rows = targets * block_size
    row_groups = rows // LANES
    elements = connectivity.shape[1]
    nodes = node_motion.shape[1]

    packed = call(
        pack_blocks, [HBM, HBM],
        [arrays((capacity, width, block_size), BF)] * box_total,
        [
            pltpu.SMEM((box_total * capacity,), I32),
            pltpu.SMEM((blocks,), I32),
            pltpu.VMEM(old_history.shape, BF),
            pltpu.SemaphoreType.DMA((2,)),
        ],
        (
            pltpu.with_memory_space_constraint(box_route, pltpu.HBM),
            pltpu.with_memory_space_constraint(old_history, pltpu.HBM),
        ),
    )
    received = {0: packed[0]}
    for k in [k for k in range(2, box_total)] + [1]:
        received[k] = lax.ppermute(packed[k], "box", [(i, i ^ k) for i in range(box_total)])
    received = [received[k] for k in range(box_total)]
    flat_weights = weights.reshape(targets, entries * block_size, block_size)
    edge = elem_size.reshape(1, elements)
    drive, base, onehot, grouped, quarter, chosen, inverse = call(
        element_parts, [VMEM] * 6,
        [
            arrays((elements, width), F32),
            arrays((SUBS, elements), F32),
            arrays((connectivity.shape[0], elements, LANES), BF),
            arrays((connectivity.shape[0], 2 * nodes // LANES, elements), BF),
            arrays((1, elements), F32),
            arrays((SUBS, shared_nodes.shape[1]), I32),
            arrays((2, nodes // LANES, LANES), I32),
        ],
        [
            pltpu.VMEM((SUBS, elements), F32),
            pltpu.VMEM((SUBS, elements), F32),
            pltpu.VMEM((2, SUBS, width), F32),
        ],
        (connectivity, node_motion, edge, couple.T, readout.T, shared_nodes),
        cost=1000,
    )
    usual = rows // dom_total
    relaxing = decay.reshape(1, width)
    if usual == LANES:
        spots, positions, table = call(
            sort_rows, [VMEM, VMEM],
            [
                arrays((2, row_groups, LANES), F32),
                arrays((dom_total, META, LANES), BF),
                arrays((2 * dom_total,), I32),
            ],
            [
                pltpu.VMEM((row_groups, LANES), F32),
                pltpu.VMEM((row_groups, LANES), F32),
                pltpu.SMEM((dom_total + 1,), I32),
            ],
            (owner_route.reshape(row_groups, LANES), owner_slot.reshape(1, rows)),
            out_specs=[VMEM, VMEM, SMEM],
        )
        masked, mass_inv, block_of = call(
            functools.partial(mask_weights, capacity), [SMEM, SMEM, VMEM],
            [
                arrays(flat_weights.shape, BF),
                arrays((targets, block_size), F32),
                arrays((targets * entries,), I32),
            ],
            [],
            (entry_slot.T, entry_count, flat_weights),
            out_specs=[VMEM, VMEM, SMEM],
        )
        payload = arrays((2 * usual + META, width), BF)
        outgoing = call(
            project_rows, [VMEM] * (6 + box_total),
            [payload] * dom_total,
            [
                pltpu.VMEM((box_total * capacity, width, block_size), BF),
                pltpu.VMEM((width, rows), BF),
                pltpu.VMEM((row_groups, LANES, width), BF),
                pltpu.SMEM(table.shape, I32),
                pltpu.SMEM(block_of.shape, I32),
                pltpu.SemaphoreType.DMA((2,)),
            ],
            (table, block_of, masked, mass_inv, spots, positions, *received),
        )
        payloads = {0: outgoing[0]}
        for k in range(1, dom_total):
            pairs = [
                (d * box_total + b, (d ^ hops(dom_total, b)[k - 1]) * box_total + b)
                for d in range(dom_total)
                for b in range(box_total)
            ]
            payloads[k] = lax.ppermute(outgoing[k], ("dom", "box"), pairs)
        order = arrival(dom_total)
        stages = [[0, *order[0]], *order[1:]]

        early = []
        for stage in stages[:-1]:
            count = len(stage)
            early = [
                call(
                    functools.partial(place_more, count),
                    [VMEM] * (count + len(early)), arrays((elements, width), F32),
                    [], [*[payloads[k] for k in stage], *early], cost=1000,
                )
            ]
        early = early[0]
        late = [payloads[k] for k in stages[-1]]
        placed = False
    else:
        early = spread_rows(received, entry_slot, entry_count, weights, owner_route, owner_slot)
        late = []
        placed = True
    export = arrays((3, shared_nodes.shape[1]), F32)
    arrived, local, *exports = call(
        functools.partial(finish, placed, len(late)),
        [VMEM] * (len(late) + 8),
        [arrays((elements, width), BF), arrays((3, nodes // LANES, LANES), F32)] + [export] * 4,
        [pltpu.VMEM((6 * SUBS, elements), F32)],
        (*late, early, base, quarter, grouped, onehot, relaxing, readout.T, chosen),
    )
    history = call(relax, [VMEM] * 3, arrays((elements, width), BF), [], (arrived, drive, relaxing))
    halo = [None] * 4
    for m in (1, 0, 3, 2):
        halo[m] = lax.ppermute(exports[m], ("dom", "box"), swaps(m))
    force = call(
        add_shared, [VMEM] * (2 + len(halo)), arrays((3, nodes), F32), [],
        (local, inverse, *halo),
    )
    return history, force


def hops(dom_total, box):
    far = dom_total // 2
    first = [dom_total - 1, *range(far + 1, dom_total - 1), far]
    near = list(range(1, far))
    turn = (1 - box) % len(near)
    return [k ^ (box % far) for k in first] + near[turn:] + near[:turn]


def arrival(dom_total):
    far = dom_total // 2
    return [
        [*range(1, far - 1), far + 1],
        [far - 1, far + 2],
        [far, *range(far + 3, dom_total)],
    ]


def solution(mesh):
    return jax.shard_map(
        body,
        mesh=mesh,
        in_specs=(
            P(("dom", "box"), None, None),
            P(("dom", "box")),
            P(("dom", "box"), None),
            P(("dom", "box")),
            P(("dom", "box"), None, None, None),
            P(("dom", "box")),
            P(("dom", "box")),
            P(None, ("dom", "box")),
            P(None, ("dom", "box")),
            P(None, ("dom", "box")),
            P(("dom", "box")),
            P(),
            P(),
            P(),
        ),
        out_specs=(P(("dom", "box"), None), P(None, ("dom", "box"))),
        check_vma=False,
    )
```
